32 devices in a mesh: tm: 8 (over z, y), space: 4 (over x, core).
Axes of the slice: x: 2, y: 2, z: 4, core: 2. Of those that a mesh axis runs over, the one named last changes fastest.
Arguments:
- queries: bfloat16 [8, 16, 32, 768], P('tm', 'space')
- key_vectors: bfloat16 [8, 16, 32, 768], P('tm', 'space')
- values: bfloat16 [8, 16, 32, 768], P('tm', 'space'), may hold values from -6 to 6
- grad_out: bfloat16 [8, 16, 32, 768], P('tm', 'space'), may hold values from -6 to 6
- windows: int32 [2, 6], replicated, may hold values from 1 to 31, as said below
Outputs:
- attended: bfloat16 [8, 16, 32, 768], P('tm', 'space')
- grad_queries: bfloat16 [8, 16, 32, 768], P('tm', 'space')
- grad_keys: bfloat16 [8, 16, 32, 768], P('tm', 'space')
- value_gradient: bfloat16 [8, 16, 32, 768], P('tm', 'space')
The draws below stay inside these ranges and needn't reach their ends.
Inputs may be any that keep to these rules, and one draw needn't show every extreme that they name: windows[0, h] is 1 to 2 and some head has 2; windows[1, h] is a quarter of 32 or more and some head has 31.
All inputs are finite; a program needn't handle non-finite values.
Results may differ from the reference program's by a relative error of at most 0.025.
Values may be sent and summed in bfloat16 or wider, within the bound.
A program may use at most 64 MiB of HBM per device.

```python
import math
import jax
import jax.numpy as jnp
from jax import lax

HEADS = 6
HD = 128
R_DEV = 4
COLS = 32
FRAMES = 8
ROWS = 16
WIDTH = 768
N_TM = 8
N_SPACE = 4


def paired_fields(key):
    grid_shape = (FRAMES, ROWS, COLS, HEADS * HD)
    base_keys = jax.random.normal(jax.random.fold_in(key, 11), grid_shape, jnp.float32)
    return base_keys


def draw_queries(key, part):
    grid_shape = (FRAMES, ROWS, COLS, HEADS * HD)
    drawn_draw = jax.random.normal(jax.random.fold_in(key, 15), grid_shape, jnp.float32)
    return drawn_draw.astype(jnp.bfloat16)


def draw_key_vectors(key, part):
    base_keys = paired_fields(key)
    return base_keys.astype(jnp.bfloat16)


def draw_windows(key, part):
    head_ids = jnp.arange(HEADS, dtype=jnp.int32)
    row_reaches = jax.random.randint(jax.random.fold_in(key, 21), (HEADS,), 1, R_DEV // 2 + 1)
    col_reaches = jax.random.randint(jax.random.fold_in(key, 22), (HEADS,), max(1, COLS // 4), COLS)
    chosen = jax.random.randint(jax.random.fold_in(key, 23), (), 0, HEADS)
    second = (chosen + 1 + jax.random.randint(jax.random.fold_in(key, 24), (), 0, HEADS - 1)) % HEADS
    row_reaches = jnp.where(head_ids == chosen, R_DEV // 2, row_reaches)
    col_reaches = jnp.where(head_ids == second, COLS - 1, col_reaches)
    return jnp.stack([row_reaches, col_reaches]).astype(jnp.int32)


def block_levels(rng, extent, shards, least, largest):
    loudness, own = 1.0, jax.random.fold_in(rng, 6)
    for dim, shards_of in shards:
        steps = jnp.exp(jax.random.uniform(jax.random.fold_in(own, dim), (shards_of,), jnp.float32, least / len(shards), largest / len(shards)))
        loudness = loudness * jnp.repeat(steps, extent[dim] // shards_of).reshape([-1 if axis == dim else 1 for axis in range(len(extent))])
    return loudness


def noise(key, dims, spread, most, split=(), kind=jnp.bfloat16):
    values = jax.random.normal(key, dims, jnp.float32) * spread
    if len(split) > 0:
        values = block_levels(key, dims, split, -0.22, 0.18) * values
    return jnp.clip(values, min=-most, max=most).astype(kind)


def setup_inputs(seed: int = 0) -> dict:
    key_of = jax.random.split(jax.random.key(seed), 6)
    return {
        "queries": draw_queries(jax.random.fold_in(key_of[5], 71), 0),
        "key_vectors": draw_key_vectors(jax.random.fold_in(key_of[5], 71), 0),
        "values": noise(key_of[2], (FRAMES, ROWS, COLS, WIDTH), 1.0, 6.0, ((0, 8), (1, 4))),
        "grad_out": noise(key_of[3], (FRAMES, ROWS, COLS, WIDTH), 1.0, 6.0, ((0, 8), (1, 4))),
        "windows": draw_windows(jax.random.fold_in(key_of[5], 71), 0),
    }


masked_score = -1e+30

def window_mask(windows, frame_index, block_index, row_extent, row_count, col_count, frame_total, row_sum_total):
    query_count = row_count * col_count
    query_ids = jnp.arange(query_count, dtype=jnp.int32)
    query_row = query_ids // col_count
    query_col = query_ids % col_count
    near_rows = row_count + 2 * row_extent
    key_ids = jnp.arange(3 * near_rows * col_count, dtype=jnp.int32)
    key_frame = key_ids // (near_rows * col_count) - 1
    key_row = key_ids // col_count % near_rows - row_extent
    key_col = key_ids % col_count
    global_frame = frame_index + key_frame
    global_row = block_index * row_count + key_row
    inside = (global_frame >= 0) & (global_frame < frame_total) & (global_row >= 0) & (global_row < row_sum_total)
    row_gap = jnp.abs(query_row[:, None] - key_row[None, :])
    col_gap = jnp.abs(query_col[:, None] - key_col[None, :])
    return inside[None, None, :] & (row_gap[None] <= windows[0][:, None, None]) & (col_gap[None] <= windows[1][:, None, None])

def rounded(array):
    return lax.optimization_barrier(array.astype(jnp.bfloat16)).astype(jnp.float32)

def reference(queries, key_vectors, values, grad_out, windows):
    frame_total, row_sum_total, col_count, feature_count = queries.shape
    head_count = windows.shape[1]
    head_size = feature_count // head_count
    row_extent = R_DEV // 2
    near_rows = R_DEV + 2 * row_extent
    score_scale = 1.0 / math.sqrt(head_size)
    padding = ((1, 1), (row_extent, row_extent), (0, 0), (0, 0))
    keys_pad = jnp.pad(key_vectors.astype(jnp.float32), padding)
    values_pad = jnp.pad(values.astype(jnp.float32), padding)
    zero_index = jnp.zeros((), jnp.int32)
    nearby_window_shape = (3, near_rows, col_count, feature_count)
    local_shape = (1, R_DEV, col_count, feature_count)

    def loop_iteration(loop_carried, step_index):
        padded_key_gradient, padded_value_gradient = loop_carried
        frame_index = (step_index // N_SPACE).astype(jnp.int32)
        block_index = (step_index % N_SPACE).astype(jnp.int32)
        window_corner = (frame_index, (block_index * R_DEV).astype(jnp.int32), zero_index, zero_index)
        near_keys = lax.dynamic_slice(keys_pad, window_corner, nearby_window_shape).reshape(-1, head_count, head_size)
        near_values = lax.dynamic_slice(values_pad, window_corner, nearby_window_shape).reshape(-1, head_count, head_size)
        local_query = lax.dynamic_slice(queries, window_corner, local_shape).astype(jnp.float32).reshape(-1, head_count, head_size)
        local_grad = lax.dynamic_slice(grad_out, window_corner, local_shape).astype(jnp.float32).reshape(-1, head_count, head_size)
        in_window = window_mask(windows, frame_index, block_index, row_extent, R_DEV, col_count, frame_total, row_sum_total)
        scores = jnp.einsum('qhd,khd->hqk', local_query, near_keys) * score_scale
        scores = jnp.where(in_window, scores, masked_score)
        row_top = lax.optimization_barrier(jnp.max(scores, axis=2, keepdims=True))
        exp_total = lax.optimization_barrier(jnp.sum(jnp.where(in_window, jnp.exp(scores - row_top), 0.0), axis=2, keepdims=True))
        log_total = row_top + jnp.log(exp_total)
        soft_weights = jnp.where(in_window, jnp.exp(scores - log_total), 0.0)
        weights_low = rounded(soft_weights)
        attended = rounded(jnp.einsum('hqk,khd->qhd', weights_low, near_values))
        out_dot = jnp.einsum('qhd,qhd->hq', local_grad, attended)[:, :, None]
        grad_weights = jnp.einsum('qhd,khd->hqk', local_grad, near_values)
        grad_scores = rounded(soft_weights * (grad_weights - out_dot))
        grad_query = rounded(jnp.einsum('hqk,khd->qhd', grad_scores, near_keys) * score_scale)
        part_keys = (jnp.einsum('hqk,qhd->khd', grad_scores, local_query) * score_scale).reshape(nearby_window_shape)
        partial_value_rows = jnp.einsum('hqk,qhd->khd', weights_low, local_grad).reshape(nearby_window_shape)
        padded_key_gradient = lax.dynamic_update_slice(padded_key_gradient, lax.dynamic_slice(padded_key_gradient, window_corner, nearby_window_shape) + part_keys, window_corner)
        padded_value_gradient = lax.dynamic_update_slice(padded_value_gradient, lax.dynamic_slice(padded_value_gradient, window_corner, nearby_window_shape) + partial_value_rows, window_corner)
        output_rows = (attended.reshape(R_DEV, col_count, feature_count), grad_query.reshape(R_DEV, col_count, feature_count))
        return ((padded_key_gradient, padded_value_gradient), output_rows)
    start_position = (jnp.zeros(keys_pad.shape, jnp.float32), jnp.zeros(values_pad.shape, jnp.float32))
    (padded_key_gradient, padded_value_gradient), (attended_every_head, query_gradient_total) = lax.scan(loop_iteration, start_position, jnp.arange(N_TM * N_SPACE, dtype=jnp.int32))
    attended = attended_every_head.reshape(frame_total, row_sum_total, col_count, feature_count).astype(jnp.bfloat16)
    grad_queries = query_gradient_total.reshape(frame_total, row_sum_total, col_count, feature_count).astype(jnp.bfloat16)
    grad_keys = padded_key_gradient[1:-1, row_extent:row_extent + row_sum_total].astype(jnp.bfloat16)
    value_gradient = padded_value_gradient[1:-1, row_extent:row_extent + row_sum_total].astype(jnp.bfloat16)
    return (attended, grad_queries, grad_keys, value_gradient)
```

```python
import functools
import math

import jax
import jax.numpy as jnp
from jax import lax
from jax.experimental import pallas as pl
from jax.experimental.pallas import tpu as pltpu
from jax.sharding import PartitionSpec as P

masked_score = -1e30
MESH = pl.DeviceIdType.MESH

STEPS = {"A": 0.0, "B": 1.05, "C": 1.9, "D": 3.4, "E": 5.0, "F": 6.6}

IN_PAIR, IN_OTHER, HALO_UP, HALO_DOWN, BACK_UP, BACK_DOWN, BACK_OTHER, BACK_PAIR = (
    0,
    1,
    2,
    5,
    8,
    11,
    14,
    15,
)
KINDS = 16


def dot_nt(a, b):
    return lax.dot_general(a, b, (((1,), (1,)), ((), ())), preferred_element_type=jnp.float32)


def dot_nn(a, b):
    return lax.dot_general(a, b, (((1,), (0,)), ((), ())), preferred_element_type=jnp.float32)


def dot_tn(a, b):
    return lax.dot_general(a, b, (((0,), (0,)), ((), ())), preferred_element_type=jnp.float32)


def kernel(
    sizes,
    win_hbm,
    q_ref,
    k_ref,
    v_ref,
    g_ref,
    att_ref,
    gq_ref,
    gk_ref,
    gv_ref,
    win_ref,
    near,
    own,
    part,
    back_out,
    back_in,
    other_out,
    other_in,
    pair_out,
    pair_in,
    row_gap,
    col_gap,
    load_sem,
    send_sem,
    recv_sem,
):
    head_count, head_size, row_count, col_count, n_tm, n_space = sizes
    tokens = row_count * col_count
    half = tokens // 2
    scale = 1.0 / math.sqrt(head_size)
    tm, sp = lax.axis_index("tm"), lax.axis_index("space")
    side = lax.rem(tm, 2)
    pair = tm + 1 - 2 * side
    relay_to = tm + 2 - 4 * side
    relay_from = tm - 2 + 4 * side
    has_to = (relay_to >= 0) & (relay_to < n_tm)
    has_other = (relay_from >= 0) & (relay_from < n_tm)
    has_up = sp > 0
    has_down = sp < n_space - 1
    heads = range(head_count)

    def when(cond, action):
        if cond is None:
            action()
        else:
            pl.when(cond)(action)

    def load(h, a):
        ref = (k_ref, v_ref, q_ref, g_ref)[a]
        target = near.at[h, a, 0, 0:tokens, :] if a < 2 else own.at[h, a - 2]
        return pltpu.make_async_copy(
            ref.at[:, h * head_size : (h + 1) * head_size],
            target,
            load_sem.at[h, a // 2],
        )

    def load_wait(h, first):
        whole = near.at[h, :, 0, 0:tokens, :] if first else own.at[h]
        pltpu.make_async_copy(whole, whole, load_sem.at[h, 0 if first else 1]).wait()

    barrier = pltpu.get_barrier_semaphore()

    def greet(cond, tm_to, sp_to):
        def signal():
            pl.semaphore_signal(barrier, inc=1, device_id=(tm_to, sp_to), device_id_type=MESH)

        when(cond, signal)

    greet(None, pair, sp)
    greet(has_to, relay_to, sp)
    greet(has_other, relay_from, sp)
    greet(has_up, tm, sp - 1)
    greet(has_down, tm, sp + 1)
    get_windows = pltpu.make_async_copy(win_hbm, win_ref, load_sem.at[head_count, 0])
    for h in heads:
        for a in range(2):
            load(h, a).start()
    get_windows.start()
    for h in heads:
        for a in range(2, 4):
            load(h, a).start()

    def remote(src, dst, send, recv, device):
        return pltpu.make_async_remote_copy(
            src_ref=src,
            dst_ref=dst,
            send_sem=send,
            recv_sem=recv,
            device_id=device,
            device_id_type=MESH,
        )

    def to_pair(h):
        return remote(
            near.at[h, :, 0, 0:tokens, :],
            near.at[h, :, 1, 0:tokens, :],
            send_sem.at[0],
            recv_sem.at[h, IN_PAIR],
            (pair, sp),
        )

    def to_relay(h):
        return remote(
            near.at[h, :, 1, 0:tokens, :],
            near.at[h, :, 2, 0:tokens, :],
            send_sem.at[1],
            recv_sem.at[h, IN_OTHER],
            (relay_to, sp),
        )

    def halo_up(h, slot):
        return remote(
            near.at[h, :, slot, 0:half, :],
            near.at[h, :, slot, tokens : tokens + half, :],
            send_sem.at[2 + slot // 2],
            recv_sem.at[h, HALO_UP + slot],
            (tm, sp - 1),
        )

    def halo_down(h, slot):
        return remote(
            near.at[h, :, slot, half:tokens, :],
            near.at[h, :, slot, tokens + half : 2 * tokens, :],
            send_sem.at[4 + slot // 2],
            recv_sem.at[h, HALO_DOWN + slot],
            (tm, sp + 1),
        )

    def back_up(h, slot):
        return remote(
            back_out.at[h, slot, 1],
            back_in.at[h, slot, 1],
            send_sem.at[6 + slot // 2],
            recv_sem.at[h, BACK_UP + slot],
            (tm, sp - 1),
        )

    def back_down(h, slot):
        return remote(
            back_out.at[h, slot, 0],
            back_in.at[h, slot, 0],
            send_sem.at[8 + slot // 2],
            recv_sem.at[h, BACK_DOWN + slot],
            (tm, sp + 1),
        )

    def back_other(h):
        return remote(
            other_out.at[h],
            other_in.at[h],
            send_sem.at[10],
            recv_sem.at[h, BACK_OTHER],
            (relay_from, sp),
        )

    def back_pair(h):
        return remote(
            pair_out.at[h],
            pair_in.at[h],
            send_sem.at[11],
            recv_sem.at[h, BACK_PAIR],
            (pair, sp),
        )

    def halos(h, slot):
        when(has_up, lambda: halo_up(h, slot).start())
        when(has_down, lambda: halo_down(h, slot).start())

    expected = (
        1
        + has_to.astype(jnp.int32)
        + has_other.astype(jnp.int32)
        + has_up.astype(jnp.int32)
        + has_down.astype(jnp.int32)
    )
    pl.semaphore_wait(barrier, expected)
    for h in heads:
        load_wait(h, True)
        to_pair(h).start()
    for h in heads:
        halos(h, 0)

    @pl.when(jnp.logical_not(has_other))
    def _():
        near[:, :, 2] = jnp.zeros((head_count, 2, 2 * tokens, head_size), near.dtype)

    @pl.when(jnp.logical_not(has_to))
    def _():
        other_in[...] = jnp.zeros_like(other_in)

    @pl.when(jnp.logical_not(has_down))
    def _():
        near[:, :, :, tokens : tokens + half, :] = jnp.zeros(
            (head_count, 2, 3, half, head_size), near.dtype
        )
        back_in[:, :, 1] = jnp.zeros((head_count, 3, 2, half, head_size), near.dtype)

    @pl.when(jnp.logical_not(has_up))
    def _():
        near[:, :, :, tokens + half :, :] = jnp.zeros(
            (head_count, 2, 3, half, head_size), near.dtype
        )
        back_in[:, :, 0] = jnp.zeros((head_count, 3, 2, half, head_size), near.dtype)

    near_id = lax.broadcasted_iota(jnp.int32, (2 * tokens, tokens), 0)
    own_id = lax.broadcasted_iota(jnp.int32, (2 * tokens, tokens), 1)
    own_row, own_col = own_id // col_count, own_id % col_count
    near_row, near_col = near_id // col_count, near_id % col_count
    upper = near_row >= row_count + row_count // 2
    near_row = jnp.where(upper, near_row - 2 * row_count, near_row)
    global_row = sp * row_count + near_row
    row_inside = (global_row >= 0) & (global_row < n_space * row_count)
    row_gap[...] = jnp.where(row_inside, jnp.abs(own_row - near_row), 1 << 20)
    col_gap[...] = jnp.abs(own_col - near_col)

    for h in heads:
        load_wait(h, False)
    get_windows.wait()

    def compute(h):
        cols = slice(h * head_size, (h + 1) * head_size)
        query, grad = own[h, 0], own[h, 1]
        keys = near[h, 0].reshape(6 * tokens, head_size)
        vals = near[h, 1].reshape(6 * tokens, head_size)
        row_reach, col_reach = win_ref[0, h], win_ref[1, h]
        col_in = col_gap[...] <= col_reach
        here = (row_gap[...] <= row_reach) & col_in
        there = (row_gap[...] <= jnp.where(has_other, row_reach, -1)) & col_in
        window = jnp.concatenate([here, here, there], axis=0)
        scores = jnp.where(window, dot_nt(keys, query) * scale, masked_score)
        top = jnp.max(scores, axis=0, keepdims=True)
        powers = jnp.exp(scores - top)
        total = jnp.sum(powers, axis=0, keepdims=True)
        soft = powers * (1.0 / total)
        weights = soft.astype(jnp.bfloat16)
        grad_weights = dot_nt(vals, grad)
        out_dot = jnp.sum(soft * grad_weights, axis=0, keepdims=True)
        grad_scores = (soft * (grad_weights - out_dot)).astype(jnp.bfloat16)
        for a, partial in ((0, dot_nn(grad_scores, query)), (1, dot_nn(weights, grad))):
            for slot in range(3):
                at = 2 * slot * tokens
                part[h, slot, a] = partial[at : at + tokens]
                back_out[h, slot, 0, a] = partial[at + tokens : at + tokens + half].astype(
                    jnp.bfloat16
                )
                back_out[h, slot, 1, a] = partial[at + tokens + half : at + 2 * tokens].astype(
                    jnp.bfloat16
                )
        for slot in (2, 1, 0):
            cond_up = has_up if slot < 2 else has_up & has_other
            cond_down = has_down if slot < 2 else has_down & has_other
            when(cond_up, lambda: back_up(h, slot).start())
            when(cond_down, lambda: back_down(h, slot).start())
        att_ref[:, cols] = dot_tn(weights, vals).astype(jnp.bfloat16)
        gq_ref[:, cols] = (dot_tn(grad_scores, keys) * scale).astype(jnp.bfloat16)

    def step_a(h):
        to_pair(h).wait_recv()
        when(has_to, lambda: to_relay(h).start())
        halos(h, 1)

    def step_b(h):
        @pl.when(has_other)
        def _():
            to_relay(h).wait_recv()
            halos(h, 2)

    def step_c(h):
        @pl.when(has_down)
        def _():
            halo_up(h, 0).wait_recv()
            halo_up(h, 1).wait_recv()

        @pl.when(has_up)
        def _():
            halo_down(h, 0).wait_recv()
            halo_down(h, 1).wait_recv()

        when(has_down & has_other, lambda: halo_up(h, 2).wait_recv())
        when(has_up & has_other, lambda: halo_down(h, 2).wait_recv())
        compute(h)

    def arrive_back(h, slot):
        when(has_down, lambda: back_up(h, slot).wait_recv())
        when(has_up, lambda: back_down(h, slot).wait_recv())

    def summed(h, slot, a):
        halo = jnp.concatenate([back_in[h, slot, 0, a], back_in[h, slot, 1, a]], axis=0)
        return part[h, slot, a] + halo.astype(jnp.float32)

    def step_d(h):
        @pl.when(has_other)
        def _():
            arrive_back(h, 2)
            for a in range(2):
                other_out[h, a] = summed(h, 2, a).astype(jnp.bfloat16)
            back_other(h).start()

    def step_e(h):
        arrive_back(h, 1)
        when(has_to, lambda: back_other(h).wait_recv())
        for a in range(2):
            pair_out[h, a] = (summed(h, 1, a) + other_in[h, a].astype(jnp.float32)).astype(
                jnp.bfloat16
            )
        back_pair(h).start()

    def step_f(h):
        cols = slice(h * head_size, (h + 1) * head_size)
        arrive_back(h, 0)
        back_pair(h).wait_recv()
        key_sum = summed(h, 0, 0) + pair_in[h, 0].astype(jnp.float32)
        gk_ref[:, cols] = (key_sum * scale).astype(jnp.bfloat16)
        value_sum = summed(h, 0, 1) + pair_in[h, 1].astype(jnp.float32)
        gv_ref[:, cols] = value_sum.astype(jnp.bfloat16)

    steps = {"A": step_a, "B": step_b, "C": step_c, "D": step_d, "E": step_e, "F": step_f}
    order = sorted((h + STEPS[name], name, h) for name in steps for h in heads)
    for _, name, h in order:
        steps[name](h)

    def drain(cond, ref, i):
        when(cond, remote(ref, ref, send_sem.at[i], recv_sem.at[0, 0], (pair, sp)).wait_send)

    mine = near.at[:, :, 1, 0:tokens, :]
    early = near.at[:, :, 0:2, 0:half, :]
    late = near.at[:, :, 2, 0:half, :]
    drain(None, mine, 0)
    drain(has_to, mine, 1)
    for i, cond in ((2, has_up), (4, has_down), (6, has_up), (8, has_down)):
        drain(cond, early, i)
        drain(cond & has_other, late, i + 1) if i < 6 else None
    drain(has_up & has_other, late, 7)
    drain(has_down & has_other, late, 9)
    drain(has_other, other_out, 10)
    drain(None, pair_out, 11)


def put_out(*refs):
    sources, targets, sems = refs[:4], refs[4:8], refs[8]
    copies = [pltpu.make_async_copy(sources[i], targets[i], sems.at[i]) for i in range(4)]
    for copy in copies:
        copy.start()
    for copy in copies:
        copy.wait()


def on_device(queries, key_vectors, values, grad_out, windows):
    local_shape = queries.shape
    row_count, col_count, features = local_shape[1:]
    head_count = windows.shape[1]
    head_size = features // head_count
    tokens = row_count * col_count
    half = tokens // 2
    sizes = (
        head_count,
        head_size,
        row_count,
        col_count,
        lax.axis_size("tm"),
        lax.axis_size("space"),
    )
    flat = (tokens, features)
    low = jnp.bfloat16
    outs = pl.pallas_call(
        functools.partial(kernel, sizes),
        out_shape=[jax.ShapeDtypeStruct(flat, low)] * 4,
        in_specs=[pl.BlockSpec(memory_space=pltpu.HBM)] * 5,
        out_specs=[pl.BlockSpec(memory_space=pltpu.VMEM)] * 4,
        scratch_shapes=[
            pltpu.SMEM((2, head_count), jnp.int32),
            pltpu.VMEM((head_count, 2, 3, 2 * tokens, head_size), low),
            pltpu.VMEM((head_count, 2, tokens, head_size), low),
            pltpu.VMEM((head_count, 3, 2, tokens, head_size), jnp.float32),
            pltpu.VMEM((head_count, 3, 2, 2, half, head_size), low),
            pltpu.VMEM((head_count, 3, 2, 2, half, head_size), low),
            pltpu.VMEM((head_count, 2, tokens, head_size), low),
            pltpu.VMEM((head_count, 2, tokens, head_size), low),
            pltpu.VMEM((head_count, 2, tokens, head_size), low),
            pltpu.VMEM((head_count, 2, tokens, head_size), low),
            pltpu.VMEM((2 * tokens, tokens), jnp.int32),
            pltpu.VMEM((2 * tokens, tokens), jnp.int32),
            pltpu.SemaphoreType.DMA((head_count + 1, 2)),
            pltpu.SemaphoreType.DMA((12,)),
            pltpu.SemaphoreType.DMA((head_count, KINDS)),
        ],
        compiler_params=pltpu.CompilerParams(
            collective_id=0, has_side_effects=True, vmem_limit_bytes=55_600_000
        ),
    )(
        windows,
        queries.reshape(flat),
        key_vectors.reshape(flat),
        values.reshape(flat),
        grad_out.reshape(flat),
    )
    outs = pl.pallas_call(
        put_out,
        out_shape=[jax.ShapeDtypeStruct(flat, low)] * 4,
        in_specs=[pl.BlockSpec(memory_space=pltpu.VMEM)] * 4,
        out_specs=[pl.BlockSpec(memory_space=pltpu.HBM)] * 4,
        scratch_shapes=[
            pltpu.SemaphoreType.DMA((4,)),
        ],
        compiler_params=pltpu.CompilerParams(vmem_limit_bytes=4_000_000),
    )(*outs)
    return tuple(out.reshape(local_shape) for out in outs)


def solution(mesh):
    spec = P("tm", "space", None, None)
    return jax.shard_map(
        on_device,
        mesh=mesh,
        in_specs=(spec, spec, spec, spec, P()),
        out_specs=(spec, spec, spec, spec),
        check_vma=False,
    )
```

```python
import functools
import math

import jax
import jax.numpy as jnp
from jax import lax
from jax.experimental import pallas as pl
from jax.experimental.pallas import tpu as pltpu
from jax.sharding import PartitionSpec as P

masked_score = -1e30
MESH = pl.DeviceIdType.MESH

OUTER, OWN, PAIR, FAR = range(4)

FROM_PAIR, TO_FAR, TO_OUTER = range(3)


def dot_nt(a, b):
    return lax.dot_general(a, b, (((1,), (1,)), ((), ())), preferred_element_type=jnp.float32)


def dot_nn(a, b):
    return lax.dot_general(a, b, (((1,), (0,)), ((), ())), preferred_element_type=jnp.float32)


def when(cond, action):
    if cond is None:
        action()
    else:
        pl.when(cond)(action)


def both(a, b):
    if a is None:
        return b
    return a if b is None else a & b


def kernel(
    sizes,
    win_hbm,
    q_ref,
    k_ref,
    v_ref,
    g_ref,
    att_ref,
    gq_ref,
    gk_ref,
    gv_ref,
    win_ref,
    bias,
    staged,
    near,
    results,
    st_main,
    st_down,
    st_up,
    load_sem,
    win_sem,
    send_sem,
    piece_sem,
    halo_sem,
    result_sem,
    stat_send,
    stat_recv,
):
    head_count, head_size, row_count, col_count, n_tm, n_space = sizes
    tokens = row_count * col_count
    half = tokens // 2
    mine = head_count // 2
    scale = 1.0 / math.sqrt(head_size)
    scale2 = scale * math.log2(math.e)
    tm, sp = lax.axis_index("tm"), lax.axis_index("space")
    side = lax.rem(tm, 2)
    pair = tm + 1 - 2 * side
    inner_to = tm + 2 - 4 * side
    outer_to = tm - 2 + 4 * side
    has_far = (inner_to >= 0) & (inner_to < n_tm)
    has_outer = (outer_to >= 0) & (outer_to < n_tm)
    has_up = sp > 0
    has_down = sp < n_space - 1
    held = {OUTER: has_outer, OWN: None, PAIR: None, FAR: has_far}
    heads = range(mine)
    pieces = [(phase, j, a) for phase in range(2) for j in heads for a in range(2)]
    ins = ((k_ref, v_ref), (q_ref, g_ref))
    outs = (att_ref, gq_ref, gk_ref, gv_ref)

    def head_cols(j, of_pair=False):
        first = (1 - side if of_pair else side) * mine + j
        return pl.ds(pl.multiple_of(first * head_size, head_size), head_size)

    st_main[...] = jnp.zeros_like(st_main)
    st_down[...] = jnp.zeros_like(st_down)
    st_up[...] = jnp.zeros_like(st_up)

    barrier = pltpu.get_barrier_semaphore()

    def greet(cond, tm_to, sp_to):
        def signal():
            pl.semaphore_signal(barrier, inc=1, device_id=(tm_to, sp_to), device_id_type=MESH)

        when(cond, signal)

    greet(None, pair, sp)
    greet(has_far, inner_to, sp)
    greet(has_outer, outer_to, sp)
    greet(has_up, tm, sp - 1)
    greet(has_down, tm, sp + 1)

    def main_rows(i, slot):
        phase, j, a = pieces[i]
        return near.at[phase, j, a, slot, 0:tokens, :]

    def load(i, of_pair):
        phase, j, a = pieces[i]
        return pltpu.make_async_copy(
            ins[phase][a].at[:, head_cols(j, of_pair)],
            staged.at[i] if of_pair else main_rows(i, OWN),
            load_sem.at[i, 1 if of_pair else 0],
        )

    for of_pair in (True, False):
        for i in range(len(pieces)):
            load(i, of_pair).start()
    get_windows = pltpu.make_async_copy(win_hbm, win_ref, win_sem)
    get_windows.start()

    def remote(src, dst, send, recv, device):
        return pltpu.make_async_remote_copy(
            src_ref=src,
            dst_ref=dst,
            send_sem=send,
            recv_sem=recv,
            device_id=device,
            device_id_type=MESH,
        )

    def to_pair(i):
        return remote(
            staged.at[i],
            main_rows(i, PAIR),
            send_sem.at[0],
            piece_sem.at[i, FROM_PAIR],
            (pair, sp),
        )

    def own_to_far(i):
        return remote(
            main_rows(i, OWN),
            main_rows(i, FAR),
            send_sem.at[1],
            piece_sem.at[i, TO_FAR],
            (outer_to, sp),
        )

    def pair_to_outer(i):
        return remote(
            main_rows(i, PAIR),
            main_rows(i, OUTER),
            send_sem.at[2],
            piece_sem.at[i, TO_OUTER],
            (inner_to, sp),
        )

    def halo_up(i, slot):
        phase, j, a = pieces[i]
        rows = near.at[phase, j, a, slot]
        return remote(
            rows.at[0:half, :],
            rows.at[tokens : tokens + half, :],
            send_sem.at[3 + slot],
            halo_sem.at[phase * mine + j, slot, 0],
            (tm, sp - 1),
        )

    def halo_down(i, slot):
        phase, j, a = pieces[i]
        rows = near.at[phase, j, a, slot]
        return remote(
            rows.at[half:tokens, :],
            rows.at[tokens + half : 2 * tokens, :],
            send_sem.at[7 + slot],
            halo_sem.at[phase * mine + j, slot, 1],
            (tm, sp + 1),
        )

    def halos(i, slot):
        when(has_up, lambda: halo_up(i, slot).start())
        when(has_down, lambda: halo_down(i, slot).start())

    expected = (
        1
        + has_far.astype(jnp.int32)
        + has_outer.astype(jnp.int32)
        + has_up.astype(jnp.int32)
        + has_down.astype(jnp.int32)
    )
    pl.semaphore_wait(barrier, expected)
    for i in range(len(pieces)):
        load(i, True).wait()
        to_pair(i).start()
    for i in range(len(pieces)):
        load(i, False).wait()
        when(has_outer, lambda: own_to_far(i).start())
        halos(i, OWN)

    def clear(slots, rows):
        count = rows.stop - rows.start
        for phase in range(2):
            for j in heads:
                for slot in slots:
                    near[phase, j, :, slot, rows, :] = jnp.zeros(
                        (2, count, head_size), near.dtype
                    )

    slots = (OUTER, OWN, PAIR, FAR)
    pl.when(jnp.logical_not(has_outer))(lambda: clear((OUTER,), slice(0, 2 * tokens)))
    pl.when(jnp.logical_not(has_far))(lambda: clear((FAR,), slice(0, 2 * tokens)))
    pl.when(jnp.logical_not(has_down))(lambda: clear(slots, slice(tokens, tokens + half)))
    pl.when(jnp.logical_not(has_up))(lambda: clear(slots, slice(tokens + half, 2 * tokens)))

    own_id = lax.broadcasted_iota(jnp.int32, (tokens, 2 * tokens), 0)
    near_id = lax.broadcasted_iota(jnp.int32, (tokens, 2 * tokens), 1)
    own_row, own_col = own_id // col_count, own_id % col_count
    near_row, near_col = near_id // col_count, near_id % col_count
    upper = near_row >= row_count + row_count // 2
    near_row = jnp.where(upper, near_row - 2 * row_count, near_row)
    global_row = sp * row_count + near_row
    row_inside = (global_row >= 0) & (global_row < n_space * row_count)
    row_gap = jnp.where(row_inside, jnp.abs(own_row - near_row), 1 << 20)
    col_gap = jnp.abs(own_col - near_col)

    get_windows.wait()
    for j in heads:
        h = side * mine + j
        inside = (row_gap <= win_ref[0, h]) & (col_gap <= win_ref[1, h])
        bias[j] = jnp.where(inside, 0.0, masked_score)

    def window(j, frame):
        here = bias[j]
        there = here + jnp.where(has_outer if frame == OWN else has_far, 0.0, masked_score)
        order = [there, here, here] if frame == OWN else [here, here, there]
        return jnp.concatenate(order, axis=1)

    def around(phase, j, a, frame):
        return near[phase, j, a, frame - 1 : frame + 2].reshape(6 * tokens, head_size)

    def put(kind, j, frame, value):
        if frame == OWN:
            outs[kind][:, head_cols(j)] = value
        else:
            results[kind, j] = value

    def give(kind, j):
        return remote(
            results.at[kind, j],
            outs[kind].at[:, head_cols(j)],
            send_sem.at[11],
            result_sem.at[kind, j],
            (pair, sp),
        )

    def forward(j, frame):
        query = near[1, j, 0, frame, 0:tokens, :]
        grad = near[1, j, 1, frame, 0:tokens, :]
        keys, vals = around(0, j, 0, frame), around(0, j, 1, frame)
        scores = dot_nt(query, keys) * scale2 + window(j, frame)
        top = jnp.max(scores, axis=1, keepdims=True)
        powers = jnp.exp2(scores - top)
        total = jnp.sum(powers, axis=1, keepdims=True)
        share = 1.0 / total
        attended = dot_nn(powers.astype(jnp.bfloat16), vals) * share
        put(0, j, frame, attended.astype(jnp.bfloat16))
        grad_weights = dot_nt(grad, vals)
        out_dot = jnp.sum(powers * grad_weights, axis=1, keepdims=True) * share
        grad_scores = (powers * (grad_weights - out_dot)).astype(jnp.bfloat16)
        put(1, j, frame, (dot_nn(grad_scores, keys) * (share * scale)).astype(jnp.bfloat16))
        return top + jnp.log2(total), out_dot

    row_lane = lax.broadcasted_iota(jnp.int32, (1, tokens), 1)

    def stat_row(j, r, frame):
        parts = []
        for slot in range(frame - 1, frame + 2):
            parts.append(st_main[j, slot, r : r + 1, :])
            down, up = st_down[j, slot, r : r + 1, :], st_up[j, slot, r : r + 1, :]
            parts.append(jnp.where(row_lane < half, down, up))
        return jnp.concatenate(parts, axis=1)

    def backward(j, frame):
        key = near[0, j, 0, frame, 0:tokens, :]
        val = near[0, j, 1, frame, 0:tokens, :]
        queries, grads = around(1, j, 0, frame), around(1, j, 1, frame)
        scores = dot_nt(key, queries) * scale2 + window(j, frame)
        soft = jnp.exp2(scores - stat_row(j, 0, frame))
        put(3, j, frame, dot_nn(soft.astype(jnp.bfloat16), grads).astype(jnp.bfloat16))
        grad_scores = soft * (dot_nt(val, grads) - stat_row(j, 1, frame))
        key_sum = dot_nn(grad_scores.astype(jnp.bfloat16), queries)
        put(2, j, frame, (key_sum * scale).astype(jnp.bfloat16))

    def stat_copies(j):
        far_frame, near_frame = st_main.at[j, PAIR], st_main.at[j, OWN]
        both_frames = slice(OWN, PAIR + 1)
        found = [
            (has_far, far_frame, st_main.at[j, OUTER], (inner_to, sp), has_outer),
            (has_outer, near_frame, st_main.at[j, FAR], (outer_to, sp), has_far),
        ]
        for at, there, goes, comes in (
            (st_down, sp - 1, has_up, has_down),
            (st_up, sp + 1, has_down, has_up),
        ):
            found += [
                (goes, st_main.at[j, both_frames], at.at[j, both_frames], (tm, there), comes),
                (goes & has_far, far_frame, at.at[j, OUTER], (inner_to, there), comes & has_outer),
                (goes & has_outer, near_frame, at.at[j, FAR], (outer_to, there), comes & has_far),
            ]
        return [
            (goes, comes, remote(src, dst, stat_send.at[j, i], stat_recv.at[j, i], device))
            for i, (goes, src, dst, device, comes) in enumerate(found)
        ]

    def step_pair_in(i):
        to_pair(i).wait_recv()
        when(has_far, lambda: pair_to_outer(i).start())
        halos(i, PAIR)

    def step_far_in(i):
        @pl.when(has_far)
        def _():
            own_to_far(i).wait_recv()
            halos(i, FAR)

    def step_outer_in(i):
        @pl.when(has_outer)
        def _():
            pair_to_outer(i).wait_recv()
            halos(i, OUTER)

    def arrive_halos(phase, j, slots):
        for slot in slots:
            rows = near.at[phase, j, :, slot, 0:half, :]
            for side_in, cond in ((0, has_down), (1, has_up)):
                sem = halo_sem.at[phase * mine + j, slot, side_in]
                copy = remote(rows, rows, send_sem.at[0], sem, (pair, sp))
                when(both(cond, held[slot]), copy.wait_recv)

    stats = {}

    def step_forward_pair(j):
        arrive_halos(0, j, (OWN, PAIR, FAR))
        stats[j] = forward(j, PAIR)
        for kind in (0, 1):
            give(kind, j).start()

    def step_forward_own(j):
        arrive_halos(0, j, (OUTER,))
        found = (*forward(j, OWN), *stats.pop(j))
        lane = lax.broadcasted_iota(jnp.int32, (tokens, tokens), 1)
        spread = jnp.zeros((tokens, tokens), jnp.float32)
        for at, column in zip((0, 1, 8, 9), found, strict=True):
            spread = jnp.where(lane == at, column, spread)
        st_main[j, OWN : PAIR + 1] = spread.T[0:16, :].reshape(2, 8, tokens)
        for goes, _, copy in stat_copies(j):
            when(goes, copy.start)

    def step_backward_pair(j):
        arrive_halos(1, j, (OWN, PAIR, FAR, OUTER))
        for _, comes, copy in stat_copies(j):
            when(comes, copy.wait_recv)
        backward(j, PAIR)
        for kind in (2, 3):
            give(kind, j).start()

    def step_backward_own(j):
        backward(j, OWN)

    times = []
    for i in range(len(pieces)):
        times.append((4.6 + 0.7 * i, step_pair_in, i))
        times.append((4.65 + 0.7 * i, step_far_in, i))
        times.append((7.0 + 0.7 * i, step_outer_in, i))
    for j in heads:
        times.append((9.7 + 1.4 * j, step_forward_pair, j))
        times.append((10.3 + 1.4 * j, step_forward_own, j))
        times.append((13.9 + 1.4 * j, step_backward_pair, j))
        times.append((14.5 + 1.4 * j, step_backward_own, j))
    for _, step, index in sorted(times, key=lambda entry: entry[0]):
        step(index)

    for kind in range(4):
        for j in heads:
            give(kind, j).wait_recv()

    def drain(cond, ref, i):
        when(cond, remote(ref, ref, send_sem.at[i], result_sem.at[0, 0], (pair, sp)).wait_send)

    whole = near.at[:, :, :, PAIR, 0:tokens, :]
    part = near.at[:, :, :, PAIR, 0:half, :]
    drain(None, whole, 0)
    drain(has_outer, whole, 1)
    drain(has_far, whole, 2)
    for slot in slots:
        drain(both(has_up, held[slot]), part, 3 + slot)
        drain(both(has_down, held[slot]), part, 7 + slot)
    drain(None, results, 11)
    for j in heads:
        for goes, _, copy in stat_copies(j):
            when(goes, copy.wait_send)


def put_out(*refs):
    sources, targets, sems = refs[:4], refs[4:8], refs[8]
    copies = [pltpu.make_async_copy(sources[i], targets[i], sems.at[i]) for i in range(4)]
    for copy in copies:
        copy.start()
    for copy in copies:
        copy.wait()


def on_device(queries, key_vectors, values, grad_out, windows):
    local_shape = queries.shape
    row_count, col_count, features = local_shape[1:]
    head_count = windows.shape[1]
    head_size = features // head_count
    tokens = row_count * col_count
    mine = head_count // 2
    sizes = (
        head_count,
        head_size,
        row_count,
        col_count,
        lax.axis_size("tm"),
        lax.axis_size("space"),
    )
    flat = (tokens, features)
    low = jnp.bfloat16
    outs = pl.pallas_call(
        functools.partial(kernel, sizes),
        out_shape=[jax.ShapeDtypeStruct(flat, low)] * 4,
        in_specs=[pl.BlockSpec(memory_space=pltpu.HBM)] * 5,
        out_specs=[pl.BlockSpec(memory_space=pltpu.VMEM)] * 4,
        scratch_shapes=[
            pltpu.SMEM((2, head_count), jnp.int32),
            pltpu.VMEM((mine, tokens, 2 * tokens), jnp.float32),
            pltpu.VMEM((4 * mine, tokens, head_size), low),
            pltpu.VMEM((2, mine, 2, 4, 2 * tokens, head_size), low),
            pltpu.VMEM((4, mine, tokens, head_size), low),
            pltpu.VMEM((mine, 4, 8, tokens), jnp.float32),
            pltpu.VMEM((mine, 4, 8, tokens), jnp.float32),
            pltpu.VMEM((mine, 4, 8, tokens), jnp.float32),
            pltpu.SemaphoreType.DMA((4 * mine, 2)),
            pltpu.SemaphoreType.DMA,
            pltpu.SemaphoreType.DMA((12,)),
            pltpu.SemaphoreType.DMA((4 * mine, 3)),
            pltpu.SemaphoreType.DMA((2 * mine, 4, 2)),
            pltpu.SemaphoreType.DMA((4, mine)),
            pltpu.SemaphoreType.DMA((mine, 8)),
            pltpu.SemaphoreType.DMA((mine, 8)),
        ],
        compiler_params=pltpu.CompilerParams(
            collective_id=0, has_side_effects=True, vmem_limit_bytes=55_600_000
        ),
    )(
        windows,
        queries.reshape(flat),
        key_vectors.reshape(flat),
        values.reshape(flat),
        grad_out.reshape(flat),
    )
    outs = pl.pallas_call(
        put_out,
        out_shape=[jax.ShapeDtypeStruct(flat, low)] * 4,
        in_specs=[pl.BlockSpec(memory_space=pltpu.VMEM)] * 4,
        out_specs=[pl.BlockSpec(memory_space=pltpu.HBM)] * 4,
        scratch_shapes=[
            pltpu.SemaphoreType.DMA((4,)),
        ],
        compiler_params=pltpu.CompilerParams(vmem_limit_bytes=4_000_000),
    )(*outs)
    return tuple(out.reshape(local_shape) for out in outs)


def solution(mesh):
    spec = P("tm", "space", None, None)
    return jax.shard_map(
        on_device,
        mesh=mesh,
        in_specs=(spec, spec, spec, spec, P()),
        out_specs=(spec, spec, spec, spec),
        check_vma=False,
    )
```

```python
import functools
import math

import jax
import jax.numpy as jnp
from jax import lax
from jax.experimental import pallas as pl
from jax.experimental.pallas import tpu as pltpu
from jax.sharding import PartitionSpec as P

masked_score = -1e30
MESH = pl.DeviceIdType.MESH

OUTER, OWN, PAIR, FAR = range(4)

STAT_OWN, STAT_PAIR, STAT_OUTER, STAT_FAR = range(4)
ABOVE, BELOW = 4, 8

TO_PAIR, TO_FAR, TO_OUTER, RESULT, UP, DOWN, STAT = 0, 1, 2, 3, 4, 7, 10


def dot_nt(a, b):
    return lax.dot_general(a, b, (((1,), (1,)), ((), ())), preferred_element_type=jnp.float32)


def dot_nn(a, b):
    return lax.dot_general(a, b, (((1,), (0,)), ((), ())), preferred_element_type=jnp.float32)


def when(cond, action):
    if cond is None:
        action()
    else:
        pl.when(cond)(action)


def kernel(
    sizes,
    win_hbm,
    q_ref,
    k_ref,
    v_ref,
    g_ref,
    att_ref,
    gq_ref,
    gk_ref,
    gv_ref,
    win_ref,
    bias,
    near,
    results,
    stats,
    no_rows,
    no_stats,
    load_sem,
    send_sem,
    pair_sem,
    outer_sem,
    far_sem,
    halo_sem,
    stat_sem,
    result_sem,
):
    head_count, head_size, row_count, col_count, n_tm, n_space = sizes
    tokens = row_count * col_count
    half = tokens // 2
    mine = head_count // 2
    scale = 1.0 / math.sqrt(head_size)
    scale2 = scale * math.log2(math.e)
    tm, sp = lax.axis_index("tm"), lax.axis_index("space")
    side = lax.rem(tm, 2)
    pair = tm + 1 - 2 * side
    inner_to = tm + 2 - 4 * side
    outer_to = tm - 2 + 4 * side
    has_far = (inner_to >= 0) & (inner_to < n_tm)
    has_outer = (outer_to >= 0) & (outer_to < n_tm)
    has_up = sp > 0
    has_down = sp < n_space - 1
    heads = range(mine)
    pieces = [(phase, j, a) for phase in range(2) for j in heads for a in range(2)]
    ins = ((k_ref, v_ref), (q_ref, g_ref))
    outs = (att_ref, gq_ref, gk_ref, gv_ref)

    def head_cols(j, of_pair=False):
        first = (1 - side if of_pair else side) * mine + j
        return pl.ds(pl.multiple_of(first * head_size, head_size), head_size)

    barrier = pltpu.get_barrier_semaphore()

    def greet(cond, tm_to, sp_to):
        def signal():
            pl.semaphore_signal(barrier, inc=1, device_id=(tm_to, sp_to), device_id_type=MESH)

        when(cond, signal)

    greet(None, pair, sp)
    greet(has_far, inner_to, sp)
    greet(has_outer, outer_to, sp)
    greet(has_up, tm, sp - 1)
    greet(has_down, tm, sp + 1)

    def main_rows(i, slot):
        phase, j, a = pieces[i]
        return near.at[phase, j, a, slot, 0:tokens, :]

    def load(i):
        phase, j, a = pieces[i]
        return pltpu.make_async_copy(
            ins[phase][a].at[:, head_cols(j)], main_rows(i, OWN), load_sem.at[phase]
        )

    for i in range(len(pieces)):
        load(i).start()
    get_windows = pltpu.make_async_copy(win_hbm, win_ref, load_sem.at[2])
    get_windows.start()
    no_rows[...] = jnp.zeros_like(no_rows)
    no_stats[...] = jnp.zeros_like(no_stats)

    def remote(src, dst, send, recv, device):
        return pltpu.make_async_remote_copy(
            src_ref=src,
            dst_ref=dst,
            send_sem=send,
            recv_sem=recv,
            device_id=device,
            device_id_type=MESH,
        )

    def to_pair(i):
        phase, j, a = pieces[i]
        return remote(
            ins[phase][a].at[:, head_cols(j, True)],
            main_rows(i, PAIR),
            send_sem.at[TO_PAIR],
            pair_sem.at[i],
            (pair, sp),
        )

    def own_to_far(i):
        phase, j, a = pieces[i]
        return remote(
            main_rows(i, OWN),
            main_rows(i, FAR),
            send_sem.at[TO_FAR],
            far_sem.at[phase, j],
            (outer_to, sp),
        )

    def pair_to_outer(i):
        return remote(
            main_rows(i, PAIR),
            main_rows(i, OUTER),
            send_sem.at[TO_OUTER],
            outer_sem.at[i],
            (inner_to, sp),
        )

    def of_kind(slot):
        return {OUTER: 1, FAR: 2}.get(slot, 0)

    def halo_up(i, slot):
        phase, j, a = pieces[i]
        rows = near.at[phase, j, a, slot]
        return remote(
            rows.at[0:half, :],
            rows.at[tokens : tokens + half, :],
            send_sem.at[UP + of_kind(slot)],
            halo_sem.at[phase, j, of_kind(slot) % 2],
            (tm, sp - 1),
        )

    def halo_down(i, slot):
        phase, j, a = pieces[i]
        rows = near.at[phase, j, a, slot]
        return remote(
            rows.at[half:tokens, :],
            rows.at[tokens + half : 2 * tokens, :],
            send_sem.at[DOWN + of_kind(slot)],
            halo_sem.at[phase, j, of_kind(slot) % 2],
            (tm, sp + 1),
        )

    def halos(i, slot):
        when(has_up, lambda: halo_up(i, slot).start())
        when(has_down, lambda: halo_down(i, slot).start())

    expected = (
        1
        + has_far.astype(jnp.int32)
        + has_outer.astype(jnp.int32)
        + has_up.astype(jnp.int32)
        + has_down.astype(jnp.int32)
    )
    pl.semaphore_wait(barrier, expected)
    for i in range(len(pieces)):
        to_pair(i).start()
    for phase in range(2):
        rows = near.at[phase, :, :, OWN, 0:tokens, :]
        pltpu.make_async_copy(rows, rows, load_sem.at[phase]).wait()
        for i in range(len(pieces)):
            if pieces[i][0] == phase:
                when(has_outer, lambda: own_to_far(i).start())
                halos(i, OWN)

    def fill(source, target, sem):
        pltpu.make_async_copy(source, target, sem).start()

    def fill_side(first_row, first_stat):
        rows = slice(first_row, first_row + half)

        def all_frames():
            for phase in range(2):
                for j in heads:
                    at = near.at[phase, j, :, :, rows, :]
                    fill(no_rows.at[:, 0:1], at.at[:, 0:1], halo_sem.at[phase, j, 1])
                    fill(no_rows.at[:, 1:4], at.at[:, 1:4], halo_sem.at[phase, j, 0])
            for j in heads:
                fill(no_stats, stats.at[j, first_stat : first_stat + 4], stat_sem.at[j])

        def one_frame(slot, stat):
            for phase in range(2):
                for j in heads:
                    sem = halo_sem.at[phase, j, of_kind(slot) % 2]
                    fill(no_rows.at[:, slot], near.at[phase, j, :, slot, rows, :], sem)
            for j in heads:
                fill(no_stats.at[0], stats.at[j, first_stat + stat], stat_sem.at[j])

        return all_frames, one_frame

    for has_side, parts in (
        (has_down, fill_side(tokens, BELOW)),
        (has_up, fill_side(tokens + half, ABOVE)),
    ):
        all_frames, one_frame = parts
        pl.when(jnp.logical_not(has_side))(all_frames)
        no_outer, no_far = jnp.logical_not(has_outer), jnp.logical_not(has_far)
        pl.when(has_side & no_outer)(lambda: one_frame(OUTER, STAT_OUTER))
        pl.when(has_side & no_far)(lambda: one_frame(FAR, STAT_FAR))

    for has_frame, slot, stat in ((has_outer, OUTER, STAT_OUTER), (has_far, FAR, STAT_FAR)):

        @pl.when(jnp.logical_not(has_frame))
        def _():
            for phase in range(2):
                for j in heads:
                    near[phase, j, :, slot, 0:tokens, :] = jnp.zeros(
                        (2, tokens, head_size), near.dtype
                    )
            for j in heads:
                fill(no_stats.at[0], stats.at[j, stat], stat_sem.at[j])

    own_id = lax.broadcasted_iota(jnp.int32, (tokens, 2 * tokens), 0)
    near_id = lax.broadcasted_iota(jnp.int32, (tokens, 2 * tokens), 1)
    own_row, own_col = own_id // col_count, own_id % col_count
    near_row, near_col = near_id // col_count, near_id % col_count
    upper = near_row >= row_count + row_count // 2
    near_row = jnp.where(upper, near_row - 2 * row_count, near_row)
    global_row = sp * row_count + near_row
    row_inside = (global_row >= 0) & (global_row < n_space * row_count)
    row_gap = jnp.where(row_inside, jnp.abs(own_row - near_row), 1 << 20)
    col_gap = jnp.abs(own_col - near_col)

    get_windows.wait()
    for j in heads:
        h = side * mine + j
        inside = (row_gap <= win_ref[0, h]) & (col_gap <= win_ref[1, h])
        bias[j] = jnp.where(inside, 0.0, masked_score)

    def window(j, frame):
        here = bias[j]
        there = here + jnp.where(has_outer if frame == OWN else has_far, 0.0, masked_score)
        order = [there, here, here] if frame == OWN else [here, here, there]
        return jnp.concatenate(order, axis=1)

    def around(phase, j, a, frame):
        return near[phase, j, a, frame - 1 : frame + 2].reshape(6 * tokens, head_size)

    def put(kind, j, frame, value):
        if frame == OWN:
            outs[kind][:, head_cols(j)] = value
        else:
            results[kind, j] = value

    def give(kind, j):
        return remote(
            results.at[kind, j],
            outs[kind].at[:, head_cols(j)],
            send_sem.at[RESULT],
            result_sem,
            (pair, sp),
        )

    def forward(j, frame):
        query = near[1, j, 0, frame, 0:tokens, :]
        grad = near[1, j, 1, frame, 0:tokens, :]
        keys, vals = around(0, j, 0, frame), around(0, j, 1, frame)
        scores = dot_nt(query, keys) * scale2 + window(j, frame)
        top = jnp.max(scores, axis=1, keepdims=True)
        powers = jnp.exp2(scores - top)
        total = jnp.sum(powers, axis=1, keepdims=True)
        share = 1.0 / total
        attended = dot_nn(powers.astype(jnp.bfloat16), vals) * share
        put(0, j, frame, attended.astype(jnp.bfloat16))
        grad_weights = dot_nt(grad, vals)
        out_dot = jnp.sum(powers * grad_weights, axis=1, keepdims=True) * share
        grad_scores = (powers * (grad_weights - out_dot)).astype(jnp.bfloat16)
        put(1, j, frame, (dot_nn(grad_scores, keys) * (share * scale)).astype(jnp.bfloat16))
        return top + jnp.log2(total), out_dot

    row_lane = lax.broadcasted_iota(jnp.int32, (1, tokens), 1)

    def stat_row(j, r, frame):
        order = (STAT_OUTER, STAT_OWN, STAT_PAIR, STAT_FAR)
        parts = []
        for stat in order[frame - 1 : frame + 2]:
            parts.append(stats[j, stat, r : r + 1, :])
            down, up = stats[j, BELOW + stat, r : r + 1, :], stats[j, ABOVE + stat, r : r + 1, :]
            parts.append(jnp.where(row_lane < half, down, up))
        return jnp.concatenate(parts, axis=1)

    def backward(j, frame):
        key = near[0, j, 0, frame, 0:tokens, :]
        val = near[0, j, 1, frame, 0:tokens, :]
        queries, grads = around(1, j, 0, frame), around(1, j, 1, frame)
        scores = dot_nt(key, queries) * scale2 + window(j, frame)
        soft = jnp.exp2(scores - stat_row(j, 0, frame))
        put(3, j, frame, dot_nn(soft.astype(jnp.bfloat16), grads).astype(jnp.bfloat16))
        grad_scores = soft * (dot_nt(val, grads) - stat_row(j, 1, frame))
        key_sum = dot_nn(grad_scores.astype(jnp.bfloat16), queries)
        put(2, j, frame, (key_sum * scale).astype(jnp.bfloat16))

    def stat_copies(j):
        block = stats.at[j]
        found = [
            (has_far, STAT_PAIR, STAT_OUTER, 1, (inner_to, sp)),
            (has_outer, STAT_OWN, STAT_FAR, 1, (outer_to, sp)),
        ]
        for at, there, goes in ((BELOW, sp - 1, has_up), (ABOVE, sp + 1, has_down)):
            found += [
                (goes, STAT_OWN, at + STAT_OWN, 2, (tm, there)),
                (goes & has_far, STAT_PAIR, at + STAT_OUTER, 1, (inner_to, there)),
                (goes & has_outer, STAT_OWN, at + STAT_FAR, 1, (outer_to, there)),
            ]
        return [
            (
                goes,
                count,
                remote(
                    block.at[src : src + count],
                    block.at[dst : dst + count],
                    send_sem.at[STAT + n],
                    stat_sem.at[j],
                    device,
                ),
            )
            for n, (goes, src, dst, count, device) in enumerate(found)
        ]

    def step_pair_in(i):
        to_pair(i).wait_recv()
        when(has_far, lambda: pair_to_outer(i).start())
        halos(i, PAIR)

    def step_far_in(i):
        phase, j, _ = pieces[i]

        @pl.when(has_far)
        def _():
            rows = near.at[phase, j, :, FAR, 0:tokens, :]
            remote(rows, rows, send_sem.at[TO_FAR], far_sem.at[phase, j], (pair, sp)).wait_recv()
            for at in (i, i + 1):
                halos(at, FAR)

    def step_outer_in(i):
        @pl.when(has_outer)
        def _():
            pair_to_outer(i).wait_recv()
            halos(i, OUTER)

    def arrived(ref, sem):
        pltpu.make_async_copy(ref, ref, sem).wait()

    def arrive_halos(phase, j, outer):
        rows = slice(tokens, 2 * tokens)
        if outer:
            arrived(near.at[phase, j, :, OUTER, rows, :], halo_sem.at[phase, j, 1])
        else:
            arrived(near.at[phase, j, :, OWN : FAR + 1, rows, :], halo_sem.at[phase, j, 0])

    columns = {}

    def step_forward_pair(j):
        arrive_halos(0, j, False)
        columns[j] = forward(j, PAIR)
        for kind in (0, 1):
            give(kind, j).start()

    def step_forward_own(j):
        arrive_halos(0, j, True)
        found = (*forward(j, OWN), *columns.pop(j))
        lane = lax.broadcasted_iota(jnp.int32, (tokens, tokens), 1)
        spread = jnp.zeros((tokens, tokens), jnp.float32)
        for at, column in zip((0, 1, 8, 9), found, strict=True):
            spread = jnp.where(lane == at, column, spread)
        stats[j, STAT_OWN : STAT_PAIR + 1] = spread.T[0:16, :].reshape(2, 8, tokens)
        for goes, _, copy in stat_copies(j):
            when(goes, copy.start)

    def step_backward_pair(j):
        arrive_halos(1, j, False)
        arrived(stats.at[j, STAT_OUTER:], stat_sem.at[j])
        backward(j, PAIR)
        for kind in (2, 3):
            give(kind, j).start()

    def step_backward_own(j):
        arrive_halos(1, j, True)
        backward(j, OWN)

    times = []
    for i in range(len(pieces)):
        times.append((6.7 + 0.7 * i, step_pair_in, i))
        if pieces[i][2] == 0:
            times.append((7.41 + 0.7 * i, step_far_in, i))
        times.append((9.4 + 0.7 * i, step_outer_in, i))
    for j in heads:
        times.append((11.65 + 1.6 * j, step_forward_pair, j))
        times.append((12.45 + 1.6 * j, step_forward_own, j))
        times.append((16.4 + 1.15 * j, step_backward_pair, j))
        times.append((16.95 + 1.15 * j, step_backward_own, j))
    for _, step, index in sorted(times, key=lambda entry: entry[0]):
        step(index)

    remote(results, results, send_sem.at[RESULT], result_sem, (pair, sp)).wait()

    def drain(cond, ref, i):
        when(cond, remote(ref, ref, send_sem.at[i], result_sem, (pair, sp)).wait_send)

    whole = near.at[:, :, :, PAIR, 0:tokens, :]
    drain(None, whole, TO_PAIR)
    drain(has_outer, whole, TO_FAR)
    drain(has_far, whole, TO_OUTER)
    for first, cond in ((UP, has_up), (DOWN, has_down)):
        drain(cond, near.at[:, :, :, OWN : PAIR + 1, 0:half, :], first)
        drain(cond & has_outer, near.at[:, :, :, OUTER, 0:half, :], first + 1)
        drain(cond & has_far, near.at[:, :, :, FAR, 0:half, :], first + 2)
    for n, (goes, count, _) in enumerate(stat_copies(0)):
        drain(goes, stats.at[:, 0:count], STAT + n)


def put_out(*refs):
    sources, targets, sems = refs[:4], refs[4:8], refs[8]
    copies = [pltpu.make_async_copy(sources[i], targets[i], sems.at[i]) for i in range(4)]
    for copy in copies:
        copy.start()
    for copy in copies:
        copy.wait()


def on_device(queries, key_vectors, values, grad_out, windows):
    local_shape = queries.shape
    row_count, col_count, features = local_shape[1:]
    head_count = windows.shape[1]
    head_size = features // head_count
    tokens = row_count * col_count
    mine = head_count // 2
    half = tokens // 2
    sizes = (
        head_count,
        head_size,
        row_count,
        col_count,
        lax.axis_size("tm"),
        lax.axis_size("space"),
    )
    flat = (tokens, features)
    low = jnp.bfloat16
    outs = pl.pallas_call(
        functools.partial(kernel, sizes),
        out_shape=[jax.ShapeDtypeStruct(flat, low)] * 4,
        in_specs=[pl.BlockSpec(memory_space=pltpu.HBM)] * 5,
        out_specs=[pl.BlockSpec(memory_space=pltpu.VMEM)] * 4,
        scratch_shapes=[
            pltpu.SMEM((2, head_count), jnp.int32),
            pltpu.VMEM((mine, tokens, 2 * tokens), jnp.float32),
            pltpu.VMEM((2, mine, 2, 4, 2 * tokens, head_size), low),
            pltpu.VMEM((4, mine, tokens, head_size), low),
            pltpu.VMEM((mine, 12, 8, tokens), jnp.float32),
            pltpu.VMEM((2, 4, half, head_size), low),
            pltpu.VMEM((4, 8, tokens), jnp.float32),
            pltpu.SemaphoreType.DMA((3,)),
            pltpu.SemaphoreType.DMA((STAT + 8,)),
            pltpu.SemaphoreType.DMA((4 * mine,)),
            pltpu.SemaphoreType.DMA((4 * mine,)),
            pltpu.SemaphoreType.DMA((2, mine)),
            pltpu.SemaphoreType.DMA((2, mine, 2)),
            pltpu.SemaphoreType.DMA((mine,)),
            pltpu.SemaphoreType.DMA,
        ],
        compiler_params=pltpu.CompilerParams(
            collective_id=0, has_side_effects=True, vmem_limit_bytes=55_600_000
        ),
    )(
        pltpu.with_memory_space_constraint(windows, pltpu.HBM),
        queries.reshape(flat),
        key_vectors.reshape(flat),
        values.reshape(flat),
        grad_out.reshape(flat),
    )
    outs = pl.pallas_call(
        put_out,
        out_shape=[jax.ShapeDtypeStruct(flat, low)] * 4,
        in_specs=[pl.BlockSpec(memory_space=pltpu.VMEM)] * 4,
        out_specs=[pl.BlockSpec(memory_space=pltpu.HBM)] * 4,
        scratch_shapes=[
            pltpu.SemaphoreType.DMA((4,)),
        ],
        compiler_params=pltpu.CompilerParams(vmem_limit_bytes=4_000_000),
    )(*outs)
    return tuple(out.reshape(local_shape) for out in outs)


def solution(mesh):
    spec = P("tm", "space", None, None)
    return jax.shard_map(
        on_device,
        mesh=mesh,
        in_specs=(spec, spec, spec, spec, P()),
        out_specs=(spec, spec, spec, spec),
        check_vma=False,
    )
```

```python
import functools
import math

import jax
import jax.numpy as jnp
from jax import lax
from jax.experimental import pallas as pl
from jax.experimental.pallas import tpu as pltpu
from jax.sharding import PartitionSpec as P

masked_score = -1e30
MESH = pl.DeviceIdType.MESH

OUTER, OWN, PAIR, FAR = range(4)

STAT_OWN, STAT_PAIR, STAT_OUTER, STAT_FAR = range(4)
ABOVE, BELOW = 4, 8

TO_PAIR, TO_FAR, TO_OUTER, RESULT, UP, DOWN, STAT = 0, 1, 2, 3, 4, 7, 10


def dot_nt(a, b):
    return lax.dot_general(a, b, (((1,), (1,)), ((), ())), preferred_element_type=jnp.float32)


def dot_nn(a, b):
    return lax.dot_general(a, b, (((1,), (0,)), ((), ())), preferred_element_type=jnp.float32)


def when(cond, action):
    if cond is None:
        action()
    else:
        pl.when(cond)(action)


def kernel(
    sizes,
    win_hbm,
    q_ref,
    k_ref,
    v_ref,
    g_ref,
    att_ref,
    gq_ref,
    gk_ref,
    gv_ref,
    win_ref,
    bias,
    near,
    results,
    stats,
    scores_ref,
    grad_weights_ref,
    powers_ref,
    grad_scores_ref,
    no_rows,
    no_stats,
    load_sem,
    send_sem,
    pair_sem,
    outer_sem,
    far_sem,
    halo_sem,
    stat_sem,
    result_sem,
):
    head_count, head_size, row_count, col_count, n_tm, n_space = sizes
    tokens = row_count * col_count
    half = tokens // 2
    mine = head_count // 2
    scale = 1.0 / math.sqrt(head_size)
    scale2 = scale * math.log2(math.e)
    tm, sp = lax.axis_index("tm"), lax.axis_index("space")
    side = lax.rem(tm, 2)
    pair = tm + 1 - 2 * side
    inner_to = tm + 2 - 4 * side
    outer_to = tm - 2 + 4 * side
    has_far = (inner_to >= 0) & (inner_to < n_tm)
    has_outer = (outer_to >= 0) & (outer_to < n_tm)
    has_up = sp > 0
    has_down = sp < n_space - 1
    heads = range(mine)
    pieces = [(phase, j, a) for phase in range(2) for j in heads for a in range(2)]
    ins = ((k_ref, v_ref), (q_ref, g_ref))
    outs = (att_ref, gq_ref, gk_ref, gv_ref)

    def head_cols(j, of_pair=False):
        first = (1 - side if of_pair else side) * mine + j
        return pl.ds(pl.multiple_of(first * head_size, head_size), head_size)

    barrier = pltpu.get_barrier_semaphore()

    def greet(cond, tm_to, sp_to):
        def signal():
            pl.semaphore_signal(barrier, inc=1, device_id=(tm_to, sp_to), device_id_type=MESH)

        when(cond, signal)

    greet(None, pair, sp)
    greet(has_far, inner_to, sp)
    greet(has_outer, outer_to, sp)
    greet(has_up, tm, sp - 1)
    greet(has_down, tm, sp + 1)

    def main_rows(i, slot):
        phase, j, a = pieces[i]
        return near.at[phase, j, a, slot, 0:tokens, :]

    def load(i):
        phase, j, a = pieces[i]
        return pltpu.make_async_copy(
            ins[phase][a].at[:, head_cols(j)], main_rows(i, OWN), load_sem.at[phase]
        )

    for i in range(len(pieces)):
        load(i).start()
    get_windows = pltpu.make_async_copy(win_hbm, win_ref, load_sem.at[2])
    get_windows.start()
    no_rows[...] = jnp.zeros_like(no_rows)
    no_stats[...] = jnp.zeros_like(no_stats)

    def remote(src, dst, send, recv, device):
        return pltpu.make_async_remote_copy(
            src_ref=src,
            dst_ref=dst,
            send_sem=send,
            recv_sem=recv,
            device_id=device,
            device_id_type=MESH,
        )

    def to_pair(i):
        phase, j, a = pieces[i]
        return remote(
            ins[phase][a].at[:, head_cols(j, True)],
            main_rows(i, PAIR),
            send_sem.at[TO_PAIR],
            pair_sem.at[i],
            (pair, sp),
        )

    def own_to_far(i):
        phase, j, a = pieces[i]
        return remote(
            main_rows(i, OWN),
            main_rows(i, FAR),
            send_sem.at[TO_FAR],
            far_sem.at[phase, j],
            (outer_to, sp),
        )

    def pair_to_outer(i):
        return remote(
            main_rows(i, PAIR),
            main_rows(i, OUTER),
            send_sem.at[TO_OUTER],
            outer_sem.at[i],
            (inner_to, sp),
        )

    def of_kind(slot):
        return {OUTER: 1, FAR: 2}.get(slot, 0)

    def halo_up(i, slot):
        phase, j, a = pieces[i]
        rows = near.at[phase, j, a, slot]
        return remote(
            rows.at[0:half, :],
            rows.at[tokens : tokens + half, :],
            send_sem.at[UP + of_kind(slot)],
            halo_sem.at[phase, j, of_kind(slot) % 2],
            (tm, sp - 1),
        )

    def halo_down(i, slot):
        phase, j, a = pieces[i]
        rows = near.at[phase, j, a, slot]
        return remote(
            rows.at[half:tokens, :],
            rows.at[tokens + half : 2 * tokens, :],
            send_sem.at[DOWN + of_kind(slot)],
            halo_sem.at[phase, j, of_kind(slot) % 2],
            (tm, sp + 1),
        )

    def halos(i, slot):
        when(has_up, lambda: halo_up(i, slot).start())
        when(has_down, lambda: halo_down(i, slot).start())

    expected = (
        1
        + has_far.astype(jnp.int32)
        + has_outer.astype(jnp.int32)
        + has_up.astype(jnp.int32)
        + has_down.astype(jnp.int32)
    )
    pl.semaphore_wait(barrier, expected)
    for i in range(len(pieces)):
        to_pair(i).start()
    def step_own_out(phase):
        rows = near.at[phase, :, :, OWN, 0:tokens, :]
        pltpu.make_async_copy(rows, rows, load_sem.at[phase]).wait()
        for i in range(len(pieces)):
            if pieces[i][0] == phase:
                when(has_outer, lambda: own_to_far(i).start())
                halos(i, OWN)

    def fill(source, target, sem):
        pltpu.make_async_copy(source, target, sem).start()

    def fill_side(first_row, first_stat):
        rows = slice(first_row, first_row + half)

        def all_frames():
            for phase in range(2):
                for j in heads:
                    at = near.at[phase, j, :, :, rows, :]
                    fill(no_rows.at[:, 0:1], at.at[:, 0:1], halo_sem.at[phase, j, 1])
                    fill(no_rows.at[:, 1:4], at.at[:, 1:4], halo_sem.at[phase, j, 0])
            for j in heads:
                fill(no_stats, stats.at[j, first_stat : first_stat + 4], stat_sem.at[j])

        def one_frame(slot, stat):
            for phase in range(2):
                for j in heads:
                    sem = halo_sem.at[phase, j, of_kind(slot) % 2]
                    fill(no_rows.at[:, slot], near.at[phase, j, :, slot, rows, :], sem)
            for j in heads:
                fill(no_stats.at[0], stats.at[j, first_stat + stat], stat_sem.at[j])

        return all_frames, one_frame

    for has_side, parts in (
        (has_down, fill_side(tokens, BELOW)),
        (has_up, fill_side(tokens + half, ABOVE)),
    ):
        all_frames, one_frame = parts
        pl.when(jnp.logical_not(has_side))(all_frames)
        no_outer, no_far = jnp.logical_not(has_outer), jnp.logical_not(has_far)
        pl.when(has_side & no_outer)(lambda: one_frame(OUTER, STAT_OUTER))
        pl.when(has_side & no_far)(lambda: one_frame(FAR, STAT_FAR))

    for has_frame, slot, stat in ((has_outer, OUTER, STAT_OUTER), (has_far, FAR, STAT_FAR)):

        @pl.when(jnp.logical_not(has_frame))
        def _():
            for phase in range(2):
                for j in heads:
                    near[phase, j, :, slot, 0:tokens, :] = jnp.zeros(
                        (2, tokens, head_size), near.dtype
                    )
            for j in heads:
                fill(no_stats.at[0], stats.at[j, stat], stat_sem.at[j])

    own_id = lax.broadcasted_iota(jnp.int32, (tokens, 2 * tokens), 0)
    near_id = lax.broadcasted_iota(jnp.int32, (tokens, 2 * tokens), 1)
    own_row, own_col = own_id // col_count, own_id % col_count
    near_row, near_col = near_id // col_count, near_id % col_count
    upper = near_row >= row_count + row_count // 2
    near_row = jnp.where(upper, near_row - 2 * row_count, near_row)
    global_row = sp * row_count + near_row
    row_inside = (global_row >= 0) & (global_row < n_space * row_count)
    row_gap = jnp.where(row_inside, jnp.abs(own_row - near_row), 1 << 20)
    col_gap = jnp.abs(own_col - near_col)

    get_windows.wait()
    for j in heads:
        h = side * mine + j
        inside = (row_gap <= win_ref[0, h]) & (col_gap <= win_ref[1, h])
        bias[j] = jnp.where(inside, 0.0, masked_score)

    def window(j, frame):
        here = bias[j]
        there = here + jnp.where(has_outer if frame == OWN else has_far, 0.0, masked_score)
        order = [there, here, here] if frame == OWN else [here, here, there]
        return jnp.concatenate(order, axis=1)

    def around(phase, j, a, frame):
        return near[phase, j, a, frame - 1 : frame + 2].reshape(6 * tokens, head_size)

    def put(kind, j, frame, value):
        if frame == OWN:
            outs[kind][:, head_cols(j)] = value
        else:
            results[kind, j] = value

    def give(kind, j):
        return remote(
            results.at[kind, j],
            outs[kind].at[:, head_cols(j)],
            send_sem.at[RESULT],
            result_sem,
            (pair, sp),
        )

    def forward(j, frame):
        query = near[1, j, 0, frame, 0:tokens, :]
        grad = near[1, j, 1, frame, 0:tokens, :]
        keys, vals = around(0, j, 0, frame), around(0, j, 1, frame)
        scores = dot_nt(query, keys) * scale2 + window(j, frame)
        top = jnp.max(scores, axis=1, keepdims=True)
        powers = jnp.exp2(scores - top)
        total = jnp.sum(powers, axis=1, keepdims=True)
        share = 1.0 / total
        attended = dot_nn(powers.astype(jnp.bfloat16), vals) * share
        put(0, j, frame, attended.astype(jnp.bfloat16))
        grad_weights = dot_nt(grad, vals)
        out_dot = jnp.sum(powers * grad_weights, axis=1, keepdims=True) * share
        grad_scores = (powers * (grad_weights - out_dot)).astype(jnp.bfloat16)
        put(1, j, frame, (dot_nn(grad_scores, keys) * (share * scale)).astype(jnp.bfloat16))
        return top + jnp.log2(total), out_dot

    def forward_both(j):
        frames = slice(OWN, PAIR + 1)
        own_rows, pair_rows = slice(0, tokens), slice(tokens, 2 * tokens)
        side, middle = slice(0, 2 * tokens), slice(2 * tokens, 6 * tokens)
        parts = ((own_rows, OUTER), (pair_rows, FAR))

        def shared(a):
            return near[0, j, a, frames].reshape(4 * tokens, head_size)

        for a, out in ((0, scores_ref), (1, grad_weights_ref)):
            rows = near[1, j, a, frames, 0:tokens, :].reshape(2 * tokens, head_size)
            out[:, middle] = dot_nt(rows, shared(a))
            for at, slot in parts:
                out[at, side] = dot_nt(rows[at], near[0, j, a, slot])
        shares, found = [], []
        here = bias[j]
        for at, held in ((own_rows, has_outer), (pair_rows, has_far)):
            there = here + jnp.where(held, 0.0, masked_score)
            window_bias = jnp.concatenate([there, here, here], axis=1)
            scores = scores_ref[at] * scale2 + window_bias
            top = jnp.max(scores, axis=1, keepdims=True)
            powers = jnp.exp2(scores - top)
            total = jnp.sum(powers, axis=1, keepdims=True)
            share = 1.0 / total
            powers_ref[at] = powers.astype(jnp.bfloat16)
            grad_weights = grad_weights_ref[at]
            out_dot = jnp.sum(powers * grad_weights, axis=1, keepdims=True) * share
            grad_scores_ref[at] = (powers * (grad_weights - out_dot)).astype(jnp.bfloat16)
            shares.append(share)
            found += [top + jnp.log2(total), out_dot]
        share = jnp.concatenate(shares, axis=0)
        for kind, a, low, factor in (
            (0, 1, powers_ref, share),
            (1, 0, grad_scores_ref, share * scale),
        ):
            beside = [dot_nn(low[at, side], near[0, j, a, slot]) for at, slot in parts]
            mixed = dot_nn(low[:, middle], shared(a)) + jnp.concatenate(beside, axis=0)
            mixed = (mixed * factor).astype(jnp.bfloat16)
            put(kind, j, PAIR, mixed[tokens:])
            put(kind, j, OWN, mixed[:tokens])
        return found

    row_lane = lax.broadcasted_iota(jnp.int32, (1, tokens), 1)

    def stat_row(j, r, frame):
        order = (STAT_OUTER, STAT_OWN, STAT_PAIR, STAT_FAR)
        parts = []
        for stat in order[frame - 1 : frame + 2]:
            parts.append(stats[j, stat, r : r + 1, :])
            down, up = stats[j, BELOW + stat, r : r + 1, :], stats[j, ABOVE + stat, r : r + 1, :]
            parts.append(jnp.where(row_lane < half, down, up))
        return jnp.concatenate(parts, axis=1)

    def backward(j, frame):
        key = near[0, j, 0, frame, 0:tokens, :]
        val = near[0, j, 1, frame, 0:tokens, :]
        queries, grads = around(1, j, 0, frame), around(1, j, 1, frame)
        scores = dot_nt(key, queries) * scale2 + window(j, frame)
        soft = jnp.exp2(scores - stat_row(j, 0, frame))
        put(3, j, frame, dot_nn(soft.astype(jnp.bfloat16), grads).astype(jnp.bfloat16))
        grad_scores = soft * (dot_nt(val, grads) - stat_row(j, 1, frame))
        key_sum = dot_nn(grad_scores.astype(jnp.bfloat16), queries)
        put(2, j, frame, (key_sum * scale).astype(jnp.bfloat16))

    def stat_copies(j):
        block = stats.at[j]
        found = [
            (has_far, STAT_PAIR, STAT_OUTER, 1, (inner_to, sp)),
            (has_outer, STAT_OWN, STAT_FAR, 1, (outer_to, sp)),
        ]
        for at, there, goes in ((BELOW, sp - 1, has_up), (ABOVE, sp + 1, has_down)):
            found += [
                (goes, STAT_OWN, at + STAT_OWN, 2, (tm, there)),
                (goes & has_far, STAT_PAIR, at + STAT_OUTER, 1, (inner_to, there)),
                (goes & has_outer, STAT_OWN, at + STAT_FAR, 1, (outer_to, there)),
            ]
        return [
            (
                goes,
                count,
                remote(
                    block.at[src : src + count],
                    block.at[dst : dst + count],
                    send_sem.at[STAT + n],
                    stat_sem.at[j],
                    device,
                ),
            )
            for n, (goes, src, dst, count, device) in enumerate(found)
        ]

    def step_pair_in(i):
        to_pair(i).wait_recv()
        when(has_far, lambda: pair_to_outer(i).start())
        halos(i, PAIR)

    def step_far_in(i):
        phase, j, _ = pieces[i]

        @pl.when(has_far)
        def _():
            rows = near.at[phase, j, :, FAR, 0:tokens, :]
            remote(rows, rows, send_sem.at[TO_FAR], far_sem.at[phase, j], (pair, sp)).wait_recv()
            for at in (i, i + 1):
                halos(at, FAR)

    def step_outer_in(i):
        @pl.when(has_outer)
        def _():
            pair_to_outer(i).wait_recv()
            halos(i, OUTER)

    def arrived(ref, sem):
        pltpu.make_async_copy(ref, ref, sem).wait()

    def arrive_halos(phase, j, outer):
        rows = slice(tokens, 2 * tokens)
        if outer:
            arrived(near.at[phase, j, :, OUTER, rows, :], halo_sem.at[phase, j, 1])
        else:
            arrived(near.at[phase, j, :, OWN : FAR + 1, rows, :], halo_sem.at[phase, j, 0])

    columns = {}

    def step_forward_pair(j):
        arrive_halos(0, j, False)
        columns[j] = forward(j, PAIR)
        for kind in (0, 1):
            give(kind, j).start()

    def send_stats(j, found):
        lane = lax.broadcasted_iota(jnp.int32, (tokens, tokens), 1)
        spread = jnp.zeros((tokens, tokens), jnp.float32)
        for at, column in zip((0, 1, 8, 9), found, strict=True):
            spread = jnp.where(lane == at, column, spread)
        stats[j, STAT_OWN : STAT_PAIR + 1] = spread.T[0:16, :].reshape(2, 8, tokens)
        for goes, _, copy in stat_copies(j):
            when(goes, copy.start)

    def step_forward_own(j):
        arrive_halos(0, j, True)
        send_stats(j, (*forward(j, OWN), *columns.pop(j)))

    def step_forward_both(j):
        arrive_halos(0, j, False)
        arrive_halos(0, j, True)
        found = forward_both(j)
        for kind in (0, 1):
            give(kind, j).start()
        send_stats(j, found)

    def step_backward_pair(j):
        arrive_halos(1, j, False)
        arrived(stats.at[j, STAT_OUTER:], stat_sem.at[j])
        backward(j, PAIR)
        for kind in (2, 3):
            give(kind, j).start()

    def step_backward_own(j):
        arrive_halos(1, j, True)
        backward(j, OWN)

    times = [(0.0, step_own_out, 0), (8.0, step_own_out, 1)]
    for i in range(len(pieces)):
        times.append((6.15 + 0.7 * i, step_pair_in, i))
        if pieces[i][2] == 0:
            times.append((6.9 + 0.7 * i, step_far_in, i))
        late = 4.0 if i >= len(pieces) - 2 else 0.0
        times.append((8.75 + 0.7 * i + late, step_outer_in, i))
    for j in heads:
        if j == 0:
            times.append((11.06, step_forward_pair, j))
            times.append((12.5, step_forward_own, j))
        else:
            times.append((11.5 + 1.4 * j, step_forward_both, j))
        times.append((15.5 + 1.05 * j, step_backward_pair, j))
        times.append((16.5 + (4.5 + 0.5 * j if j > 0 else 0.0), step_backward_own, j))
    for _, step, index in sorted(times, key=lambda entry: entry[0]):
        step(index)

    remote(results, results, send_sem.at[RESULT], result_sem, (pair, sp)).wait()

    def drain(cond, ref, i):
        when(cond, remote(ref, ref, send_sem.at[i], result_sem, (pair, sp)).wait_send)

    whole = near.at[:, :, :, PAIR, 0:tokens, :]
    drain(None, whole, TO_PAIR)
    drain(has_outer, whole, TO_FAR)
    drain(has_far, whole, TO_OUTER)
    for first, cond in ((UP, has_up), (DOWN, has_down)):
        drain(cond, near.at[:, :, :, OWN : PAIR + 1, 0:half, :], first)
        drain(cond & has_outer, near.at[:, :, :, OUTER, 0:half, :], first + 1)
        drain(cond & has_far, near.at[:, :, :, FAR, 0:half, :], first + 2)
    for n, (goes, count, _) in enumerate(stat_copies(0)):
        drain(goes, stats.at[:, 0:count], STAT + n)


def put_out(*refs):
    sources, targets, sems = refs[:4], refs[4:8], refs[8]
    copies = [pltpu.make_async_copy(sources[i], targets[i], sems.at[i]) for i in range(4)]
    for copy in copies:
        copy.start()
    for copy in copies:
        copy.wait()


def on_device(queries, key_vectors, values, grad_out, windows):
    local_shape = queries.shape
    row_count, col_count, features = local_shape[1:]
    head_count = windows.shape[1]
    head_size = features // head_count
    tokens = row_count * col_count
    mine = head_count // 2
    half = tokens // 2
    sizes = (
        head_count,
        head_size,
        row_count,
        col_count,
        lax.axis_size("tm"),
        lax.axis_size("space"),
    )
    flat = (tokens, features)
    low = jnp.bfloat16
    outs = pl.pallas_call(
        functools.partial(kernel, sizes),
        out_shape=[jax.ShapeDtypeStruct(flat, low)] * 4,
        in_specs=[pl.BlockSpec(memory_space=pltpu.HBM)] * 5,
        out_specs=[pl.BlockSpec(memory_space=pltpu.VMEM)] * 4,
        scratch_shapes=[
            pltpu.SMEM((2, head_count), jnp.int32),
            pltpu.VMEM((mine, tokens, 2 * tokens), jnp.float32),
            pltpu.VMEM((2, mine, 2, 4, 2 * tokens, head_size), low),
            pltpu.VMEM((4, mine, tokens, head_size), low),
            pltpu.VMEM((mine, 12, 8, tokens), jnp.float32),
            pltpu.VMEM((2 * tokens, 6 * tokens), jnp.float32),
            pltpu.VMEM((2 * tokens, 6 * tokens), jnp.float32),
            pltpu.VMEM((2 * tokens, 6 * tokens), low),
            pltpu.VMEM((2 * tokens, 6 * tokens), low),
            pltpu.VMEM((2, 4, half, head_size), low),
            pltpu.VMEM((4, 8, tokens), jnp.float32),
            pltpu.SemaphoreType.DMA((3,)),
            pltpu.SemaphoreType.DMA((STAT + 8,)),
            pltpu.SemaphoreType.DMA((4 * mine,)),
            pltpu.SemaphoreType.DMA((4 * mine,)),
            pltpu.SemaphoreType.DMA((2, mine)),
            pltpu.SemaphoreType.DMA((2, mine, 2)),
            pltpu.SemaphoreType.DMA((mine,)),
            pltpu.SemaphoreType.DMA,
        ],
        compiler_params=pltpu.CompilerParams(
            collective_id=0, has_side_effects=True, vmem_limit_bytes=55_600_000
        ),
    )(
        pltpu.with_memory_space_constraint(windows, pltpu.HBM),
        queries.reshape(flat),
        key_vectors.reshape(flat),
        values.reshape(flat),
        grad_out.reshape(flat),
    )
    outs = pl.pallas_call(
        put_out,
        out_shape=[jax.ShapeDtypeStruct(flat, low)] * 4,
        in_specs=[pl.BlockSpec(memory_space=pltpu.VMEM)] * 4,
        out_specs=[pl.BlockSpec(memory_space=pltpu.HBM)] * 4,
        scratch_shapes=[
            pltpu.SemaphoreType.DMA((4,)),
        ],
        compiler_params=pltpu.CompilerParams(vmem_limit_bytes=4_000_000),
    )(*outs)
    return tuple(out.reshape(local_shape) for out in outs)


def solution(mesh):
    spec = P("tm", "space", None, None)
    return jax.shard_map(
        on_device,
        mesh=mesh,
        in_specs=(spec, spec, spec, spec, P()),
        out_specs=(spec, spec, spec, spec),
        check_vma=False,
    )
```

```python
import functools
import math

import jax
import jax.numpy as jnp
from jax import lax
from jax.experimental import pallas as pl
from jax.experimental.pallas import tpu as pltpu
from jax.sharding import PartitionSpec as P

masked_score = -1e30
MESH = pl.DeviceIdType.MESH

OUTER, OWN, PAIR, FAR = range(4)

STAT_OWN, STAT_PAIR, STAT_OUTER, STAT_FAR = range(4)
ABOVE, BELOW = 4, 8

TO_PAIR, TO_FAR, TO_OUTER, RESULT, UP, DOWN, STAT = 0, 1, 2, 3, 4, 7, 10


def dot_nt(a, b):
    return lax.dot_general(a, b, (((1,), (1,)), ((), ())), preferred_element_type=jnp.float32)


def dot_nn(a, b):
    return lax.dot_general(a, b, (((1,), (0,)), ((), ())), preferred_element_type=jnp.float32)


def when(cond, action):
    if cond is None:
        action()
    else:
        pl.when(cond)(action)


def kernel(
    sizes,
    win_hbm,
    q_ref,
    k_ref,
    v_ref,
    g_ref,
    att_ref,
    gq_ref,
    gk_ref,
    gv_ref,
    win_ref,
    bias,
    near,
    results,
    stats,
    scores_ref,
    grad_weights_ref,
    powers_ref,
    grad_scores_ref,
    no_rows,
    no_stats,
    load_sem,
    send_sem,
    pair_sem,
    outer_sem,
    far_sem,
    halo_sem,
    stat_sem,
    result_sem,
):
    head_count, head_size, row_count, col_count, n_tm, n_space = sizes
    tokens = row_count * col_count
    half = tokens // 2
    mine = head_count // 2
    scale = 1.0 / math.sqrt(head_size)
    scale2 = scale * math.log2(math.e)
    tm, sp = lax.axis_index("tm"), lax.axis_index("space")
    side = lax.rem(tm, 2)
    pair = tm + 1 - 2 * side
    inner_to = tm + 2 - 4 * side
    outer_to = tm - 2 + 4 * side
    has_far = (inner_to >= 0) & (inner_to < n_tm)
    has_outer = (outer_to >= 0) & (outer_to < n_tm)
    has_up = sp > 0
    has_down = sp < n_space - 1
    heads = range(mine)
    pieces = [(phase, j, a) for phase in range(2) for j in heads for a in range(2)]
    ins = ((k_ref, v_ref), (q_ref, g_ref))
    outs = (att_ref, gq_ref, gk_ref, gv_ref)

    def head_cols(j, of_pair=False):
        first = (1 - side if of_pair else side) * mine + j
        return pl.ds(pl.multiple_of(first * head_size, head_size), head_size)

    barrier = pltpu.get_barrier_semaphore()

    def greet(cond, tm_to, sp_to):
        def signal():
            pl.semaphore_signal(barrier, inc=1, device_id=(tm_to, sp_to), device_id_type=MESH)

        when(cond, signal)

    greet(None, pair, sp)
    greet(has_far, inner_to, sp)
    greet(has_outer, outer_to, sp)
    greet(has_up, tm, sp - 1)
    greet(has_down, tm, sp + 1)

    def main_rows(i, slot):
        phase, j, a = pieces[i]
        return near.at[phase, j, a, slot, 0:tokens, :]

    def load(i):
        phase, j, a = pieces[i]
        return pltpu.make_async_copy(
            ins[phase][a].at[:, head_cols(j)], main_rows(i, OWN), load_sem.at[phase]
        )

    for i in range(len(pieces)):
        load(i).start()
    get_windows = pltpu.make_async_copy(win_hbm, win_ref, load_sem.at[2])
    get_windows.start()
    no_rows[...] = jnp.zeros_like(no_rows)
    no_stats[...] = jnp.zeros_like(no_stats)

    def remote(src, dst, send, recv, device):
        return pltpu.make_async_remote_copy(
            src_ref=src,
            dst_ref=dst,
            send_sem=send,
            recv_sem=recv,
            device_id=device,
            device_id_type=MESH,
        )

    def to_pair(i):
        phase, j, a = pieces[i]
        return remote(
            ins[phase][a].at[:, head_cols(j, True)],
            main_rows(i, PAIR),
            send_sem.at[TO_PAIR],
            pair_sem.at[i],
            (pair, sp),
        )

    def own_to_far(i):
        phase, j, a = pieces[i]
        return remote(
            main_rows(i, OWN),
            main_rows(i, FAR),
            send_sem.at[TO_FAR],
            far_sem.at[phase, j],
            (outer_to, sp),
        )

    def pair_to_outer(i):
        return remote(
            main_rows(i, PAIR),
            main_rows(i, OUTER),
            send_sem.at[TO_OUTER],
            outer_sem.at[i],
            (inner_to, sp),
        )

    def of_kind(slot):
        return {OUTER: 1, FAR: 2}.get(slot, 0)

    def halo_up(i, slot):
        phase, j, a = pieces[i]
        rows = near.at[phase, j, a, slot]
        return remote(
            rows.at[0:half, :],
            rows.at[tokens : tokens + half, :],
            send_sem.at[UP + of_kind(slot)],
            halo_sem.at[phase, j, of_kind(slot) % 2],
            (tm, sp - 1),
        )

    def halo_down(i, slot):
        phase, j, a = pieces[i]
        rows = near.at[phase, j, a, slot]
        return remote(
            rows.at[half:tokens, :],
            rows.at[tokens + half : 2 * tokens, :],
            send_sem.at[DOWN + of_kind(slot)],
            halo_sem.at[phase, j, of_kind(slot) % 2],
            (tm, sp + 1),
        )

    def halos(i, slot):
        when(has_up, lambda: halo_up(i, slot).start())
        when(has_down, lambda: halo_down(i, slot).start())

    expected = (
        1
        + has_far.astype(jnp.int32)
        + has_outer.astype(jnp.int32)
        + has_up.astype(jnp.int32)
        + has_down.astype(jnp.int32)
    )
    pl.semaphore_wait(barrier, expected)
    for i in range(len(pieces)):
        to_pair(i).start()
    def step_own_out(phase):
        rows = near.at[phase, :, :, OWN, 0:tokens, :]
        pltpu.make_async_copy(rows, rows, load_sem.at[phase]).wait()
        for i in range(len(pieces)):
            if pieces[i][0] == phase:
                when(has_outer, lambda: own_to_far(i).start())
                halos(i, OWN)

    def fill(source, target, sem):
        pltpu.make_async_copy(source, target, sem).start()

    def fill_side(first_row, first_stat):
        rows = slice(first_row, first_row + half)

        def all_frames():
            for phase in range(2):
                for j in heads:
                    at = near.at[phase, j, :, :, rows, :]
                    fill(no_rows.at[:, 0:1], at.at[:, 0:1], halo_sem.at[phase, j, 1])
                    fill(no_rows.at[:, 1:4], at.at[:, 1:4], halo_sem.at[phase, j, 0])
            for j in heads:
                fill(no_stats, stats.at[j, first_stat : first_stat + 4], stat_sem.at[j])

        def one_frame(slot, stat):
            for phase in range(2):
                for j in heads:
                    sem = halo_sem.at[phase, j, of_kind(slot) % 2]
                    fill(no_rows.at[:, slot], near.at[phase, j, :, slot, rows, :], sem)
            for j in heads:
                fill(no_stats.at[0], stats.at[j, first_stat + stat], stat_sem.at[j])

        return all_frames, one_frame

    for has_side, parts in (
        (has_down, fill_side(tokens, BELOW)),
        (has_up, fill_side(tokens + half, ABOVE)),
    ):
        all_frames, one_frame = parts
        pl.when(jnp.logical_not(has_side))(all_frames)
        no_outer, no_far = jnp.logical_not(has_outer), jnp.logical_not(has_far)
        pl.when(has_side & no_outer)(lambda: one_frame(OUTER, STAT_OUTER))
        pl.when(has_side & no_far)(lambda: one_frame(FAR, STAT_FAR))

    for has_frame, slot, stat in ((has_outer, OUTER, STAT_OUTER), (has_far, FAR, STAT_FAR)):

        @pl.when(jnp.logical_not(has_frame))
        def _():
            for phase in range(2):
                for j in heads:
                    near[phase, j, :, slot, 0:tokens, :] = jnp.zeros(
                        (2, tokens, head_size), near.dtype
                    )
            for j in heads:
                fill(no_stats.at[0], stats.at[j, stat], stat_sem.at[j])

    own_id = lax.broadcasted_iota(jnp.int32, (tokens, 2 * tokens), 0)
    near_id = lax.broadcasted_iota(jnp.int32, (tokens, 2 * tokens), 1)
    own_row, own_col = own_id // col_count, own_id % col_count
    near_row, near_col = near_id // col_count, near_id % col_count
    upper = near_row >= row_count + row_count // 2
    near_row = jnp.where(upper, near_row - 2 * row_count, near_row)
    global_row = sp * row_count + near_row
    row_inside = (global_row >= 0) & (global_row < n_space * row_count)
    row_gap = jnp.where(row_inside, jnp.abs(own_row - near_row), 1 << 20)
    col_gap = jnp.abs(own_col - near_col)

    get_windows.wait()
    for j in heads:
        h = side * mine + j
        inside = (row_gap <= win_ref[0, h]) & (col_gap <= win_ref[1, h])
        bias[j] = jnp.where(inside, 0.0, masked_score)

    def window(j, frame):
        here = bias[j]
        there = here + jnp.where(has_outer if frame == OWN else has_far, 0.0, masked_score)
        order = [there, here, here] if frame == OWN else [here, here, there]
        return jnp.concatenate(order, axis=1)

    def around(phase, j, a, frame):
        return near[phase, j, a, frame - 1 : frame + 2].reshape(6 * tokens, head_size)

    def put(kind, j, frame, value):
        if frame == OWN:
            outs[kind][:, head_cols(j)] = value
        else:
            results[kind, j] = value

    def give(kind, j):
        return remote(
            results.at[kind, j],
            outs[kind].at[:, head_cols(j)],
            send_sem.at[RESULT],
            result_sem,
            (pair, sp),
        )

    def forward(j, frame):
        query = near[1, j, 0, frame, 0:tokens, :]
        grad = near[1, j, 1, frame, 0:tokens, :]
        keys, vals = around(0, j, 0, frame), around(0, j, 1, frame)
        scores = dot_nt(query, keys) * scale2 + window(j, frame)
        top = jnp.max(scores, axis=1, keepdims=True)
        powers = jnp.exp2(scores - top)
        total = jnp.sum(powers, axis=1, keepdims=True)
        share = 1.0 / total
        attended = dot_nn(powers.astype(jnp.bfloat16), vals) * share
        put(0, j, frame, attended.astype(jnp.bfloat16))
        grad_weights = dot_nt(grad, vals)
        out_dot = jnp.sum(powers * grad_weights, axis=1, keepdims=True) * share
        grad_scores = (powers * (grad_weights - out_dot)).astype(jnp.bfloat16)
        put(1, j, frame, (dot_nn(grad_scores, keys) * (share * scale)).astype(jnp.bfloat16))
        return top + jnp.log2(total), out_dot

    def forward_both(j):
        frames = slice(OWN, PAIR + 1)
        own_rows, pair_rows = slice(0, tokens), slice(tokens, 2 * tokens)
        side, middle = slice(0, 2 * tokens), slice(2 * tokens, 6 * tokens)
        parts = ((own_rows, OUTER), (pair_rows, FAR))

        def shared(a):
            return near[0, j, a, frames].reshape(4 * tokens, head_size)

        for a, out in ((0, scores_ref), (1, grad_weights_ref)):
            rows = near[1, j, a, frames, 0:tokens, :].reshape(2 * tokens, head_size)
            out[:, middle] = dot_nt(rows, shared(a))
            for at, slot in parts:
                out[at, side] = dot_nt(rows[at], near[0, j, a, slot])
        shares, found = [], []
        here = bias[j]
        for at, held in ((own_rows, has_outer), (pair_rows, has_far)):
            there = here + jnp.where(held, 0.0, masked_score)
            window_bias = jnp.concatenate([there, here, here], axis=1)
            scores = scores_ref[at] * scale2 + window_bias
            top = jnp.max(scores, axis=1, keepdims=True)
            powers = jnp.exp2(scores - top)
            total = jnp.sum(powers, axis=1, keepdims=True)
            share = 1.0 / total
            powers_ref[at] = powers.astype(jnp.bfloat16)
            grad_weights = grad_weights_ref[at]
            out_dot = jnp.sum(powers * grad_weights, axis=1, keepdims=True) * share
            grad_scores_ref[at] = (powers * (grad_weights - out_dot)).astype(jnp.bfloat16)
            shares.append(share)
            found += [top + jnp.log2(total), out_dot]
        send_stats(j, found)
        share = jnp.concatenate(shares, axis=0)
        for kind, a, low, factor in (
            (0, 1, powers_ref, share),
            (1, 0, grad_scores_ref, share * scale),
        ):
            beside = [dot_nn(low[at, side], near[0, j, a, slot]) for at, slot in parts]
            mixed = dot_nn(low[:, middle], shared(a)) + jnp.concatenate(beside, axis=0)
            mixed = (mixed * factor).astype(jnp.bfloat16)
            put(kind, j, PAIR, mixed[tokens:])
            put(kind, j, OWN, mixed[:tokens])

    row_lane = lax.broadcasted_iota(jnp.int32, (1, tokens), 1)

    def stat_row(j, r, frame):
        order = (STAT_OUTER, STAT_OWN, STAT_PAIR, STAT_FAR)
        parts = []
        for stat in order[frame - 1 : frame + 2]:
            parts.append(stats[j, stat, r : r + 1, :])
            down, up = stats[j, BELOW + stat, r : r + 1, :], stats[j, ABOVE + stat, r : r + 1, :]
            parts.append(jnp.where(row_lane < half, down, up))
        return jnp.concatenate(parts, axis=1)

    def backward_rows(frame):
        return slice((frame - OWN) * tokens, (frame - OWN + 1) * tokens)

    def backward_start(j, frame):
        at = backward_rows(frame)
        key = near[0, j, 0, frame, 0:tokens, :]
        val = near[0, j, 1, frame, 0:tokens, :]
        scores_ref[at] = dot_nt(key, around(1, j, 0, frame)) * scale2 + window(j, frame)
        grad_weights_ref[at] = dot_nt(val, around(1, j, 1, frame))

    def backward(j, frame):
        at = backward_rows(frame)
        soft = jnp.exp2(scores_ref[at] - stat_row(j, 0, frame))
        grad_scores = soft * (grad_weights_ref[at] - stat_row(j, 1, frame))
        value_sum = dot_nn(soft.astype(jnp.bfloat16), around(1, j, 1, frame))
        put(3, j, frame, value_sum.astype(jnp.bfloat16))
        key_sum = dot_nn(grad_scores.astype(jnp.bfloat16), around(1, j, 0, frame))
        put(2, j, frame, (key_sum * scale).astype(jnp.bfloat16))

    def stat_copies(j):
        block = stats.at[j]
        found = [
            (has_far, STAT_PAIR, STAT_OUTER, 1, (inner_to, sp)),
            (has_outer, STAT_OWN, STAT_FAR, 1, (outer_to, sp)),
        ]
        for at, there, goes in ((BELOW, sp - 1, has_up), (ABOVE, sp + 1, has_down)):
            found += [
                (goes, STAT_OWN, at + STAT_OWN, 2, (tm, there)),
                (goes & has_far, STAT_PAIR, at + STAT_OUTER, 1, (inner_to, there)),
                (goes & has_outer, STAT_OWN, at + STAT_FAR, 1, (outer_to, there)),
            ]
        return [
            (
                goes,
                count,
                remote(
                    block.at[src : src + count],
                    block.at[dst : dst + count],
                    send_sem.at[STAT + n],
                    stat_sem.at[j],
                    device,
                ),
            )
            for n, (goes, src, dst, count, device) in enumerate(found)
        ]

    def step_pair_in(i):
        to_pair(i).wait_recv()
        when(has_far, lambda: pair_to_outer(i).start())
        halos(i, PAIR)

    def step_far_in(i):
        phase, j, _ = pieces[i]

        @pl.when(has_far)
        def _():
            rows = near.at[phase, j, :, FAR, 0:tokens, :]
            remote(rows, rows, send_sem.at[TO_FAR], far_sem.at[phase, j], (pair, sp)).wait_recv()
            for at in (i, i + 1):
                halos(at, FAR)

    def step_outer_in(i):
        @pl.when(has_outer)
        def _():
            pair_to_outer(i).wait_recv()
            halos(i, OUTER)

    def arrived(ref, sem):
        pltpu.make_async_copy(ref, ref, sem).wait()

    def arrive_halos(phase, j, outer):
        rows = slice(tokens, 2 * tokens)
        if outer:
            arrived(near.at[phase, j, :, OUTER, rows, :], halo_sem.at[phase, j, 1])
        else:
            arrived(near.at[phase, j, :, OWN : FAR + 1, rows, :], halo_sem.at[phase, j, 0])

    columns = {}

    def step_forward_pair(j):
        arrive_halos(0, j, False)
        columns[j] = forward(j, PAIR)
        for kind in (0, 1):
            give(kind, j).start()

    def send_stats(j, found):
        lane = lax.broadcasted_iota(jnp.int32, (tokens, tokens), 1)
        spread = jnp.zeros((tokens, tokens), jnp.float32)
        for at, column in zip((0, 1, 8, 9), found, strict=True):
            spread = jnp.where(lane == at, column, spread)
        stats[j, STAT_OWN : STAT_PAIR + 1] = spread.T[0:16, :].reshape(2, 8, tokens)
        for goes, _, copy in stat_copies(j):
            when(goes, copy.start)

    def step_forward_own(j):
        arrive_halos(0, j, True)
        send_stats(j, (*forward(j, OWN), *columns.pop(j)))

    def step_forward_both(j):
        arrive_halos(0, j, False)
        arrive_halos(0, j, True)
        forward_both(j)
        for kind in (0, 1):
            give(kind, j).start()

    def step_backward_pair(j):
        arrive_halos(1, j, False)
        backward_start(j, PAIR)
        arrived(stats.at[j, STAT_OUTER:], stat_sem.at[j])
        backward(j, PAIR)
        for kind in (3, 2):
            give(kind, j).start()

    def step_backward_own(j):
        arrive_halos(1, j, True)
        backward_start(j, OWN)
        backward(j, OWN)

    times = [(0.0, step_own_out, 0), (8.0, step_own_out, 1)]
    for i in range(len(pieces)):
        times.append((6.15 + 0.7 * i, step_pair_in, i))
        if pieces[i][2] == 0:
            times.append((6.9 + 0.7 * i, step_far_in, i))
        late = 4.0 if i >= len(pieces) - 2 else 0.0
        times.append((8.75 + 0.7 * i + late, step_outer_in, i))
    for j in heads:
        if j == 0:
            times.append((11.06, step_forward_pair, j))
            times.append((12.5, step_forward_own, j))
        else:
            times.append((11.5 + 1.4 * j, step_forward_both, j))
        times.append((15.5 + 1.05 * j, step_backward_pair, j))
        times.append((16.5 + (4.5 + 0.5 * j if j > 0 else 0.0), step_backward_own, j))
    for _, step, index in sorted(times, key=lambda entry: entry[0]):
        step(index)

    remote(results, results, send_sem.at[RESULT], result_sem, (pair, sp)).wait()

    def drain(cond, ref, i):
        when(cond, remote(ref, ref, send_sem.at[i], result_sem, (pair, sp)).wait_send)

    whole = near.at[:, :, :, PAIR, 0:tokens, :]
    drain(None, whole, TO_PAIR)
    drain(has_outer, whole, TO_FAR)
    drain(has_far, whole, TO_OUTER)
    for first, cond in ((UP, has_up), (DOWN, has_down)):
        drain(cond, near.at[:, :, :, OWN : PAIR + 1, 0:half, :], first)
        drain(cond & has_outer, near.at[:, :, :, OUTER, 0:half, :], first + 1)
        drain(cond & has_far, near.at[:, :, :, FAR, 0:half, :], first + 2)
    for n, (goes, count, _) in enumerate(stat_copies(0)):
        drain(goes, stats.at[:, 0:count], STAT + n)


def put_out(*refs):
    sources, targets, sems = refs[:4], refs[4:8], refs[8]
    copies = [pltpu.make_async_copy(sources[i], targets[i], sems.at[i]) for i in range(4)]
    for copy in copies:
        copy.start()
    for copy in copies:
        copy.wait()


def on_device(queries, key_vectors, values, grad_out, windows):
    local_shape = queries.shape
    row_count, col_count, features = local_shape[1:]
    head_count = windows.shape[1]
    head_size = features // head_count
    tokens = row_count * col_count
    mine = head_count // 2
    half = tokens // 2
    sizes = (
        head_count,
        head_size,
        row_count,
        col_count,
        lax.axis_size("tm"),
        lax.axis_size("space"),
    )
    flat = (tokens, features)
    low = jnp.bfloat16
    outs = pl.pallas_call(
        functools.partial(kernel, sizes),
        out_shape=[jax.ShapeDtypeStruct(flat, low)] * 4,
        in_specs=[pl.BlockSpec(memory_space=pltpu.HBM)] * 5,
        out_specs=[pl.BlockSpec(memory_space=pltpu.VMEM)] * 4,
        scratch_shapes=[
            pltpu.SMEM((2, head_count), jnp.int32),
            pltpu.VMEM((mine, tokens, 2 * tokens), jnp.float32),
            pltpu.VMEM((2, mine, 2, 4, 2 * tokens, head_size), low),
            pltpu.VMEM((4, mine, tokens, head_size), low),
            pltpu.VMEM((mine, 12, 8, tokens), jnp.float32),
            pltpu.VMEM((2 * tokens, 6 * tokens), jnp.float32),
            pltpu.VMEM((2 * tokens, 6 * tokens), jnp.float32),
            pltpu.VMEM((2 * tokens, 6 * tokens), low),
            pltpu.VMEM((2 * tokens, 6 * tokens), low),
            pltpu.VMEM((2, 4, half, head_size), low),
            pltpu.VMEM((4, 8, tokens), jnp.float32),
            pltpu.SemaphoreType.DMA((3,)),
            pltpu.SemaphoreType.DMA((STAT + 8,)),
            pltpu.SemaphoreType.DMA((4 * mine,)),
            pltpu.SemaphoreType.DMA((4 * mine,)),
            pltpu.SemaphoreType.DMA((2, mine)),
            pltpu.SemaphoreType.DMA((2, mine, 2)),
            pltpu.SemaphoreType.DMA((mine,)),
            pltpu.SemaphoreType.DMA,
        ],
        compiler_params=pltpu.CompilerParams(
            collective_id=0, has_side_effects=True, vmem_limit_bytes=55_600_000
        ),
    )(
        pltpu.with_memory_space_constraint(windows, pltpu.HBM),
        queries.reshape(flat),
        key_vectors.reshape(flat),
        values.reshape(flat),
        grad_out.reshape(flat),
    )
    outs = pl.pallas_call(
        put_out,
        out_shape=[jax.ShapeDtypeStruct(flat, low)] * 4,
        in_specs=[pl.BlockSpec(memory_space=pltpu.VMEM)] * 4,
        out_specs=[pl.BlockSpec(memory_space=pltpu.HBM)] * 4,
        scratch_shapes=[
            pltpu.SemaphoreType.DMA((4,)),
        ],
        compiler_params=pltpu.CompilerParams(vmem_limit_bytes=4_000_000),
    )(*outs)
    return tuple(out.reshape(local_shape) for out in outs)


def solution(mesh):
    spec = P("tm", "space", None, None)
    return jax.shard_map(
        on_device,
        mesh=mesh,
        in_specs=(spec, spec, spec, spec, P()),
        out_specs=(spec, spec, spec, spec),
        check_vma=False,
    )
```

```python
import functools
import math

import jax
import jax.numpy as jnp
from jax import lax
from jax.experimental import pallas as pl
from jax.experimental.pallas import tpu as pltpu
from jax.sharding import PartitionSpec as P

masked_score = -1e30
MESH = pl.DeviceIdType.MESH

OUTER, OWN, PAIR, FAR = range(4)

STAT_OWN, STAT_PAIR, STAT_FAR, STAT_OUTER = range(4)
ABOVE, BELOW = 4, 8

TO_PAIR, TO_FAR, TO_OUTER, RESULT, UP, DOWN, STAT = 0, 1, 2, 3, 4, 7, 10


def dot_nt(a, b):
    return lax.dot_general(a, b, (((1,), (1,)), ((), ())), preferred_element_type=jnp.float32)


def dot_nn(a, b):
    return lax.dot_general(a, b, (((1,), (0,)), ((), ())), preferred_element_type=jnp.float32)


def when(cond, action):
    if cond is None:
        action()
    else:
        pl.when(cond)(action)


def kernel(
    sizes,
    win_hbm,
    q_ref,
    k_ref,
    v_ref,
    g_ref,
    att_ref,
    gq_ref,
    gk_ref,
    gv_ref,
    win_ref,
    bias,
    near,
    results,
    stats,
    scores_ref,
    grad_weights_ref,
    powers_ref,
    grad_scores_ref,
    no_rows,
    no_stats,
    load_sem,
    send_sem,
    pair_sem,
    outer_sem,
    far_sem,
    halo_sem,
    stat_sem,
    result_sem,
):
    head_count, head_size, row_count, col_count, n_tm, n_space = sizes
    tokens = row_count * col_count
    half = tokens // 2
    mine = head_count // 2
    scale = 1.0 / math.sqrt(head_size)
    scale2 = scale * math.log2(math.e)
    tm, sp = lax.axis_index("tm"), lax.axis_index("space")
    side = lax.rem(tm, 2)
    pair = tm + 1 - 2 * side
    inner_to = tm + 2 - 4 * side
    outer_to = tm - 2 + 4 * side
    has_far = (inner_to >= 0) & (inner_to < n_tm)
    has_outer = (outer_to >= 0) & (outer_to < n_tm)
    has_up = sp > 0
    has_down = sp < n_space - 1
    heads = range(mine)
    blocks = [(phase, j) for phase in range(2) for j in heads]
    blocks.insert(mine - 1, blocks.pop(mine))
    pieces = [(phase, j, a) for phase, j in blocks for a in range(2)]
    ins = ((k_ref, v_ref), (q_ref, g_ref))
    outs = (att_ref, gq_ref, gk_ref, gv_ref)

    def head_cols(j, of_pair=False):
        first = (1 - side if of_pair else side) * mine + j
        return pl.ds(pl.multiple_of(first * head_size, head_size), head_size)

    barrier = pltpu.get_barrier_semaphore()

    def greet(cond, tm_to, sp_to):
        def signal():
            pl.semaphore_signal(barrier, inc=1, device_id=(tm_to, sp_to), device_id_type=MESH)

        when(cond, signal)

    greet(None, pair, sp)
    greet(has_far, inner_to, sp)
    greet(has_outer, outer_to, sp)
    greet(has_up, tm, sp - 1)
    greet(has_down, tm, sp + 1)

    def main_rows(i, slot):
        phase, j, a = pieces[i]
        return near.at[phase, j, a, slot, 0:tokens, :]

    def load(i):
        phase, j, a = pieces[i]
        return pltpu.make_async_copy(
            ins[phase][a].at[:, head_cols(j)], main_rows(i, OWN), load_sem.at[phase]
        )

    for i in range(len(pieces)):
        load(i).start()
    get_windows = pltpu.make_async_copy(win_hbm, win_ref, load_sem.at[2])
    get_windows.start()
    no_rows[...] = jnp.zeros_like(no_rows)
    no_stats[...] = jnp.zeros_like(no_stats)

    def remote(src, dst, send, recv, device):
        return pltpu.make_async_remote_copy(
            src_ref=src,
            dst_ref=dst,
            send_sem=send,
            recv_sem=recv,
            device_id=device,
            device_id_type=MESH,
        )

    def to_pair(i):
        phase, j, a = pieces[i]
        return remote(
            ins[phase][a].at[:, head_cols(j, True)],
            main_rows(i, PAIR),
            send_sem.at[TO_PAIR],
            pair_sem.at[i],
            (pair, sp),
        )

    def own_to_far(i):
        phase, j, a = pieces[i]
        return remote(
            main_rows(i, OWN),
            main_rows(i, FAR),
            send_sem.at[TO_FAR],
            far_sem.at[phase, j],
            (outer_to, sp),
        )

    def pair_to_outer(i):
        return remote(
            main_rows(i, PAIR),
            main_rows(i, OUTER),
            send_sem.at[TO_OUTER],
            outer_sem.at[i],
            (inner_to, sp),
        )

    def of_kind(slot):
        return {OUTER: 1, FAR: 2}.get(slot, 0)

    def halo_up(i, slot):
        phase, j, a = pieces[i]
        rows = near.at[phase, j, a, slot]
        return remote(
            rows.at[0:half, :],
            rows.at[tokens : tokens + half, :],
            send_sem.at[UP + of_kind(slot)],
            halo_sem.at[phase, j, of_kind(slot) % 2],
            (tm, sp - 1),
        )

    def halo_down(i, slot):
        phase, j, a = pieces[i]
        rows = near.at[phase, j, a, slot]
        return remote(
            rows.at[half:tokens, :],
            rows.at[tokens + half : 2 * tokens, :],
            send_sem.at[DOWN + of_kind(slot)],
            halo_sem.at[phase, j, of_kind(slot) % 2],
            (tm, sp + 1),
        )

    def halos(i, slot):
        when(has_up, lambda: halo_up(i, slot).start())
        when(has_down, lambda: halo_down(i, slot).start())

    expected = (
        1
        + has_far.astype(jnp.int32)
        + has_outer.astype(jnp.int32)
        + has_up.astype(jnp.int32)
        + has_down.astype(jnp.int32)
    )
    pl.semaphore_wait(barrier, expected)
    for i in range(len(pieces)):
        to_pair(i).start()
    def step_own_out(phase):
        rows = near.at[phase, :, :, OWN, 0:tokens, :]
        pltpu.make_async_copy(rows, rows, load_sem.at[phase]).wait()
        for i in range(len(pieces)):
            if pieces[i][0] == phase:
                when(has_outer, lambda: own_to_far(i).start())
                halos(i, OWN)

    def fill(source, target, sem):
        pltpu.make_async_copy(source, target, sem).start()

    def fill_side(first_row, first_stat):
        rows = slice(first_row, first_row + half)

        def all_frames():
            for phase in range(2):
                for j in heads:
                    at = near.at[phase, j, :, :, rows, :]
                    fill(no_rows.at[:, 0:1], at.at[:, 0:1], halo_sem.at[phase, j, 1])
                    fill(no_rows.at[:, 1:4], at.at[:, 1:4], halo_sem.at[phase, j, 0])
            for j in heads:
                last = first_stat + STAT_OUTER
                fill(no_stats.at[0:3], stats.at[j, first_stat:last], stat_sem.at[j, 0])
                fill(no_stats.at[3], stats.at[j, last], stat_sem.at[j, 1])

        def one_frame(slot, stat):
            for phase in range(2):
                for j in heads:
                    sem = halo_sem.at[phase, j, of_kind(slot) % 2]
                    fill(no_rows.at[:, slot], near.at[phase, j, :, slot, rows, :], sem)
            for j in heads:
                sem = stat_sem.at[j, stat // STAT_OUTER]
                fill(no_stats.at[0], stats.at[j, first_stat + stat], sem)

        return all_frames, one_frame

    for has_side, parts in (
        (has_down, fill_side(tokens, BELOW)),
        (has_up, fill_side(tokens + half, ABOVE)),
    ):
        all_frames, one_frame = parts
        pl.when(jnp.logical_not(has_side))(all_frames)
        no_outer, no_far = jnp.logical_not(has_outer), jnp.logical_not(has_far)
        pl.when(has_side & no_outer)(lambda: one_frame(OUTER, STAT_OUTER))
        pl.when(has_side & no_far)(lambda: one_frame(FAR, STAT_FAR))

    for has_frame, slot, stat in ((has_outer, OUTER, STAT_OUTER), (has_far, FAR, STAT_FAR)):

        @pl.when(jnp.logical_not(has_frame))
        def _():
            for phase in range(2):
                for j in heads:
                    near[phase, j, :, slot, 0:tokens, :] = jnp.zeros(
                        (2, tokens, head_size), near.dtype
                    )
            for j in heads:
                fill(no_stats.at[0], stats.at[j, stat], stat_sem.at[j, stat // STAT_OUTER])

    own_id = lax.broadcasted_iota(jnp.int32, (tokens, 2 * tokens), 0)
    near_id = lax.broadcasted_iota(jnp.int32, (tokens, 2 * tokens), 1)
    own_row, own_col = own_id // col_count, own_id % col_count
    near_row, near_col = near_id // col_count, near_id % col_count
    upper = near_row >= row_count + row_count // 2
    near_row = jnp.where(upper, near_row - 2 * row_count, near_row)
    global_row = sp * row_count + near_row
    row_inside = (global_row >= 0) & (global_row < n_space * row_count)
    row_gap = jnp.where(row_inside, jnp.abs(own_row - near_row), 1 << 20)
    col_gap = jnp.abs(own_col - near_col)

    get_windows.wait()
    for j in heads:
        h = side * mine + j
        inside = (row_gap <= win_ref[0, h]) & (col_gap <= win_ref[1, h])
        bias[j] = jnp.where(inside, 0.0, masked_score)

    def window(j, frame):
        here = bias[j]
        there = here + jnp.where(has_outer if frame == OWN else has_far, 0.0, masked_score)
        order = [there, here, here] if frame == OWN else [here, here, there]
        return jnp.concatenate(order, axis=1)

    def around(phase, j, a, frame):
        return near[phase, j, a, frame - 1 : frame + 2].reshape(6 * tokens, head_size)

    def put(kind, j, frame, value):
        if frame == OWN:
            outs[kind][:, head_cols(j)] = value
        else:
            results[kind, j] = value

    def give(kind, j):
        return remote(
            results.at[kind, j],
            outs[kind].at[:, head_cols(j)],
            send_sem.at[RESULT],
            result_sem,
            (pair, sp),
        )

    def forward(j, frame):
        at = slice((frame - OWN) * tokens, (frame - OWN + 1) * tokens)
        scores_ref[at] = dot_nt(near[1, j, 0, frame, 0:tokens, :], around(0, j, 0, frame))
        grad_weights_ref[at] = dot_nt(near[1, j, 1, frame, 0:tokens, :], around(0, j, 1, frame))
        scores = scores_ref[at] * scale2 + window(j, frame)
        top = jnp.max(scores, axis=1, keepdims=True)
        powers = jnp.exp2(scores - top)
        total = jnp.sum(powers, axis=1, keepdims=True)
        share = 1.0 / total
        powers_ref[at] = powers.astype(jnp.bfloat16)
        grad_weights = grad_weights_ref[at]
        out_dot = jnp.sum(powers * grad_weights, axis=1, keepdims=True) * share
        grad_scores_ref[at] = (powers * (grad_weights - out_dot)).astype(jnp.bfloat16)
        found = (top + jnp.log2(total), out_dot)
        if frame == PAIR:
            columns[j] = found
        else:
            send_stats(j, (*found, *columns.pop(j)))
        attended = dot_nn(powers_ref[at], around(0, j, 1, frame)) * share
        put(0, j, frame, attended.astype(jnp.bfloat16))
        query_sum = dot_nn(grad_scores_ref[at], around(0, j, 0, frame)) * (share * scale)
        put(1, j, frame, query_sum.astype(jnp.bfloat16))
    row_lane = lax.broadcasted_iota(jnp.int32, (1, tokens), 1)

    def stat_row(j, r, frame):
        order = (STAT_OUTER, STAT_OWN, STAT_PAIR, STAT_FAR)
        parts = []
        for stat in order[frame - 1 : frame + 2]:
            parts.append(stats[j, stat, r : r + 1, :])
            down, up = stats[j, BELOW + stat, r : r + 1, :], stats[j, ABOVE + stat, r : r + 1, :]
            parts.append(jnp.where(row_lane < half, down, up))
        return jnp.concatenate(parts, axis=1)

    def backward_rows(frame):
        return slice((frame - OWN) * tokens, (frame - OWN + 1) * tokens)

    def backward_start(j, frame):
        at = backward_rows(frame)
        key = near[0, j, 0, frame, 0:tokens, :]
        val = near[0, j, 1, frame, 0:tokens, :]
        scores_ref[at] = dot_nt(key, around(1, j, 0, frame)) * scale2 + window(j, frame)
        grad_weights_ref[at] = dot_nt(val, around(1, j, 1, frame))

    def backward(j, frame):
        at = backward_rows(frame)
        soft = jnp.exp2(scores_ref[at] - stat_row(j, 0, frame))
        grad_scores = soft * (grad_weights_ref[at] - stat_row(j, 1, frame))
        value_sum = dot_nn(soft.astype(jnp.bfloat16), around(1, j, 1, frame))
        put(3, j, frame, value_sum.astype(jnp.bfloat16))
        key_sum = dot_nn(grad_scores.astype(jnp.bfloat16), around(1, j, 0, frame))
        put(2, j, frame, (key_sum * scale).astype(jnp.bfloat16))

    def stat_copies(j):
        block = stats.at[j]
        found = [
            (has_far, STAT_PAIR, STAT_OUTER, 1, (inner_to, sp)),
            (has_outer, STAT_OWN, STAT_FAR, 1, (outer_to, sp)),
        ]
        for at, there, goes in ((BELOW, sp - 1, has_up), (ABOVE, sp + 1, has_down)):
            found += [
                (goes, STAT_OWN, at + STAT_OWN, 2, (tm, there)),
                (goes & has_far, STAT_PAIR, at + STAT_OUTER, 1, (inner_to, there)),
                (goes & has_outer, STAT_OWN, at + STAT_FAR, 1, (outer_to, there)),
            ]
        return [
            (
                goes,
                count,
                remote(
                    block.at[src : src + count],
                    block.at[dst : dst + count],
                    send_sem.at[STAT + n],
                    stat_sem.at[j, dst % 4 // STAT_OUTER],
                    device,
                ),
            )
            for n, (goes, src, dst, count, device) in enumerate(found)
        ]

    def step_pair_in(i):
        to_pair(i).wait_recv()
        when(has_far, lambda: pair_to_outer(i).start())
        halos(i, PAIR)

    def step_far_in(i):
        phase, j, _ = pieces[i]

        @pl.when(has_far)
        def _():
            rows = near.at[phase, j, :, FAR, 0:tokens, :]
            remote(rows, rows, send_sem.at[TO_FAR], far_sem.at[phase, j], (pair, sp)).wait_recv()
            for at in (i, i + 1):
                halos(at, FAR)

    def step_outer_in(i):
        @pl.when(has_outer)
        def _():
            pair_to_outer(i).wait_recv()
            halos(i, OUTER)

    def arrived(ref, sem):
        pltpu.make_async_copy(ref, ref, sem).wait()

    def arrive_halos(phase, j, outer):
        rows = slice(tokens, 2 * tokens)
        if outer:
            arrived(near.at[phase, j, :, OUTER, rows, :], halo_sem.at[phase, j, 1])
        else:
            arrived(near.at[phase, j, :, OWN : FAR + 1, rows, :], halo_sem.at[phase, j, 0])

    columns = {}

    def step_forward_pair(j):
        arrive_halos(0, j, False)
        forward(j, PAIR)
        for kind in (0, 1):
            give(kind, j).start()

    def send_stats(j, found):
        lane = lax.broadcasted_iota(jnp.int32, (tokens, tokens), 1)
        spread = jnp.zeros((tokens, tokens), jnp.float32)
        for at, column in zip((0, 1, 8, 9), found, strict=True):
            spread = jnp.where(lane == at, column, spread)
        stats[j, STAT_OWN : STAT_PAIR + 1] = spread.T[0:16, :].reshape(2, 8, tokens)
        for goes, _, copy in stat_copies(j):
            when(goes, copy.start)

    def step_forward_own(j):
        arrive_halos(0, j, True)
        forward(j, OWN)

    def step_backward_pair(j):
        arrive_halos(1, j, False)
        backward_start(j, PAIR)
        arrived(stats.at[j, 0:7], stat_sem.at[j, 0])
        backward(j, PAIR)
        for kind in (3, 2):
            give(kind, j).start()

    def step_backward_own(j):
        arrive_halos(1, j, True)
        backward_start(j, OWN)
        arrived(stats.at[j, 0:3], stat_sem.at[j, 1])
        backward(j, OWN)

    times = [(0.0, step_own_out, 0), (7.5, step_own_out, 1)]
    for i, (phase, j, a) in enumerate(pieces):
        times.append((6.15 + 0.7 * i, step_pair_in, i))
        if a == 0:
            at = 6.9 + 0.7 * i if phase == 0 else (11.85 if j == 0 else 14.46)
            times.append((at, step_far_in, i))
        late = 0.0
        if phase == 1:
            late = 2.2 if j == 0 else (0.25 if j == mine - 1 else 0.0)
        times.append((8.75 + 0.7 * i + late, step_outer_in, i))
    for j in heads:
        times.append((9.66 if j == 0 else 11.1 + 1.4 * j, step_forward_pair, j))
        times.append((13.1 + 1.4 * j if j == mine - 1 else 11.5 + 2.2 * j, step_forward_own, j))
        times.append((15.0 + 1.6 * j, step_backward_pair, j))
        times.append((16.75 + (4.5 + 0.5 * j if j > 0 else 0.0), step_backward_own, j))
    for _, step, index in sorted(times, key=lambda entry: entry[0]):
        step(index)

    remote(results, results, send_sem.at[RESULT], result_sem, (pair, sp)).wait()

    def drain(cond, ref, i):
        when(cond, remote(ref, ref, send_sem.at[i], result_sem, (pair, sp)).wait_send)

    whole = near.at[:, :, :, PAIR, 0:tokens, :]
    drain(None, whole, TO_PAIR)
    drain(has_outer, whole, TO_FAR)
    drain(has_far, whole, TO_OUTER)
    for first, cond in ((UP, has_up), (DOWN, has_down)):
        drain(cond, near.at[:, :, :, OWN : PAIR + 1, 0:half, :], first)
        drain(cond & has_outer, near.at[:, :, :, OUTER, 0:half, :], first + 1)
        drain(cond & has_far, near.at[:, :, :, FAR, 0:half, :], first + 2)
    for n, (goes, count, _) in enumerate(stat_copies(0)):
        drain(goes, stats.at[:, 0:count], STAT + n)


def put_out(*refs):
    sources, targets, sems = refs[:4], refs[4:8], refs[8]
    copies = [pltpu.make_async_copy(sources[i], targets[i], sems.at[i]) for i in range(4)]
    for copy in copies:
        copy.start()
    for copy in copies:
        copy.wait()


def on_device(queries, key_vectors, values, grad_out, windows):
    local_shape = queries.shape
    row_count, col_count, features = local_shape[1:]
    head_count = windows.shape[1]
    head_size = features // head_count
    tokens = row_count * col_count
    mine = head_count // 2
    half = tokens // 2
    sizes = (
        head_count,
        head_size,
        row_count,
        col_count,
        lax.axis_size("tm"),
        lax.axis_size("space"),
    )
    flat = (tokens, features)
    low = jnp.bfloat16
    outs = pl.pallas_call(
        functools.partial(kernel, sizes),
        out_shape=[jax.ShapeDtypeStruct(flat, low)] * 4,
        in_specs=[pl.BlockSpec(memory_space=pltpu.HBM)] * 5,
        out_specs=[pl.BlockSpec(memory_space=pltpu.VMEM)] * 4,
        scratch_shapes=[
            pltpu.SMEM((2, head_count), jnp.int32),
            pltpu.VMEM((mine, tokens, 2 * tokens), jnp.float32),
            pltpu.VMEM((2, mine, 2, 4, 2 * tokens, head_size), low),
            pltpu.VMEM((4, mine, tokens, head_size), low),
            pltpu.VMEM((mine, 12, 8, tokens), jnp.float32),
            pltpu.VMEM((2 * tokens, 6 * tokens), jnp.float32),
            pltpu.VMEM((2 * tokens, 6 * tokens), jnp.float32),
            pltpu.VMEM((2 * tokens, 6 * tokens), low),
            pltpu.VMEM((2 * tokens, 6 * tokens), low),
            pltpu.VMEM((2, 4, half, head_size), low),
            pltpu.VMEM((4, 8, tokens), jnp.float32),
            pltpu.SemaphoreType.DMA((3,)),
            pltpu.SemaphoreType.DMA((STAT + 8,)),
            pltpu.SemaphoreType.DMA((4 * mine,)),
            pltpu.SemaphoreType.DMA((4 * mine,)),
            pltpu.SemaphoreType.DMA((2, mine)),
            pltpu.SemaphoreType.DMA((2, mine, 2)),
            pltpu.SemaphoreType.DMA((mine, 2)),
            pltpu.SemaphoreType.DMA,
        ],
        compiler_params=pltpu.CompilerParams(
            collective_id=0, has_side_effects=True, vmem_limit_bytes=55_600_000
        ),
    )(
        pltpu.with_memory_space_constraint(windows, pltpu.HBM),
        queries.reshape(flat),
        key_vectors.reshape(flat),
        values.reshape(flat),
        grad_out.reshape(flat),
    )
    outs = pl.pallas_call(
        put_out,
        out_shape=[jax.ShapeDtypeStruct(flat, low)] * 4,
        in_specs=[pl.BlockSpec(memory_space=pltpu.VMEM)] * 4,
        out_specs=[pl.BlockSpec(memory_space=pltpu.HBM)] * 4,
        scratch_shapes=[
            pltpu.SemaphoreType.DMA((4,)),
        ],
        compiler_params=pltpu.CompilerParams(vmem_limit_bytes=4_000_000),
    )(*outs)
    return tuple(out.reshape(local_shape) for out in outs)


def solution(mesh):
    spec = P("tm", "space", None, None)
    return jax.shard_map(
        on_device,
        mesh=mesh,
        in_specs=(spec, spec, spec, spec, P()),
        out_specs=(spec, spec, spec, spec),
        check_vma=False,
    )
```

```python
import functools
import math

import jax
import jax.numpy as jnp
from jax import lax
from jax.experimental import pallas as pl
from jax.experimental.pallas import tpu as pltpu
from jax.sharding import PartitionSpec as P

masked_score = -1e30
MESH = pl.DeviceIdType.MESH

OUTER, OWN, PAIR, FAR = range(4)

STAT_OWN, STAT_PAIR, STAT_FAR, STAT_OUTER = range(4)
ABOVE, BELOW = 4, 8

TO_PAIR, TO_FAR, TO_OUTER, RESULT, UP, DOWN, STAT = 0, 1, 2, 3, 4, 7, 10


def dot_nt(a, b):
    return lax.dot_general(a, b, (((1,), (1,)), ((), ())), preferred_element_type=jnp.float32)


def dot_nn(a, b):
    return lax.dot_general(a, b, (((1,), (0,)), ((), ())), preferred_element_type=jnp.float32)


def when(cond, action):
    if cond is None:
        action()
    else:
        pl.when(cond)(action)


def kernel(
    sizes,
    win_hbm,
    q_ref,
    k_ref,
    v_ref,
    g_ref,
    att_ref,
    gq_ref,
    gk_ref,
    gv_ref,
    win_ref,
    bias,
    near,
    results,
    stats,
    scores_ref,
    grad_weights_ref,
    powers_ref,
    grad_scores_ref,
    no_rows,
    no_stats,
    load_sem,
    send_sem,
    pair_sem,
    outer_sem,
    far_sem,
    halo_sem,
    stat_sem,
    result_sem,
):
    head_count, head_size, row_count, col_count, n_tm, n_space = sizes
    tokens = row_count * col_count
    half = tokens // 2
    mine = head_count // 2
    scale = 1.0 / math.sqrt(head_size)
    scale2 = scale * math.log2(math.e)
    tm, sp = lax.axis_index("tm"), lax.axis_index("space")
    side = lax.rem(tm, 2)
    pair = tm + 1 - 2 * side
    inner_to = tm + 2 - 4 * side
    outer_to = tm - 2 + 4 * side
    has_far = (inner_to >= 0) & (inner_to < n_tm)
    has_outer = (outer_to >= 0) & (outer_to < n_tm)
    has_up = sp > 0
    has_down = sp < n_space - 1
    heads = range(mine)
    pieces = [(phase, j, a) for phase in range(2) for j in heads for a in range(2)]
    ins = ((k_ref, v_ref), (q_ref, g_ref))
    outs = (att_ref, gq_ref, gk_ref, gv_ref)

    def head_cols(j, of_pair=False):
        first = (1 - side if of_pair else side) * mine + j
        return pl.ds(pl.multiple_of(first * head_size, head_size), head_size)

    barrier = pltpu.get_barrier_semaphore()

    def greet(cond, tm_to, sp_to):
        def signal():
            pl.semaphore_signal(barrier, inc=1, device_id=(tm_to, sp_to), device_id_type=MESH)

        when(cond, signal)

    greet(None, pair, sp)
    greet(has_far, inner_to, sp)
    greet(has_outer, outer_to, sp)
    greet(has_up, tm, sp - 1)
    greet(has_down, tm, sp + 1)

    def main_rows(i, slot):
        phase, j, a = pieces[i]
        return near.at[phase, j, a, slot, 0:tokens, :]

    def load(i):
        phase, j, a = pieces[i]
        return pltpu.make_async_copy(
            ins[phase][a].at[:, head_cols(j)], main_rows(i, OWN), load_sem.at[phase]
        )

    for i in range(len(pieces)):
        load(i).start()
    get_windows = pltpu.make_async_copy(win_hbm, win_ref, load_sem.at[2])
    get_windows.start()
    no_rows[...] = jnp.zeros_like(no_rows)
    no_stats[...] = jnp.zeros_like(no_stats)

    def remote(src, dst, send, recv, device):
        return pltpu.make_async_remote_copy(
            src_ref=src,
            dst_ref=dst,
            send_sem=send,
            recv_sem=recv,
            device_id=device,
            device_id_type=MESH,
        )

    def to_pair(i):
        phase, j, a = pieces[i]
        return remote(
            ins[phase][a].at[:, head_cols(j, True)],
            main_rows(i, PAIR),
            send_sem.at[TO_PAIR],
            pair_sem.at[i],
            (pair, sp),
        )

    def own_to_far(i):
        phase, j, a = pieces[i]
        return remote(
            main_rows(i, OWN),
            main_rows(i, FAR),
            send_sem.at[TO_FAR],
            far_sem.at[phase, j],
            (outer_to, sp),
        )

    def pair_to_outer(i):
        return remote(
            main_rows(i, PAIR),
            main_rows(i, OUTER),
            send_sem.at[TO_OUTER],
            outer_sem.at[i],
            (inner_to, sp),
        )

    def of_kind(slot):
        return {OUTER: 1, FAR: 2}.get(slot, 0)

    def halo_up(i, slot):
        phase, j, a = pieces[i]
        rows = near.at[phase, j, a, slot]
        return remote(
            rows.at[0:half, :],
            rows.at[tokens : tokens + half, :],
            send_sem.at[UP + of_kind(slot)],
            halo_sem.at[phase, j, of_kind(slot) % 2],
            (tm, sp - 1),
        )

    def halo_down(i, slot):
        phase, j, a = pieces[i]
        rows = near.at[phase, j, a, slot]
        return remote(
            rows.at[half:tokens, :],
            rows.at[tokens + half : 2 * tokens, :],
            send_sem.at[DOWN + of_kind(slot)],
            halo_sem.at[phase, j, of_kind(slot) % 2],
            (tm, sp + 1),
        )

    def halos(i, slot):
        when(has_up, lambda: halo_up(i, slot).start())
        when(has_down, lambda: halo_down(i, slot).start())

    expected = (
        1
        + has_far.astype(jnp.int32)
        + has_outer.astype(jnp.int32)
        + has_up.astype(jnp.int32)
        + has_down.astype(jnp.int32)
    )
    pl.semaphore_wait(barrier, expected)
    for i in range(len(pieces)):
        to_pair(i).start()
    def step_own_out(phase):
        rows = near.at[phase, :, :, OWN, 0:tokens, :]
        pltpu.make_async_copy(rows, rows, load_sem.at[phase]).wait()
        for i in range(len(pieces)):
            if pieces[i][0] == phase:
                when(has_outer, lambda: own_to_far(i).start())
                if phase == 0:
                    halos(i, OWN)

    def step_own_halo(j):
        for i in range(len(pieces)):
            if pieces[i][:2] == (1, j):
                halos(i, OWN)

    def fill(source, target, sem):
        pltpu.make_async_copy(source, target, sem).start()

    def fill_side(first_row, first_stat):
        rows = slice(first_row, first_row + half)

        def all_frames():
            for phase in range(2):
                for j in heads:
                    at = near.at[phase, j, :, :, rows, :]
                    fill(no_rows.at[:, 0:1], at.at[:, 0:1], halo_sem.at[phase, j, 1])
                    fill(no_rows.at[:, 1:4], at.at[:, 1:4], halo_sem.at[phase, j, 0])
            for j in heads:
                last = first_stat + STAT_OUTER
                fill(no_stats.at[0:3], stats.at[j, first_stat:last], stat_sem.at[j, 0])
                fill(no_stats.at[3], stats.at[j, last], stat_sem.at[j, 1])

        def one_frame(slot, stat):
            for phase in range(2):
                for j in heads:
                    sem = halo_sem.at[phase, j, of_kind(slot) % 2]
                    fill(no_rows.at[:, slot], near.at[phase, j, :, slot, rows, :], sem)
            for j in heads:
                sem = stat_sem.at[j, stat // STAT_OUTER]
                fill(no_stats.at[0], stats.at[j, first_stat + stat], sem)

        return all_frames, one_frame

    for has_side, parts in (
        (has_down, fill_side(tokens, BELOW)),
        (has_up, fill_side(tokens + half, ABOVE)),
    ):
        all_frames, one_frame = parts
        pl.when(jnp.logical_not(has_side))(all_frames)
        no_outer, no_far = jnp.logical_not(has_outer), jnp.logical_not(has_far)
        pl.when(has_side & no_outer)(lambda: one_frame(OUTER, STAT_OUTER))
        pl.when(has_side & no_far)(lambda: one_frame(FAR, STAT_FAR))

    for has_frame, slot, stat in ((has_outer, OUTER, STAT_OUTER), (has_far, FAR, STAT_FAR)):

        @pl.when(jnp.logical_not(has_frame))
        def _():
            for phase in range(2):
                for j in heads:
                    near[phase, j, :, slot, 0:tokens, :] = jnp.zeros(
                        (2, tokens, head_size), near.dtype
                    )
            for j in heads:
                fill(no_stats.at[0], stats.at[j, stat], stat_sem.at[j, stat // STAT_OUTER])

    own_id = lax.broadcasted_iota(jnp.int32, (tokens, 2 * tokens), 0)
    near_id = lax.broadcasted_iota(jnp.int32, (tokens, 2 * tokens), 1)
    own_row, own_col = own_id // col_count, own_id % col_count
    near_row, near_col = near_id // col_count, near_id % col_count
    upper = near_row >= row_count + row_count // 2
    near_row = jnp.where(upper, near_row - 2 * row_count, near_row)
    global_row = sp * row_count + near_row
    row_inside = (global_row >= 0) & (global_row < n_space * row_count)
    row_gap = jnp.where(row_inside, jnp.abs(own_row - near_row), 1 << 20)
    col_gap = jnp.abs(own_col - near_col)

    get_windows.wait()
    for j in heads:
        h = side * mine + j
        inside = (row_gap <= win_ref[0, h]) & (col_gap <= win_ref[1, h])
        bias[j] = jnp.where(inside, 0.0, masked_score)

    def window(j, frame):
        here = bias[j]
        there = here + jnp.where(has_outer if frame == OWN else has_far, 0.0, masked_score)
        order = [there, here, here] if frame == OWN else [here, here, there]
        return jnp.concatenate(order, axis=1)

    def around(phase, j, a, frame):
        return near[phase, j, a, frame - 1 : frame + 2].reshape(6 * tokens, head_size)

    def put(kind, j, frame, value):
        if frame == OWN:
            outs[kind][:, head_cols(j)] = value
        else:
            results[kind, j] = value

    def give(kind, j):
        return remote(
            results.at[kind, j],
            outs[kind].at[:, head_cols(j)],
            send_sem.at[RESULT],
            result_sem,
            (pair, sp),
        )

    def forward(j, frame):
        at = slice((frame - OWN) * tokens, (frame - OWN + 1) * tokens)
        scores_ref[at] = dot_nt(near[1, j, 0, frame, 0:tokens, :], around(0, j, 0, frame))
        grad_weights_ref[at] = dot_nt(near[1, j, 1, frame, 0:tokens, :], around(0, j, 1, frame))
        scores = scores_ref[at] * scale2 + window(j, frame)
        top = jnp.max(scores, axis=1, keepdims=True)
        powers = jnp.exp2(scores - top)
        total = jnp.sum(powers, axis=1, keepdims=True)
        share = 1.0 / total
        powers_ref[at] = powers.astype(jnp.bfloat16)
        grad_weights = grad_weights_ref[at]
        out_dot = jnp.sum(powers * grad_weights, axis=1, keepdims=True) * share
        grad_scores_ref[at] = (powers * (grad_weights - out_dot)).astype(jnp.bfloat16)
        found = (top + jnp.log2(total), out_dot)
        if frame == PAIR:
            columns[j] = found
        else:
            send_stats(j, (*found, *columns.pop(j)))
        attended = dot_nn(powers_ref[at], around(0, j, 1, frame)) * share
        put(0, j, frame, attended.astype(jnp.bfloat16))
        query_sum = dot_nn(grad_scores_ref[at], around(0, j, 0, frame)) * (share * scale)
        put(1, j, frame, query_sum.astype(jnp.bfloat16))
    row_lane = lax.broadcasted_iota(jnp.int32, (1, tokens), 1)

    def stat_row(j, r, frame):
        order = (STAT_OUTER, STAT_OWN, STAT_PAIR, STAT_FAR)
        parts = []
        for stat in order[frame - 1 : frame + 2]:
            parts.append(stats[j, stat, r : r + 1, :])
            down, up = stats[j, BELOW + stat, r : r + 1, :], stats[j, ABOVE + stat, r : r + 1, :]
            parts.append(jnp.where(row_lane < half, down, up))
        return jnp.concatenate(parts, axis=1)

    def backward_rows(frame):
        return slice((frame - OWN) * tokens, (frame - OWN + 1) * tokens)

    def backward_start(j, frame):
        at = backward_rows(frame)
        key = near[0, j, 0, frame, 0:tokens, :]
        val = near[0, j, 1, frame, 0:tokens, :]
        scores_ref[at] = dot_nt(key, around(1, j, 0, frame)) * scale2 + window(j, frame)
        grad_weights_ref[at] = dot_nt(val, around(1, j, 1, frame))

    def backward(j, frame):
        at = backward_rows(frame)
        soft = jnp.exp2(scores_ref[at] - stat_row(j, 0, frame))
        grad_scores = soft * (grad_weights_ref[at] - stat_row(j, 1, frame))
        value_sum = dot_nn(soft.astype(jnp.bfloat16), around(1, j, 1, frame))
        put(3, j, frame, value_sum.astype(jnp.bfloat16))
        key_sum = dot_nn(grad_scores.astype(jnp.bfloat16), around(1, j, 0, frame))
        put(2, j, frame, (key_sum * scale).astype(jnp.bfloat16))

    def stat_copies(j):
        block = stats.at[j]
        found = [
            (has_far, STAT_PAIR, STAT_OUTER, 1, (inner_to, sp)),
            (has_outer, STAT_OWN, STAT_FAR, 1, (outer_to, sp)),
        ]
        for at, there, goes in ((BELOW, sp - 1, has_up), (ABOVE, sp + 1, has_down)):
            found += [
                (goes, STAT_OWN, at + STAT_OWN, 2, (tm, there)),
                (goes & has_far, STAT_PAIR, at + STAT_OUTER, 1, (inner_to, there)),
                (goes & has_outer, STAT_OWN, at + STAT_FAR, 1, (outer_to, there)),
            ]
        return [
            (
                goes,
                count,
                remote(
                    block.at[src : src + count],
                    block.at[dst : dst + count],
                    send_sem.at[STAT + n],
                    stat_sem.at[j, dst % 4 // STAT_OUTER],
                    device,
                ),
            )
            for n, (goes, src, dst, count, device) in enumerate(found)
        ]

    def step_pair_in(i):
        to_pair(i).wait_recv()
        when(has_far, lambda: pair_to_outer(i).start())
        halos(i, PAIR)

    def step_far_in(i):
        phase, j, _ = pieces[i]

        @pl.when(has_far)
        def _():
            rows = near.at[phase, j, :, FAR, 0:tokens, :]
            remote(rows, rows, send_sem.at[TO_FAR], far_sem.at[phase, j], (pair, sp)).wait_recv()
            for at in (i, i + 1):
                halos(at, FAR)

    def step_outer_in(i):
        @pl.when(has_outer)
        def _():
            pair_to_outer(i).wait_recv()
            halos(i, OUTER)

    def arrived(ref, sem):
        pltpu.make_async_copy(ref, ref, sem).wait()

    def arrive_halos(phase, j, outer):
        rows = slice(tokens, 2 * tokens)
        if outer:
            arrived(near.at[phase, j, :, OUTER, rows, :], halo_sem.at[phase, j, 1])
        else:
            arrived(near.at[phase, j, :, OWN : FAR + 1, rows, :], halo_sem.at[phase, j, 0])

    columns = {}

    def step_forward_pair(j):
        arrive_halos(0, j, False)
        forward(j, PAIR)
        for kind in (0, 1):
            give(kind, j).start()

    def send_stats(j, found):
        lane = lax.broadcasted_iota(jnp.int32, (tokens, tokens), 1)
        spread = jnp.zeros((tokens, tokens), jnp.float32)
        for at, column in zip((0, 1, 8, 9), found, strict=True):
            spread = jnp.where(lane == at, column, spread)
        stats[j, STAT_OWN : STAT_PAIR + 1] = spread.T[0:16, :].reshape(2, 8, tokens)
        for goes, _, copy in stat_copies(j):
            when(goes, copy.start)

    def step_forward_own(j):
        arrive_halos(0, j, True)
        forward(j, OWN)

    def step_backward_pair(j):
        arrive_halos(1, j, False)
        backward_start(j, PAIR)
        arrived(stats.at[j, 0:7], stat_sem.at[j, 0])
        backward(j, PAIR)
        for kind in (3, 2):
            give(kind, j).start()

    def step_backward_own(j):
        arrive_halos(1, j, True)
        backward_start(j, OWN)
        arrived(stats.at[j, 0:3], stat_sem.at[j, 1])
        backward(j, OWN)

    times = [(0.0, step_own_out, 0), (7.5, step_own_out, 1)]
    for i, (phase, j, a) in enumerate(pieces):
        times.append((6.15 + 0.7 * i, step_pair_in, i))
        if a == 0:
            at = 6.9 + 0.7 * i if phase == 0 else (12.6 if j == 0 else 14.0)
            times.append((at, step_far_in, i))
        times.append((8.75 + 0.7 * i + phase, step_outer_in, i))
    for j in heads:
        times.append((7.55 + 2.8 * j, step_own_halo, j))
        times.append((11.06 + 1.42 * j, step_forward_pair, j))
        times.append((11.35 + 1.8 * j, step_forward_own, j))
        times.append((15.0 + 1.5 * j, step_backward_pair, j))
        times.append((16.6 + (4.5 + 0.5 * j if j > 0 else 0.0), step_backward_own, j))
    for _, step, index in sorted(times, key=lambda entry: entry[0]):
        step(index)

    remote(results, results, send_sem.at[RESULT], result_sem, (pair, sp)).wait()

    def drain(cond, ref, i):
        when(cond, remote(ref, ref, send_sem.at[i], result_sem, (pair, sp)).wait_send)

    whole = near.at[:, :, :, PAIR, 0:tokens, :]
    drain(None, whole, TO_PAIR)
    drain(has_outer, whole, TO_FAR)
    drain(has_far, whole, TO_OUTER)
    for first, cond in ((UP, has_up), (DOWN, has_down)):
        drain(cond, near.at[:, :, :, OWN : PAIR + 1, 0:half, :], first)
        drain(cond & has_outer, near.at[:, :, :, OUTER, 0:half, :], first + 1)
        drain(cond & has_far, near.at[:, :, :, FAR, 0:half, :], first + 2)
    for n, (goes, count, _) in enumerate(stat_copies(0)):
        drain(goes, stats.at[:, 0:count], STAT + n)


def put_out(*refs):
    sources, targets, sems = refs[:4], refs[4:8], refs[8]
    copies = [pltpu.make_async_copy(sources[i], targets[i], sems.at[i]) for i in range(4)]
    for copy in copies:
        copy.start()
    for copy in copies:
        copy.wait()


def on_device(queries, key_vectors, values, grad_out, windows):
    local_shape = queries.shape
    row_count, col_count, features = local_shape[1:]
    head_count = windows.shape[1]
    head_size = features // head_count
    tokens = row_count * col_count
    mine = head_count // 2
    half = tokens // 2
    sizes = (
        head_count,
        head_size,
        row_count,
        col_count,
        lax.axis_size("tm"),
        lax.axis_size("space"),
    )
    flat = (tokens, features)
    low = jnp.bfloat16
    outs = pl.pallas_call(
        functools.partial(kernel, sizes),
        out_shape=[jax.ShapeDtypeStruct(flat, low)] * 4,
        in_specs=[pl.BlockSpec(memory_space=pltpu.HBM)] * 5,
        out_specs=[pl.BlockSpec(memory_space=pltpu.VMEM)] * 4,
        scratch_shapes=[
            pltpu.SMEM((2, head_count), jnp.int32),
            pltpu.VMEM((mine, tokens, 2 * tokens), jnp.float32),
            pltpu.VMEM((2, mine, 2, 4, 2 * tokens, head_size), low),
            pltpu.VMEM((4, mine, tokens, head_size), low),
            pltpu.VMEM((mine, 12, 8, tokens), jnp.float32),
            pltpu.VMEM((2 * tokens, 6 * tokens), jnp.float32),
            pltpu.VMEM((2 * tokens, 6 * tokens), jnp.float32),
            pltpu.VMEM((2 * tokens, 6 * tokens), low),
            pltpu.VMEM((2 * tokens, 6 * tokens), low),
            pltpu.VMEM((2, 4, half, head_size), low),
            pltpu.VMEM((4, 8, tokens), jnp.float32),
            pltpu.SemaphoreType.DMA((3,)),
            pltpu.SemaphoreType.DMA((STAT + 8,)),
            pltpu.SemaphoreType.DMA((4 * mine,)),
            pltpu.SemaphoreType.DMA((4 * mine,)),
            pltpu.SemaphoreType.DMA((2, mine)),
            pltpu.SemaphoreType.DMA((2, mine, 2)),
            pltpu.SemaphoreType.DMA((mine, 2)),
            pltpu.SemaphoreType.DMA,
        ],
        compiler_params=pltpu.CompilerParams(
            collective_id=0, has_side_effects=True, vmem_limit_bytes=55_600_000
        ),
    )(
        pltpu.with_memory_space_constraint(windows, pltpu.HBM),
        queries.reshape(flat),
        key_vectors.reshape(flat),
        values.reshape(flat),
        grad_out.reshape(flat),
    )
    outs = pl.pallas_call(
        put_out,
        out_shape=[jax.ShapeDtypeStruct(flat, low)] * 4,
        in_specs=[pl.BlockSpec(memory_space=pltpu.VMEM)] * 4,
        out_specs=[pl.BlockSpec(memory_space=pltpu.HBM)] * 4,
        scratch_shapes=[
            pltpu.SemaphoreType.DMA((4,)),
        ],
        compiler_params=pltpu.CompilerParams(vmem_limit_bytes=4_000_000),
    )(*outs)
    return tuple(out.reshape(local_shape) for out in outs)


def solution(mesh):
    spec = P("tm", "space", None, None)
    return jax.shard_map(
        on_device,
        mesh=mesh,
        in_specs=(spec, spec, spec, spec, P()),
        out_specs=(spec, spec, spec, spec),
        check_vma=False,
    )
```

```python
import functools
import math

import jax
import jax.numpy as jnp
from jax import lax
from jax.experimental import pallas as pl
from jax.experimental.pallas import tpu as pltpu
from jax.sharding import PartitionSpec as P

masked_score = -1e30
MESH = pl.DeviceIdType.MESH

OUTER, OWN, PAIR, FAR = range(4)

STAT_OWN, STAT_PAIR, STAT_FAR, STAT_OUTER = range(4)
ABOVE, BELOW = 4, 8

TO_PAIR, TO_FAR, TO_OUTER, RESULT, UP, DOWN, STAT = 0, 1, 2, 3, 4, 7, 10


def dot_nt(a, b):
    return lax.dot_general(a, b, (((1,), (1,)), ((), ())), preferred_element_type=jnp.float32)


def dot_nn(a, b):
    return lax.dot_general(a, b, (((1,), (0,)), ((), ())), preferred_element_type=jnp.float32)


def when(cond, action):
    if cond is None:
        action()
    else:
        pl.when(cond)(action)


def kernel(
    sizes,
    win_hbm,
    q_ref,
    k_ref,
    v_ref,
    g_ref,
    att_ref,
    gq_ref,
    gk_ref,
    gv_ref,
    win_ref,
    bias,
    near,
    results,
    stats,
    scores_ref,
    grad_weights_ref,
    powers_ref,
    grad_scores_ref,
    no_rows,
    no_stats,
    load_sem,
    send_sem,
    pair_sem,
    outer_sem,
    far_sem,
    halo_sem,
    stat_sem,
    result_sem,
):
    head_count, head_size, row_count, col_count, n_tm, n_space = sizes
    tokens = row_count * col_count
    half = tokens // 2
    mine = head_count // 2
    scale = 1.0 / math.sqrt(head_size)
    scale2 = scale * math.log2(math.e)
    tm, sp = lax.axis_index("tm"), lax.axis_index("space")
    side = lax.rem(tm, 2)
    pair = tm + 1 - 2 * side
    inner_to = tm + 2 - 4 * side
    outer_to = tm - 2 + 4 * side
    has_far = (inner_to >= 0) & (inner_to < n_tm)
    has_outer = (outer_to >= 0) & (outer_to < n_tm)
    has_up = sp > 0
    has_down = sp < n_space - 1
    heads = range(mine)
    pieces = [(phase, j, a) for phase in range(2) for j in heads for a in range(2)]
    ins = ((k_ref, v_ref), (q_ref, g_ref))
    outs = (att_ref, gq_ref, gk_ref, gv_ref)

    def head_cols(j, of_pair=False):
        first = (1 - side if of_pair else side) * mine + j
        return pl.ds(pl.multiple_of(first * head_size, head_size), head_size)

    barrier = pltpu.get_barrier_semaphore()

    def greet(cond, tm_to, sp_to):
        def signal():
            pl.semaphore_signal(barrier, inc=1, device_id=(tm_to, sp_to), device_id_type=MESH)

        when(cond, signal)

    greet(None, pair, sp)
    greet(has_far, inner_to, sp)
    greet(has_outer, outer_to, sp)
    greet(has_up, tm, sp - 1)
    greet(has_down, tm, sp + 1)

    def main_rows(i, slot):
        phase, j, a = pieces[i]
        return near.at[phase, j, a, slot, 0:tokens, :]

    def load(i):
        phase, j, a = pieces[i]
        return pltpu.make_async_copy(
            ins[phase][a].at[:, head_cols(j)], main_rows(i, OWN), load_sem.at[phase]
        )

    for i in range(len(pieces)):
        load(i).start()
    get_windows = pltpu.make_async_copy(win_hbm, win_ref, load_sem.at[2])
    get_windows.start()
    no_rows[...] = jnp.zeros_like(no_rows)
    no_stats[...] = jnp.zeros_like(no_stats)

    def remote(src, dst, send, recv, device):
        return pltpu.make_async_remote_copy(
            src_ref=src,
            dst_ref=dst,
            send_sem=send,
            recv_sem=recv,
            device_id=device,
            device_id_type=MESH,
        )

    def to_pair(i):
        phase, j, a = pieces[i]
        return remote(
            ins[phase][a].at[:, head_cols(j, True)],
            main_rows(i, PAIR),
            send_sem.at[TO_PAIR],
            pair_sem.at[i],
            (pair, sp),
        )

    def own_to_far(i):
        phase, j, a = pieces[i]
        return remote(
            main_rows(i, OWN),
            main_rows(i, FAR),
            send_sem.at[TO_FAR],
            far_sem.at[phase, j],
            (outer_to, sp),
        )

    def pair_to_outer(i):
        return remote(
            main_rows(i, PAIR),
            main_rows(i, OUTER),
            send_sem.at[TO_OUTER],
            outer_sem.at[i],
            (inner_to, sp),
        )

    def of_kind(slot):
        return {OUTER: 1, FAR: 2}.get(slot, 0)

    def halo_up(i, slot):
        phase, j, a = pieces[i]
        rows = near.at[phase, j, a, slot]
        return remote(
            rows.at[0:half, :],
            rows.at[tokens : tokens + half, :],
            send_sem.at[UP + of_kind(slot)],
            halo_sem.at[phase, j, of_kind(slot) % 2],
            (tm, sp - 1),
        )

    def halo_down(i, slot):
        phase, j, a = pieces[i]
        rows = near.at[phase, j, a, slot]
        return remote(
            rows.at[half:tokens, :],
            rows.at[tokens + half : 2 * tokens, :],
            send_sem.at[DOWN + of_kind(slot)],
            halo_sem.at[phase, j, of_kind(slot) % 2],
            (tm, sp + 1),
        )

    def halos(i, slot):
        when(has_up, lambda: halo_up(i, slot).start())
        when(has_down, lambda: halo_down(i, slot).start())

    expected = (
        1
        + has_far.astype(jnp.int32)
        + has_outer.astype(jnp.int32)
        + has_up.astype(jnp.int32)
        + has_down.astype(jnp.int32)
    )
    pl.semaphore_wait(barrier, expected)
    for i in range(len(pieces)):
        to_pair(i).start()
    def step_own_out(phase):
        rows = near.at[phase, :, :, OWN, 0:tokens, :]
        pltpu.make_async_copy(rows, rows, load_sem.at[phase]).wait()
        for i in range(len(pieces)):
            if pieces[i][0] == phase:
                when(has_outer, lambda: own_to_far(i).start())
                if phase == 0:
                    halos(i, OWN)

    def step_own_halo(j):
        for i in range(len(pieces)):
            if pieces[i][:2] == (1, j):
                halos(i, OWN)

    def fill(source, target, sem):
        pltpu.make_async_copy(source, target, sem).start()

    def fill_side(first_row, first_stat):
        rows = slice(first_row, first_row + half)

        def all_frames():
            for phase in range(2):
                for j in heads:
                    at = near.at[phase, j, :, :, rows, :]
                    fill(no_rows.at[:, 0:1], at.at[:, 0:1], halo_sem.at[phase, j, 1])
                    fill(no_rows.at[:, 1:4], at.at[:, 1:4], halo_sem.at[phase, j, 0])
            for j in heads:
                last = first_stat + STAT_OUTER
                fill(no_stats.at[0:3], stats.at[j, first_stat:last], stat_sem.at[j, 0])
                fill(no_stats.at[3], stats.at[j, last], stat_sem.at[j, 1])

        def one_frame(slot, stat):
            for phase in range(2):
                for j in heads:
                    sem = halo_sem.at[phase, j, of_kind(slot) % 2]
                    fill(no_rows.at[:, slot], near.at[phase, j, :, slot, rows, :], sem)
            for j in heads:
                sem = stat_sem.at[j, stat // STAT_OUTER]
                fill(no_stats.at[0], stats.at[j, first_stat + stat], sem)

        return all_frames, one_frame

    for has_side, parts in (
        (has_down, fill_side(tokens, BELOW)),
        (has_up, fill_side(tokens + half, ABOVE)),
    ):
        all_frames, one_frame = parts
        pl.when(jnp.logical_not(has_side))(all_frames)
        no_outer, no_far = jnp.logical_not(has_outer), jnp.logical_not(has_far)
        pl.when(has_side & no_outer)(lambda: one_frame(OUTER, STAT_OUTER))
        pl.when(has_side & no_far)(lambda: one_frame(FAR, STAT_FAR))

    for has_frame, slot, stat in ((has_outer, OUTER, STAT_OUTER), (has_far, FAR, STAT_FAR)):

        @pl.when(jnp.logical_not(has_frame))
        def _():
            for phase in range(2):
                for j in heads:
                    near[phase, j, :, slot, 0:tokens, :] = jnp.zeros(
                        (2, tokens, head_size), near.dtype
                    )
            for j in heads:
                fill(no_stats.at[0], stats.at[j, stat], stat_sem.at[j, stat // STAT_OUTER])

    own_id = lax.broadcasted_iota(jnp.int32, (tokens, 2 * tokens), 0)
    near_id = lax.broadcasted_iota(jnp.int32, (tokens, 2 * tokens), 1)
    own_row, own_col = own_id // col_count, own_id % col_count
    near_row, near_col = near_id // col_count, near_id % col_count
    upper = near_row >= row_count + row_count // 2
    near_row = jnp.where(upper, near_row - 2 * row_count, near_row)
    global_row = sp * row_count + near_row
    row_inside = (global_row >= 0) & (global_row < n_space * row_count)
    row_gap = jnp.where(row_inside, jnp.abs(own_row - near_row), 1 << 20)
    col_gap = jnp.abs(own_col - near_col)

    get_windows.wait()
    for j in heads:
        h = side * mine + j
        inside = (row_gap <= win_ref[0, h]) & (col_gap <= win_ref[1, h])
        bias[j] = jnp.where(inside, 0.0, masked_score)

    def window(j, frame):
        here = bias[j]
        there = here + jnp.where(has_outer if frame == OWN else has_far, 0.0, masked_score)
        order = [there, here, here] if frame == OWN else [here, here, there]
        return jnp.concatenate(order, axis=1)

    def around(phase, j, a, frame):
        return near[phase, j, a, frame - 1 : frame + 2].reshape(6 * tokens, head_size)

    def put(kind, j, frame, value):
        if frame == OWN:
            outs[kind][:, head_cols(j)] = value
        else:
            results[kind, j] = value

    def give(kind, j):
        return remote(
            results.at[kind, j],
            outs[kind].at[:, head_cols(j)],
            send_sem.at[RESULT],
            result_sem,
            (pair, sp),
        )

    def forward(j, frame):
        at = slice((frame - OWN) * tokens, (frame - OWN + 1) * tokens)
        scores_ref[at] = dot_nt(near[1, j, 0, frame, 0:tokens, :], around(0, j, 0, frame))
        grad_weights_ref[at] = dot_nt(near[1, j, 1, frame, 0:tokens, :], around(0, j, 1, frame))
        scores = scores_ref[at] * scale2 + window(j, frame)
        top = jnp.max(scores, axis=1, keepdims=True)
        powers = jnp.exp2(scores - top)
        total = jnp.sum(powers, axis=1, keepdims=True)
        share = 1.0 / total
        powers_ref[at] = powers.astype(jnp.bfloat16)
        grad_weights = grad_weights_ref[at]
        out_dot = jnp.sum(powers * grad_weights, axis=1, keepdims=True) * share
        grad_scores_ref[at] = (powers * (grad_weights - out_dot)).astype(jnp.bfloat16)
        found = (top + jnp.log2(total), out_dot)
        if frame == PAIR:
            columns[j] = found
        else:
            send_stats(j, (*found, *columns.pop(j)))
        attended = dot_nn(powers_ref[at], around(0, j, 1, frame)) * share
        put(0, j, frame, attended.astype(jnp.bfloat16))
        query_sum = dot_nn(grad_scores_ref[at], around(0, j, 0, frame)) * (share * scale)
        put(1, j, frame, query_sum.astype(jnp.bfloat16))
    row_lane = lax.broadcasted_iota(jnp.int32, (1, tokens), 1)

    def stat_row(j, r, frame):
        order = (STAT_OUTER, STAT_OWN, STAT_PAIR, STAT_FAR)
        parts = []
        for stat in order[frame - 1 : frame + 2]:
            parts.append(stats[j, stat, r : r + 1, :])
            down, up = stats[j, BELOW + stat, r : r + 1, :], stats[j, ABOVE + stat, r : r + 1, :]
            parts.append(jnp.where(row_lane < half, down, up))
        return jnp.concatenate(parts, axis=1)

    def backward_rows(frame):
        return slice((frame - OWN) * tokens, (frame - OWN + 1) * tokens)

    def backward_start(j, frame):
        at = backward_rows(frame)
        key = near[0, j, 0, frame, 0:tokens, :]
        val = near[0, j, 1, frame, 0:tokens, :]
        scores_ref[at] = dot_nt(key, around(1, j, 0, frame)) * scale2 + window(j, frame)
        grad_weights_ref[at] = dot_nt(val, around(1, j, 1, frame))

    def backward(j, frame):
        at = backward_rows(frame)
        soft = jnp.exp2(scores_ref[at] - stat_row(j, 0, frame))
        grad_scores = soft * (grad_weights_ref[at] - stat_row(j, 1, frame))
        value_sum = dot_nn(soft.astype(jnp.bfloat16), around(1, j, 1, frame))
        put(3, j, frame, value_sum.astype(jnp.bfloat16))
        key_sum = dot_nn(grad_scores.astype(jnp.bfloat16), around(1, j, 0, frame))
        put(2, j, frame, (key_sum * scale).astype(jnp.bfloat16))

    def stat_copies(j):
        block = stats.at[j]
        found = [
            (has_far, STAT_PAIR, STAT_OUTER, 1, (inner_to, sp)),
            (has_outer, STAT_OWN, STAT_FAR, 1, (outer_to, sp)),
        ]
        for at, there, goes in ((BELOW, sp - 1, has_up), (ABOVE, sp + 1, has_down)):
            found += [
                (goes, STAT_OWN, at + STAT_OWN, 2, (tm, there)),
                (goes & has_far, STAT_PAIR, at + STAT_OUTER, 1, (inner_to, there)),
                (goes & has_outer, STAT_OWN, at + STAT_FAR, 1, (outer_to, there)),
            ]
        return [
            (
                goes,
                count,
                remote(
                    block.at[src : src + count],
                    block.at[dst : dst + count],
                    send_sem.at[STAT + n],
                    stat_sem.at[j, dst % 4 // STAT_OUTER],
                    device,
                ),
            )
            for n, (goes, src, dst, count, device) in enumerate(found)
        ]

    def step_pair_in(i):
        to_pair(i).wait_recv()
        when(has_far, lambda: pair_to_outer(i).start())
        halos(i, PAIR)

    def step_far_in(i):
        phase, j, _ = pieces[i]

        @pl.when(has_far)
        def _():
            rows = near.at[phase, j, :, FAR, 0:tokens, :]
            remote(rows, rows, send_sem.at[TO_FAR], far_sem.at[phase, j], (pair, sp)).wait_recv()
            for at in (i, i + 1):
                halos(at, FAR)

    def step_outer_in(i):
        @pl.when(has_outer)
        def _():
            pair_to_outer(i).wait_recv()
            halos(i, OUTER)

    def arrived(ref, sem):
        pltpu.make_async_copy(ref, ref, sem).wait()

    def arrive_halos(phase, j, outer):
        rows = slice(tokens, 2 * tokens)
        if outer:
            arrived(near.at[phase, j, :, OUTER, rows, :], halo_sem.at[phase, j, 1])
        else:
            arrived(near.at[phase, j, :, OWN : FAR + 1, rows, :], halo_sem.at[phase, j, 0])

    columns = {}

    def step_forward_pair(j):
        arrive_halos(0, j, False)
        forward(j, PAIR)
        for kind in (0, 1):
            give(kind, j).start()

    def send_stats(j, found):
        lane = lax.broadcasted_iota(jnp.int32, (tokens, tokens), 1)
        spread = jnp.zeros((tokens, tokens), jnp.float32)
        for at, column in zip((0, 1, 8, 9), found, strict=True):
            spread = jnp.where(lane == at, column, spread)
        stats[j, STAT_OWN : STAT_PAIR + 1] = spread.T[0:16, :].reshape(2, 8, tokens)
        for goes, _, copy in stat_copies(j):
            when(goes, copy.start)

    def step_forward_own(j):
        arrive_halos(0, j, True)
        forward(j, OWN)

    def step_backward_pair(j):
        arrive_halos(1, j, False)
        backward_start(j, PAIR)
        arrived(stats.at[j, 0:7], stat_sem.at[j, 0])
        backward(j, PAIR)
        for kind in (3, 2):
            give(kind, j).start()

    def step_backward_own(j):
        arrive_halos(1, j, True)
        backward_start(j, OWN)
        arrived(stats.at[j, 0:3], stat_sem.at[j, 1])
        backward(j, OWN)

    times = [(0.0, step_own_out, 0), (7.5, step_own_out, 1)]
    for i, (phase, j, a) in enumerate(pieces):
        times.append((6.15 + 0.7 * i, step_pair_in, i))
        if a == 0:
            at = 6.9 + 0.7 * i if phase == 0 else (11.2 if j == 0 else 14.0)
            times.append((at, step_far_in, i))
        late = 1.0 if phase == 1 else (0.3 if (j, a) == (mine - 1, 1) else 0.0)
        times.append((8.75 + 0.7 * i + late, step_outer_in, i))
    for j in heads:
        times.append((7.55 + 2.8 * j, step_own_halo, j))
        times.append((11.06 + 1.42 * j, step_forward_pair, j))
        times.append((11.35 + 1.8 * j, step_forward_own, j))
        times.append((14.9 + 1.55 * j, step_backward_pair, j))
        times.append((16.6 + (4.5 + 0.5 * j if j > 0 else 0.0), step_backward_own, j))
    for _, step, index in sorted(times, key=lambda entry: entry[0]):
        step(index)

    remote(results, results, send_sem.at[RESULT], result_sem, (pair, sp)).wait()

    def drain(cond, ref, i):
        when(cond, remote(ref, ref, send_sem.at[i], result_sem, (pair, sp)).wait_send)

    whole = near.at[:, :, :, PAIR, 0:tokens, :]
    drain(None, whole, TO_PAIR)
    drain(has_outer, whole, TO_FAR)
    drain(has_far, whole, TO_OUTER)
    for first, cond in ((UP, has_up), (DOWN, has_down)):
        drain(cond, near.at[:, :, :, OWN : PAIR + 1, 0:half, :], first)
        drain(cond & has_outer, near.at[:, :, :, OUTER, 0:half, :], first + 1)
        drain(cond & has_far, near.at[:, :, :, FAR, 0:half, :], first + 2)
    for n, (goes, count, _) in enumerate(stat_copies(0)):
        drain(goes, stats.at[:, 0:count], STAT + n)


def put_out(*refs):
    sources, targets, sems = refs[:4], refs[4:8], refs[8]
    copies = [pltpu.make_async_copy(sources[i], targets[i], sems.at[i]) for i in range(4)]
    for copy in copies:
        copy.start()
    for copy in copies:
        copy.wait()


def on_device(queries, key_vectors, values, grad_out, windows):
    local_shape = queries.shape
    row_count, col_count, features = local_shape[1:]
    head_count = windows.shape[1]
    head_size = features // head_count
    tokens = row_count * col_count
    mine = head_count // 2
    half = tokens // 2
    sizes = (
        head_count,
        head_size,
        row_count,
        col_count,
        lax.axis_size("tm"),
        lax.axis_size("space"),
    )
    flat = (tokens, features)
    low = jnp.bfloat16
    outs = pl.pallas_call(
        functools.partial(kernel, sizes),
        out_shape=[jax.ShapeDtypeStruct(flat, low)] * 4,
        in_specs=[pl.BlockSpec(memory_space=pltpu.HBM)] * 5,
        out_specs=[pl.BlockSpec(memory_space=pltpu.VMEM)] * 4,
        scratch_shapes=[
            pltpu.SMEM((2, head_count), jnp.int32),
            pltpu.VMEM((mine, tokens, 2 * tokens), jnp.float32),
            pltpu.VMEM((2, mine, 2, 4, 2 * tokens, head_size), low),
            pltpu.VMEM((4, mine, tokens, head_size), low),
            pltpu.VMEM((mine, 12, 8, tokens), jnp.float32),
            pltpu.VMEM((2 * tokens, 6 * tokens), jnp.float32),
            pltpu.VMEM((2 * tokens, 6 * tokens), jnp.float32),
            pltpu.VMEM((2 * tokens, 6 * tokens), low),
            pltpu.VMEM((2 * tokens, 6 * tokens), low),
            pltpu.VMEM((2, 4, half, head_size), low),
            pltpu.VMEM((4, 8, tokens), jnp.float32),
            pltpu.SemaphoreType.DMA((3,)),
            pltpu.SemaphoreType.DMA((STAT + 8,)),
            pltpu.SemaphoreType.DMA((4 * mine,)),
            pltpu.SemaphoreType.DMA((4 * mine,)),
            pltpu.SemaphoreType.DMA((2, mine)),
            pltpu.SemaphoreType.DMA((2, mine, 2)),
            pltpu.SemaphoreType.DMA((mine, 2)),
            pltpu.SemaphoreType.DMA,
        ],
        compiler_params=pltpu.CompilerParams(
            collective_id=0, has_side_effects=True, vmem_limit_bytes=55_600_000
        ),
    )(
        pltpu.with_memory_space_constraint(windows, pltpu.HBM),
        queries.reshape(flat),
        key_vectors.reshape(flat),
        values.reshape(flat),
        grad_out.reshape(flat),
    )
    outs = pl.pallas_call(
        put_out,
        out_shape=[jax.ShapeDtypeStruct(flat, low)] * 4,
        in_specs=[pl.BlockSpec(memory_space=pltpu.VMEM)] * 4,
        out_specs=[pl.BlockSpec(memory_space=pltpu.HBM)] * 4,
        scratch_shapes=[
            pltpu.SemaphoreType.DMA((4,)),
        ],
        compiler_params=pltpu.CompilerParams(vmem_limit_bytes=4_000_000),
    )(*outs)
    return tuple(out.reshape(local_shape) for out in outs)


def solution(mesh):
    spec = P("tm", "space", None, None)
    return jax.shard_map(
        on_device,
        mesh=mesh,
        in_specs=(spec, spec, spec, spec, P()),
        out_specs=(spec, spec, spec, spec),
        check_vma=False,
    )
```

```python
import functools
import math

import jax
import jax.numpy as jnp
from jax import lax
from jax.experimental import pallas as pl
from jax.experimental.pallas import tpu as pltpu
from jax.sharding import PartitionSpec as P

masked_score = -1e30
MESH = pl.DeviceIdType.MESH

OUTER, OWN, PAIR, FAR = range(4)

STAT_OWN, STAT_PAIR, STAT_FAR, STAT_OUTER = range(4)
ABOVE, BELOW = 4, 8

TO_PAIR, TO_FAR, TO_OUTER, RESULT, UP, DOWN, STAT = 0, 1, 2, 3, 4, 7, 10


def dot_nt(a, b):
    return lax.dot_general(a, b, (((1,), (1,)), ((), ())), preferred_element_type=jnp.float32)


def dot_nn(a, b):
    return lax.dot_general(a, b, (((1,), (0,)), ((), ())), preferred_element_type=jnp.float32)


def when(cond, action):
    if cond is None:
        action()
    else:
        pl.when(cond)(action)


def kernel(
    sizes,
    win_hbm,
    q_ref,
    k_ref,
    v_ref,
    g_ref,
    att_ref,
    gq_ref,
    gk_ref,
    gv_ref,
    win_ref,
    bias,
    near,
    results,
    stats,
    scores_ref,
    grad_weights_ref,
    powers_ref,
    grad_scores_ref,
    no_rows,
    no_stats,
    load_sem,
    send_sem,
    pair_sem,
    outer_sem,
    far_sem,
    halo_sem,
    stat_sem,
    result_sem,
):
    head_count, head_size, row_count, col_count, n_tm, n_space = sizes
    tokens = row_count * col_count
    half = tokens // 2
    mine = head_count // 2
    scale = 1.0 / math.sqrt(head_size)
    scale2 = scale * math.log2(math.e)
    tm, sp = lax.axis_index("tm"), lax.axis_index("space")
    side = lax.rem(tm, 2)
    pair = tm + 1 - 2 * side
    inner_to = tm + 2 - 4 * side
    outer_to = tm - 2 + 4 * side
    has_far = (inner_to >= 0) & (inner_to < n_tm)
    has_outer = (outer_to >= 0) & (outer_to < n_tm)
    has_up = sp > 0
    has_down = sp < n_space - 1
    heads = range(mine)
    pieces = [(phase, j, a) for phase in range(2) for j in heads for a in range(2)]
    ins = ((k_ref, v_ref), (q_ref, g_ref))
    outs = (att_ref, gq_ref, gk_ref, gv_ref)

    def head_cols(j, of_pair=False):
        first = (1 - side if of_pair else side) * mine + j
        return pl.ds(pl.multiple_of(first * head_size, head_size), head_size)

    barrier = pltpu.get_barrier_semaphore()

    def greet(cond, tm_to, sp_to):
        def signal():
            pl.semaphore_signal(barrier, inc=1, device_id=(tm_to, sp_to), device_id_type=MESH)

        when(cond, signal)

    greet(None, pair, sp)
    greet(has_far, inner_to, sp)
    greet(has_outer, outer_to, sp)
    greet(has_up, tm, sp - 1)
    greet(has_down, tm, sp + 1)

    def main_rows(i, slot):
        phase, j, a = pieces[i]
        return near.at[phase, j, a, slot, 0:tokens, :]

    def load(i):
        phase, j, a = pieces[i]
        return pltpu.make_async_copy(
            ins[phase][a].at[:, head_cols(j)], main_rows(i, OWN), load_sem.at[phase]
        )

    for i in range(len(pieces)):
        load(i).start()
    get_windows = pltpu.make_async_copy(win_hbm, win_ref, load_sem.at[2])
    get_windows.start()
    no_rows[...] = jnp.zeros_like(no_rows)
    no_stats[...] = jnp.zeros_like(no_stats)

    def remote(src, dst, send, recv, device):
        return pltpu.make_async_remote_copy(
            src_ref=src,
            dst_ref=dst,
            send_sem=send,
            recv_sem=recv,
            device_id=device,
            device_id_type=MESH,
        )

    def piece_sem(i):
        phase, j, _ = pieces[i]
        return i if phase == 0 else 2 * mine + j

    def arrive_piece(i, slot, sem):
        phase, j, a = pieces[i]
        rows = near.at[phase, j, slice(a, a + 1) if phase == 0 else slice(0, 2), slot, 0:tokens, :]
        pltpu.make_async_copy(rows, rows, sem.at[piece_sem(i)]).wait()

    def group(i):
        return (i,) if pieces[i][0] == 0 else (i - 1, i)

    def to_pair(i):
        phase, j, a = pieces[i]
        return remote(
            ins[phase][a].at[:, head_cols(j, True)],
            main_rows(i, PAIR),
            send_sem.at[TO_PAIR],
            pair_sem.at[piece_sem(i)],
            (pair, sp),
        )

    def own_to_far(i):
        phase, j, a = pieces[i]
        return remote(
            main_rows(i, OWN),
            main_rows(i, FAR),
            send_sem.at[TO_FAR],
            far_sem.at[phase, j],
            (outer_to, sp),
        )

    def pair_to_outer(i):
        return remote(
            main_rows(i, PAIR),
            main_rows(i, OUTER),
            send_sem.at[TO_OUTER],
            outer_sem.at[piece_sem(i)],
            (inner_to, sp),
        )

    def of_kind(slot):
        return {OUTER: 1, FAR: 2}.get(slot, 0)

    def halo_up(i, slot):
        phase, j, a = pieces[i]
        rows = near.at[phase, j, a, slot]
        return remote(
            rows.at[0:half, :],
            rows.at[tokens : tokens + half, :],
            send_sem.at[UP + of_kind(slot)],
            halo_sem.at[phase, j, of_kind(slot) % 2],
            (tm, sp - 1),
        )

    def halo_down(i, slot):
        phase, j, a = pieces[i]
        rows = near.at[phase, j, a, slot]
        return remote(
            rows.at[half:tokens, :],
            rows.at[tokens + half : 2 * tokens, :],
            send_sem.at[DOWN + of_kind(slot)],
            halo_sem.at[phase, j, of_kind(slot) % 2],
            (tm, sp + 1),
        )

    def halos(i, slot):
        when(has_up, lambda: halo_up(i, slot).start())
        when(has_down, lambda: halo_down(i, slot).start())

    expected = (
        1
        + has_far.astype(jnp.int32)
        + has_outer.astype(jnp.int32)
        + has_up.astype(jnp.int32)
        + has_down.astype(jnp.int32)
    )
    pl.semaphore_wait(barrier, expected)
    for i in range(len(pieces)):
        to_pair(i).start()
    def step_own_out(phase):
        rows = near.at[phase, :, :, OWN, 0:tokens, :]
        pltpu.make_async_copy(rows, rows, load_sem.at[phase]).wait()
        for i in range(len(pieces)):
            if pieces[i][0] == phase:
                when(has_outer, lambda: own_to_far(i).start())
                if phase == 0:
                    halos(i, OWN)

    def step_own_halo(j):
        for i in range(len(pieces)):
            if pieces[i][:2] == (1, j):
                halos(i, OWN)

    def fill(source, target, sem):
        pltpu.make_async_copy(source, target, sem).start()

    def fill_side(first_row, first_stat):
        rows = slice(first_row, first_row + half)

        def all_frames():
            for phase in range(2):
                for j in heads:
                    at = near.at[phase, j, :, :, rows, :]
                    fill(no_rows.at[:, 0:1], at.at[:, 0:1], halo_sem.at[phase, j, 1])
                    fill(no_rows.at[:, 1:4], at.at[:, 1:4], halo_sem.at[phase, j, 0])
            for j in heads:
                last = first_stat + STAT_OUTER
                fill(no_stats.at[0:3], stats.at[j, first_stat:last], stat_sem.at[j, 0])
                fill(no_stats.at[3], stats.at[j, last], stat_sem.at[j, 1])

        def one_frame(slot, stat):
            for phase in range(2):
                for j in heads:
                    sem = halo_sem.at[phase, j, of_kind(slot) % 2]
                    fill(no_rows.at[:, slot], near.at[phase, j, :, slot, rows, :], sem)
            for j in heads:
                sem = stat_sem.at[j, stat // STAT_OUTER]
                fill(no_stats.at[0], stats.at[j, first_stat + stat], sem)

        return all_frames, one_frame

    for has_side, parts in (
        (has_down, fill_side(tokens, BELOW)),
        (has_up, fill_side(tokens + half, ABOVE)),
    ):
        all_frames, one_frame = parts
        pl.when(jnp.logical_not(has_side))(all_frames)
        no_outer, no_far = jnp.logical_not(has_outer), jnp.logical_not(has_far)
        pl.when(has_side & no_outer)(lambda: one_frame(OUTER, STAT_OUTER))
        pl.when(has_side & no_far)(lambda: one_frame(FAR, STAT_FAR))

    for has_frame, slot, stat in ((has_outer, OUTER, STAT_OUTER), (has_far, FAR, STAT_FAR)):

        @pl.when(jnp.logical_not(has_frame))
        def _():
            for phase in range(2):
                for j in heads:
                    near[phase, j, :, slot, 0:tokens, :] = jnp.zeros(
                        (2, tokens, head_size), near.dtype
                    )
            for j in heads:
                fill(no_stats.at[0], stats.at[j, stat], stat_sem.at[j, stat // STAT_OUTER])

    own_id = lax.broadcasted_iota(jnp.int32, (tokens, 2 * tokens), 0)
    near_id = lax.broadcasted_iota(jnp.int32, (tokens, 2 * tokens), 1)
    own_row, own_col = own_id // col_count, own_id % col_count
    near_row, near_col = near_id // col_count, near_id % col_count
    upper = near_row >= row_count + row_count // 2
    near_row = jnp.where(upper, near_row - 2 * row_count, near_row)
    global_row = sp * row_count + near_row
    row_inside = (global_row >= 0) & (global_row < n_space * row_count)
    row_gap = jnp.where(row_inside, jnp.abs(own_row - near_row), 1 << 20)
    col_gap = jnp.abs(own_col - near_col)

    get_windows.wait()
    for j in heads:
        h = side * mine + j
        inside = (row_gap <= win_ref[0, h]) & (col_gap <= win_ref[1, h])
        bias[j] = jnp.where(inside, 0.0, masked_score)

    def window(j, frame):
        here = bias[j]
        there = here + jnp.where(has_outer if frame == OWN else has_far, 0.0, masked_score)
        order = [there, here, here] if frame == OWN else [here, here, there]
        return jnp.concatenate(order, axis=1)

    def around(phase, j, a, frame):
        return near[phase, j, a, frame - 1 : frame + 2].reshape(6 * tokens, head_size)

    def put(kind, j, frame, value):
        if frame == OWN:
            outs[kind][:, head_cols(j)] = value
        else:
            results[kind, j] = value

    def give(kind, j):
        return remote(
            results.at[kind, j],
            outs[kind].at[:, head_cols(j)],
            send_sem.at[RESULT],
            result_sem,
            (pair, sp),
        )

    def forward(j, frame):
        at = slice((frame - OWN) * tokens, (frame - OWN + 1) * tokens)
        scores_ref[at] = dot_nt(near[1, j, 0, frame, 0:tokens, :], around(0, j, 0, frame))
        grad_weights_ref[at] = dot_nt(near[1, j, 1, frame, 0:tokens, :], around(0, j, 1, frame))
        scores = scores_ref[at] * scale2 + window(j, frame)
        top = jnp.max(scores, axis=1, keepdims=True)
        powers = jnp.exp2(scores - top)
        total = jnp.sum(powers, axis=1, keepdims=True)
        share = 1.0 / total
        powers_ref[at] = powers.astype(jnp.bfloat16)
        grad_weights = grad_weights_ref[at]
        out_dot = jnp.sum(powers * grad_weights, axis=1, keepdims=True) * share
        grad_scores_ref[at] = (powers * (grad_weights - out_dot)).astype(jnp.bfloat16)
        found = (top + jnp.log2(total), out_dot)
        if frame == PAIR:
            columns[j] = found
        else:
            send_stats(j, (*found, *columns.pop(j)))
        attended = dot_nn(powers_ref[at], around(0, j, 1, frame)) * share
        put(0, j, frame, attended.astype(jnp.bfloat16))
        query_sum = dot_nn(grad_scores_ref[at], around(0, j, 0, frame)) * (share * scale)
        put(1, j, frame, query_sum.astype(jnp.bfloat16))
    row_lane = lax.broadcasted_iota(jnp.int32, (1, tokens), 1)

    def stat_row(j, r, frame):
        order = (STAT_OUTER, STAT_OWN, STAT_PAIR, STAT_FAR)
        parts = []
        for stat in order[frame - 1 : frame + 2]:
            parts.append(stats[j, stat, r : r + 1, :])
            down, up = stats[j, BELOW + stat, r : r + 1, :], stats[j, ABOVE + stat, r : r + 1, :]
            parts.append(jnp.where(row_lane < half, down, up))
        return jnp.concatenate(parts, axis=1)

    def backward_rows(frame):
        return slice((frame - OWN) * tokens, (frame - OWN + 1) * tokens)

    def backward_start(j, frame):
        at = backward_rows(frame)
        key = near[0, j, 0, frame, 0:tokens, :]
        val = near[0, j, 1, frame, 0:tokens, :]
        scores_ref[at] = dot_nt(key, around(1, j, 0, frame)) * scale2 + window(j, frame)
        grad_weights_ref[at] = dot_nt(val, around(1, j, 1, frame))

    def backward(j, frame):
        at = backward_rows(frame)
        soft = jnp.exp2(scores_ref[at] - stat_row(j, 0, frame))
        grad_scores = soft * (grad_weights_ref[at] - stat_row(j, 1, frame))
        value_sum = dot_nn(soft.astype(jnp.bfloat16), around(1, j, 1, frame))
        put(3, j, frame, value_sum.astype(jnp.bfloat16))
        key_sum = dot_nn(grad_scores.astype(jnp.bfloat16), around(1, j, 0, frame))
        put(2, j, frame, (key_sum * scale).astype(jnp.bfloat16))

    def stat_copies(j):
        block = stats.at[j]
        found = [
            (has_far, STAT_PAIR, STAT_OUTER, 1, (inner_to, sp)),
            (has_outer, STAT_OWN, STAT_FAR, 1, (outer_to, sp)),
        ]
        for at, there, goes in ((BELOW, sp - 1, has_up), (ABOVE, sp + 1, has_down)):
            found += [
                (goes, STAT_OWN, at + STAT_OWN, 2, (tm, there)),
                (goes & has_far, STAT_PAIR, at + STAT_OUTER, 1, (inner_to, there)),
                (goes & has_outer, STAT_OWN, at + STAT_FAR, 1, (outer_to, there)),
            ]
        return [
            (
                goes,
                count,
                remote(
                    block.at[src : src + count],
                    block.at[dst : dst + count],
                    send_sem.at[STAT + n],
                    stat_sem.at[j, dst % 4 // STAT_OUTER],
                    device,
                ),
            )
            for n, (goes, src, dst, count, device) in enumerate(found)
        ]

    def step_pair_in(i):
        arrive_piece(i, PAIR, pair_sem)
        for at in group(i):
            when(has_far, lambda: pair_to_outer(at).start())
            halos(at, PAIR)

    def step_far_in(i):
        phase, j, _ = pieces[i]

        @pl.when(has_far)
        def _():
            rows = near.at[phase, j, :, FAR, 0:tokens, :]
            remote(rows, rows, send_sem.at[TO_FAR], far_sem.at[phase, j], (pair, sp)).wait_recv()
            for at in (i, i + 1):
                halos(at, FAR)

    def step_outer_in(i):
        @pl.when(has_outer)
        def _():
            arrive_piece(i, OUTER, outer_sem)
            for at in group(i):
                halos(at, OUTER)

    def arrived(ref, sem):
        pltpu.make_async_copy(ref, ref, sem).wait()

    def arrive_halos(phase, j, outer):
        rows = slice(tokens, 2 * tokens)
        if outer:
            arrived(near.at[phase, j, :, OUTER, rows, :], halo_sem.at[phase, j, 1])
        else:
            arrived(near.at[phase, j, :, OWN : FAR + 1, rows, :], halo_sem.at[phase, j, 0])

    columns = {}

    def step_forward_pair(j):
        arrive_halos(0, j, False)
        forward(j, PAIR)
        for kind in (0, 1):
            give(kind, j).start()

    def send_stats(j, found):
        lane = lax.broadcasted_iota(jnp.int32, (tokens, tokens), 1)
        spread = jnp.zeros((tokens, tokens), jnp.float32)
        for at, column in zip((0, 1, 8, 9), found, strict=True):
            spread = jnp.where(lane == at, column, spread)
        stats[j, STAT_OWN : STAT_PAIR + 1] = spread.T[0:16, :].reshape(2, 8, tokens)
        for goes, _, copy in stat_copies(j):
            when(goes, copy.start)

    def step_forward_own(j):
        arrive_halos(0, j, True)
        forward(j, OWN)

    def step_backward_pair(j):
        arrive_halos(1, j, False)
        backward_start(j, PAIR)
        arrived(stats.at[j, 0:7], stat_sem.at[j, 0])
        backward(j, PAIR)
        for kind in (3, 2):
            give(kind, j).start()

    def step_backward_own(j):
        arrive_halos(1, j, True)
        backward_start(j, OWN)
        arrived(stats.at[j, 0:3], stat_sem.at[j, 1])
        backward(j, OWN)

    times = [(0.0, step_own_out, 0), (7.5, step_own_out, 1)]
    for i, (phase, j, a) in enumerate(pieces):
        alone = phase == 0 or a == 1
        if alone:
            times.append((6.15 + 0.7 * i, step_pair_in, i))
        if a == 0:
            at = 6.9 + 0.7 * i if phase == 0 else (11.2 if j == 0 else 14.0)
            times.append((at, step_far_in, i))
        late = 1.0 if phase == 1 else (0.95 - 0.65 * a if j == mine - 1 else 0.0)
        if alone:
            times.append((8.75 + 0.7 * i + late, step_outer_in, i))
    for j in heads:
        times.append((7.55 + 2.8 * j, step_own_halo, j))
        times.append((11.06 + 1.42 * j, step_forward_pair, j))
        times.append((11.35 + 1.8 * j, step_forward_own, j))
        times.append((14.9 + 1.55 * j, step_backward_pair, j))
        times.append((16.6 + (4.5 + 0.5 * j if j > 0 else 0.0), step_backward_own, j))
    for _, step, index in sorted(times, key=lambda entry: entry[0]):
        step(index)

    remote(results, results, send_sem.at[RESULT], result_sem, (pair, sp)).wait()

    def drain(cond, ref, i):
        when(cond, remote(ref, ref, send_sem.at[i], result_sem, (pair, sp)).wait_send)

    whole = near.at[:, :, :, PAIR, 0:tokens, :]
    drain(None, whole, TO_PAIR)
    drain(has_outer, whole, TO_FAR)
    drain(has_far, whole, TO_OUTER)
    for first, cond in ((UP, has_up), (DOWN, has_down)):
        drain(cond, near.at[:, :, :, OWN : PAIR + 1, 0:half, :], first)
        drain(cond & has_outer, near.at[:, :, :, OUTER, 0:half, :], first + 1)
        drain(cond & has_far, near.at[:, :, :, FAR, 0:half, :], first + 2)
    for n, (goes, count, _) in enumerate(stat_copies(0)):
        drain(goes, stats.at[:, 0:count], STAT + n)


def put_out(*refs):
    sources, targets, sems = refs[:4], refs[4:8], refs[8]
    copies = [pltpu.make_async_copy(sources[i], targets[i], sems.at[i]) for i in range(4)]
    for copy in copies:
        copy.start()
    for copy in copies:
        copy.wait()


def on_device(queries, key_vectors, values, grad_out, windows):
    local_shape = queries.shape
    row_count, col_count, features = local_shape[1:]
    head_count = windows.shape[1]
    head_size = features // head_count
    tokens = row_count * col_count
    mine = head_count // 2
    half = tokens // 2
    sizes = (
        head_count,
        head_size,
        row_count,
        col_count,
        lax.axis_size("tm"),
        lax.axis_size("space"),
    )
    flat = (tokens, features)
    low = jnp.bfloat16
    outs = pl.pallas_call(
        functools.partial(kernel, sizes),
        out_shape=[jax.ShapeDtypeStruct(flat, low)] * 4,
        in_specs=[pl.BlockSpec(memory_space=pltpu.HBM)] * 5,
        out_specs=[pl.BlockSpec(memory_space=pltpu.VMEM)] * 4,
        scratch_shapes=[
            pltpu.SMEM((2, head_count), jnp.int32),
            pltpu.VMEM((mine, tokens, 2 * tokens), jnp.float32),
            pltpu.VMEM((2, mine, 2, 4, 2 * tokens, head_size), low),
            pltpu.VMEM((4, mine, tokens, head_size), low),
            pltpu.VMEM((mine, 12, 8, tokens), jnp.float32),
            pltpu.VMEM((2 * tokens, 6 * tokens), jnp.float32),
            pltpu.VMEM((2 * tokens, 6 * tokens), jnp.float32),
            pltpu.VMEM((2 * tokens, 6 * tokens), low),
            pltpu.VMEM((2 * tokens, 6 * tokens), low),
            pltpu.VMEM((2, 4, half, head_size), low),
            pltpu.VMEM((4, 8, tokens), jnp.float32),
            pltpu.SemaphoreType.DMA((3,)),
            pltpu.SemaphoreType.DMA((STAT + 8,)),
            pltpu.SemaphoreType.DMA((3 * mine,)),
            pltpu.SemaphoreType.DMA((3 * mine,)),
            pltpu.SemaphoreType.DMA((2, mine)),
            pltpu.SemaphoreType.DMA((2, mine, 2)),
            pltpu.SemaphoreType.DMA((mine, 2)),
            pltpu.SemaphoreType.DMA,
        ],
        compiler_params=pltpu.CompilerParams(
            collective_id=0, has_side_effects=True, vmem_limit_bytes=55_600_000
        ),
    )(
        pltpu.with_memory_space_constraint(windows, pltpu.HBM),
        queries.reshape(flat),
        key_vectors.reshape(flat),
        values.reshape(flat),
        grad_out.reshape(flat),
    )
    outs = pl.pallas_call(
        put_out,
        out_shape=[jax.ShapeDtypeStruct(flat, low)] * 4,
        in_specs=[pl.BlockSpec(memory_space=pltpu.VMEM)] * 4,
        out_specs=[pl.BlockSpec(memory_space=pltpu.HBM)] * 4,
        scratch_shapes=[
            pltpu.SemaphoreType.DMA((4,)),
        ],
        compiler_params=pltpu.CompilerParams(vmem_limit_bytes=4_000_000),
    )(*outs)
    return tuple(out.reshape(local_shape) for out in outs)


def solution(mesh):
    spec = P("tm", "space", None, None)
    return jax.shard_map(
        on_device,
        mesh=mesh,
        in_specs=(spec, spec, spec, spec, P()),
        out_specs=(spec, spec, spec, spec),
        check_vma=False,
    )
```

```python
import functools
import math

import jax
import jax.numpy as jnp
from jax import lax
from jax.experimental import pallas as pl
from jax.experimental.pallas import tpu as pltpu
from jax.sharding import PartitionSpec as P

masked_score = -1e30
MESH = pl.DeviceIdType.MESH

OUTER, OWN, PAIR, FAR = range(4)

STAT_OWN, STAT_PAIR, STAT_FAR, STAT_OUTER = range(4)
ABOVE, BELOW = 4, 8

TO_PAIR, TO_FAR, TO_OUTER, RESULT, UP, DOWN, STAT = 0, 1, 2, 3, 4, 7, 10


def dot_nt(a, b):
    return lax.dot_general(a, b, (((1,), (1,)), ((), ())), preferred_element_type=jnp.float32)


def dot_nn(a, b):
    return lax.dot_general(a, b, (((1,), (0,)), ((), ())), preferred_element_type=jnp.float32)


def when(cond, action):
    if cond is None:
        action()
    else:
        pl.when(cond)(action)


def kernel(
    sizes,
    win_hbm,
    q_ref,
    k_ref,
    v_ref,
    g_ref,
    att_ref,
    gq_ref,
    gk_ref,
    gv_ref,
    win_ref,
    bias,
    near,
    results,
    stats,
    scores_ref,
    grad_weights_ref,
    powers_ref,
    grad_scores_ref,
    no_rows,
    no_stats,
    load_sem,
    send_sem,
    pair_sem,
    outer_sem,
    far_sem,
    halo_sem,
    stat_sem,
    result_sem,
):
    head_count, head_size, row_count, col_count, n_tm, n_space = sizes
    tokens = row_count * col_count
    half = tokens // 2
    mine = head_count // 2
    scale = 1.0 / math.sqrt(head_size)
    scale2 = scale * math.log2(math.e)
    tm, sp = lax.axis_index("tm"), lax.axis_index("space")
    side = lax.rem(tm, 2)
    pair = tm + 1 - 2 * side
    inner_to = tm + 2 - 4 * side
    outer_to = tm - 2 + 4 * side
    has_far = (inner_to >= 0) & (inner_to < n_tm)
    has_outer = (outer_to >= 0) & (outer_to < n_tm)
    has_up = sp > 0
    has_down = sp < n_space - 1
    heads = range(mine)
    pieces = [(phase, j, a) for phase in range(2) for j in heads for a in range(2)]
    ins = ((k_ref, v_ref), (q_ref, g_ref))
    outs = (att_ref, gq_ref, gk_ref, gv_ref)

    def head_cols(j, of_pair=False):
        first = (1 - side if of_pair else side) * mine + j
        return pl.ds(pl.multiple_of(first * head_size, head_size), head_size)

    barrier = pltpu.get_barrier_semaphore()

    def greet(cond, tm_to, sp_to):
        def signal():
            pl.semaphore_signal(barrier, inc=1, device_id=(tm_to, sp_to), device_id_type=MESH)

        when(cond, signal)

    greet(None, pair, sp)
    greet(has_far, inner_to, sp)
    greet(has_outer, outer_to, sp)
    greet(has_up, tm, sp - 1)
    greet(has_down, tm, sp + 1)

    def main_rows(i, slot):
        phase, j, a = pieces[i]
        return near.at[phase, j, a, slot, 0:tokens, :]

    def load(i):
        phase, j, a = pieces[i]
        return pltpu.make_async_copy(
            ins[phase][a].at[:, head_cols(j)], main_rows(i, OWN), load_sem.at[phase]
        )

    for i in range(len(pieces)):
        load(i).start()
    get_windows = pltpu.make_async_copy(win_hbm, win_ref, load_sem.at[2])
    get_windows.start()
    no_rows[...] = jnp.zeros_like(no_rows)
    no_stats[...] = jnp.zeros_like(no_stats)

    def remote(src, dst, send, recv, device):
        return pltpu.make_async_remote_copy(
            src_ref=src,
            dst_ref=dst,
            send_sem=send,
            recv_sem=recv,
            device_id=device,
            device_id_type=MESH,
        )

    def to_pair(i):
        phase, j, a = pieces[i]
        return remote(
            ins[phase][a].at[:, head_cols(j, True)],
            main_rows(i, PAIR),
            send_sem.at[TO_PAIR],
            pair_sem.at[i],
            (pair, sp),
        )

    def own_to_far(i):
        phase, j, a = pieces[i]
        return remote(
            main_rows(i, OWN),
            main_rows(i, FAR),
            send_sem.at[TO_FAR],
            far_sem.at[phase, j],
            (outer_to, sp),
        )

    def pair_to_outer(i):
        return remote(
            main_rows(i, PAIR),
            main_rows(i, OUTER),
            send_sem.at[TO_OUTER],
            outer_sem.at[i],
            (inner_to, sp),
        )

    def of_kind(slot):
        return {OUTER: 1, FAR: 2}.get(slot, 0)

    def halo_up(i, slot):
        phase, j, a = pieces[i]
        rows = near.at[phase, j, a, slot]
        return remote(
            rows.at[0:half, :],
            rows.at[tokens : tokens + half, :],
            send_sem.at[UP + of_kind(slot)],
            halo_sem.at[phase, j, of_kind(slot) % 2],
            (tm, sp - 1),
        )

    def halo_down(i, slot):
        phase, j, a = pieces[i]
        rows = near.at[phase, j, a, slot]
        return remote(
            rows.at[half:tokens, :],
            rows.at[tokens + half : 2 * tokens, :],
            send_sem.at[DOWN + of_kind(slot)],
            halo_sem.at[phase, j, of_kind(slot) % 2],
            (tm, sp + 1),
        )

    def halos(i, slot):
        when(has_up, lambda: halo_up(i, slot).start())
        when(has_down, lambda: halo_down(i, slot).start())

    expected = (
        1
        + has_far.astype(jnp.int32)
        + has_outer.astype(jnp.int32)
        + has_up.astype(jnp.int32)
        + has_down.astype(jnp.int32)
    )
    pl.semaphore_wait(barrier, expected)
    for i in range(len(pieces)):
        to_pair(i).start()
    def step_own_out(phase):
        rows = near.at[phase, :, :, OWN, 0:tokens, :]
        pltpu.make_async_copy(rows, rows, load_sem.at[phase]).wait()
        for i in range(len(pieces)):
            if pieces[i][0] == phase:
                when(has_outer, lambda: own_to_far(i).start())
                if phase == 0:
                    halos(i, OWN)

    def step_own_halo(j):
        for i in range(len(pieces)):
            if pieces[i][:2] == (1, j):
                halos(i, OWN)

    def fill(source, target, sem):
        pltpu.make_async_copy(source, target, sem).start()

    def fill_side(first_row, first_stat):
        rows = slice(first_row, first_row + half)

        def all_frames():
            for phase in range(2):
                for j in heads:
                    at = near.at[phase, j, :, :, rows, :]
                    fill(no_rows.at[:, 0:1], at.at[:, 0:1], halo_sem.at[phase, j, 1])
                    fill(no_rows.at[:, 1:4], at.at[:, 1:4], halo_sem.at[phase, j, 0])
            for j in heads:
                last = first_stat + STAT_OUTER
                fill(no_stats.at[0:3], stats.at[j, first_stat:last], stat_sem.at[j, 0])
                fill(no_stats.at[3], stats.at[j, last], stat_sem.at[j, 1])

        def one_frame(slot, stat):
            for phase in range(2):
                for j in heads:
                    sem = halo_sem.at[phase, j, of_kind(slot) % 2]
                    fill(no_rows.at[:, slot], near.at[phase, j, :, slot, rows, :], sem)
            for j in heads:
                sem = stat_sem.at[j, stat // STAT_OUTER]
                fill(no_stats.at[0], stats.at[j, first_stat + stat], sem)

        return all_frames, one_frame

    for has_side, parts in (
        (has_down, fill_side(tokens, BELOW)),
        (has_up, fill_side(tokens + half, ABOVE)),
    ):
        all_frames, one_frame = parts
        pl.when(jnp.logical_not(has_side))(all_frames)
        no_outer, no_far = jnp.logical_not(has_outer), jnp.logical_not(has_far)
        pl.when(has_side & no_outer)(lambda: one_frame(OUTER, STAT_OUTER))
        pl.when(has_side & no_far)(lambda: one_frame(FAR, STAT_FAR))

    for has_frame, slot, stat in ((has_outer, OUTER, STAT_OUTER), (has_far, FAR, STAT_FAR)):

        @pl.when(jnp.logical_not(has_frame))
        def _():
            for phase in range(2):
                for j in heads:
                    near[phase, j, :, slot, 0:tokens, :] = jnp.zeros(
                        (2, tokens, head_size), near.dtype
                    )
            for j in heads:
                fill(no_stats.at[0], stats.at[j, stat], stat_sem.at[j, stat // STAT_OUTER])

    own_id = lax.broadcasted_iota(jnp.int32, (tokens, 2 * tokens), 0)
    near_id = lax.broadcasted_iota(jnp.int32, (tokens, 2 * tokens), 1)
    own_row, own_col = own_id // col_count, own_id % col_count
    near_row, near_col = near_id // col_count, near_id % col_count
    upper = near_row >= row_count + row_count // 2
    near_row = jnp.where(upper, near_row - 2 * row_count, near_row)
    global_row = sp * row_count + near_row
    row_inside = (global_row >= 0) & (global_row < n_space * row_count)
    row_gap = jnp.where(row_inside, jnp.abs(own_row - near_row), 1 << 20)
    col_gap = jnp.abs(own_col - near_col)

    get_windows.wait()
    for j in heads:
        h = side * mine + j
        inside = (row_gap <= win_ref[0, h]) & (col_gap <= win_ref[1, h])
        bias[j] = jnp.where(inside, 0.0, masked_score)

    def window(j, frame):
        here = bias[j]
        there = here + jnp.where(has_outer if frame == OWN else has_far, 0.0, masked_score)
        order = [there, here, here] if frame == OWN else [here, here, there]
        return jnp.concatenate(order, axis=1)

    def around(phase, j, a, frame):
        return near[phase, j, a, frame - 1 : frame + 2].reshape(6 * tokens, head_size)

    def put(kind, j, frame, value):
        if frame == OWN:
            outs[kind][:, head_cols(j)] = value
        else:
            results[kind, j] = value

    def give(kind, j):
        return remote(
            results.at[kind, j],
            outs[kind].at[:, head_cols(j)],
            send_sem.at[RESULT],
            result_sem,
            (pair, sp),
        )

    def score(j, frame):
        at = slice((frame - OWN) * tokens, (frame - OWN + 1) * tokens)
        scores_ref[at] = dot_nt(near[1, j, 0, frame, 0:tokens, :], around(0, j, 0, frame))

    def forward(j, frame):
        at = slice((frame - OWN) * tokens, (frame - OWN + 1) * tokens)
        if frame == OWN:
            score(j, frame)
        grad_weights_ref[at] = dot_nt(near[1, j, 1, frame, 0:tokens, :], around(0, j, 1, frame))
        scores = scores_ref[at] * scale2 + window(j, frame)
        top = jnp.max(scores, axis=1, keepdims=True)
        powers = jnp.exp2(scores - top)
        total = jnp.sum(powers, axis=1, keepdims=True)
        share = 1.0 / total
        powers_ref[at] = powers.astype(jnp.bfloat16)
        grad_weights = grad_weights_ref[at]
        out_dot = jnp.sum(powers * grad_weights, axis=1, keepdims=True) * share
        grad_scores_ref[at] = (powers * (grad_weights - out_dot)).astype(jnp.bfloat16)
        found = (top + jnp.log2(total), out_dot)
        if frame == PAIR:
            columns[j] = found
        else:
            send_stats(j, (*found, *columns.pop(j)))
        attended = dot_nn(powers_ref[at], around(0, j, 1, frame)) * share
        put(0, j, frame, attended.astype(jnp.bfloat16))
        query_sum = dot_nn(grad_scores_ref[at], around(0, j, 0, frame)) * (share * scale)
        put(1, j, frame, query_sum.astype(jnp.bfloat16))
    row_lane = lax.broadcasted_iota(jnp.int32, (1, tokens), 1)

    def stat_row(j, r, frame):
        order = (STAT_OUTER, STAT_OWN, STAT_PAIR, STAT_FAR)
        parts = []
        for stat in order[frame - 1 : frame + 2]:
            parts.append(stats[j, stat, r : r + 1, :])
            down, up = stats[j, BELOW + stat, r : r + 1, :], stats[j, ABOVE + stat, r : r + 1, :]
            parts.append(jnp.where(row_lane < half, down, up))
        return jnp.concatenate(parts, axis=1)

    def backward_rows(frame):
        return slice((frame - OWN) * tokens, (frame - OWN + 1) * tokens)

    def backward_start(j, frame):
        at = backward_rows(frame)
        key = near[0, j, 0, frame, 0:tokens, :]
        val = near[0, j, 1, frame, 0:tokens, :]
        scores_ref[at] = dot_nt(key, around(1, j, 0, frame)) * scale2 + window(j, frame)
        grad_weights_ref[at] = dot_nt(val, around(1, j, 1, frame))

    def backward(j, frame):
        at = backward_rows(frame)
        soft = jnp.exp2(scores_ref[at] - stat_row(j, 0, frame))
        grad_scores = soft * (grad_weights_ref[at] - stat_row(j, 1, frame))
        value_sum = dot_nn(soft.astype(jnp.bfloat16), around(1, j, 1, frame))
        put(3, j, frame, value_sum.astype(jnp.bfloat16))
        key_sum = dot_nn(grad_scores.astype(jnp.bfloat16), around(1, j, 0, frame))
        put(2, j, frame, (key_sum * scale).astype(jnp.bfloat16))

    def stat_copies(j):
        block = stats.at[j]
        found = [
            (has_far, STAT_PAIR, STAT_OUTER, 1, (inner_to, sp)),
            (has_outer, STAT_OWN, STAT_FAR, 1, (outer_to, sp)),
        ]
        for at, there, goes in ((BELOW, sp - 1, has_up), (ABOVE, sp + 1, has_down)):
            found += [
                (goes, STAT_OWN, at + STAT_OWN, 2, (tm, there)),
                (goes & has_far, STAT_PAIR, at + STAT_OUTER, 1, (inner_to, there)),
                (goes & has_outer, STAT_OWN, at + STAT_FAR, 1, (outer_to, there)),
            ]
        return [
            (
                goes,
                count,
                remote(
                    block.at[src : src + count],
                    block.at[dst : dst + count],
                    send_sem.at[STAT + n],
                    stat_sem.at[j, dst % 4 // STAT_OUTER],
                    device,
                ),
            )
            for n, (goes, src, dst, count, device) in enumerate(found)
        ]

    def step_pair_in(i):
        to_pair(i).wait_recv()
        when(has_far, lambda: pair_to_outer(i).start())
        halos(i, PAIR)

    def step_far_in(i):
        phase, j, _ = pieces[i]

        @pl.when(has_far)
        def _():
            rows = near.at[phase, j, :, FAR, 0:tokens, :]
            remote(rows, rows, send_sem.at[TO_FAR], far_sem.at[phase, j], (pair, sp)).wait_recv()
            for at in (i, i + 1):
                halos(at, FAR)

    def step_outer_in(i):
        @pl.when(has_outer)
        def _():
            pair_to_outer(i).wait_recv()
            halos(i, OUTER)

    def arrived(ref, sem):
        pltpu.make_async_copy(ref, ref, sem).wait()

    def arrive_halos(phase, j, outer):
        rows = slice(tokens, 2 * tokens)
        if outer:
            arrived(near.at[phase, j, :, OUTER, rows, :], halo_sem.at[phase, j, 1])
        else:
            arrived(near.at[phase, j, :, OWN : FAR + 1, rows, :], halo_sem.at[phase, j, 0])

    columns = {}

    def step_score_pair(j):
        arrive_halos(0, j, False)
        score(j, PAIR)

    def step_forward_pair(j):
        forward(j, PAIR)
        for kind in (0, 1):
            give(kind, j).start()

    def send_stats(j, found):
        lane = lax.broadcasted_iota(jnp.int32, (tokens, tokens), 1)
        spread = jnp.zeros((tokens, tokens), jnp.float32)
        for at, column in zip((0, 1, 8, 9), found, strict=True):
            spread = jnp.where(lane == at, column, spread)
        stats[j, STAT_OWN : STAT_PAIR + 1] = spread.T[0:16, :].reshape(2, 8, tokens)
        for goes, _, copy in stat_copies(j):
            when(goes, copy.start)

    def step_forward_own(j):
        arrive_halos(0, j, True)
        forward(j, OWN)

    def step_backward_pair(j):
        arrive_halos(1, j, False)
        backward_start(j, PAIR)
        arrived(stats.at[j, 0:7], stat_sem.at[j, 0])
        backward(j, PAIR)
        for kind in (3, 2):
            give(kind, j).start()

    def step_backward_own(j):
        arrive_halos(1, j, True)
        backward_start(j, OWN)
        arrived(stats.at[j, 0:3], stat_sem.at[j, 1])
        backward(j, OWN)

    times = [(0.0, step_own_out, 0), (7.5, step_own_out, 1)]
    for i, (phase, j, a) in enumerate(pieces):
        times.append((6.15 + 0.7 * i, step_pair_in, i))
        if a == 0:
            at = 6.9 + 0.7 * i if phase == 0 else (11.2 if j == 0 else 14.0)
            times.append((at, step_far_in, i))
        late = 1.0 if phase == 1 else (0.3 if (j, a) == (mine - 1, 1) else 0.0)
        times.append((8.75 + 0.7 * i + late, step_outer_in, i))
    for j in heads:
        times.append((7.55 + 2.8 * j, step_own_halo, j))
        times.append((10.36 + 1.4 * j, step_score_pair, j))
        times.append((11.06 + 1.42 * j, step_forward_pair, j))
        times.append((11.35 + 1.8 * j, step_forward_own, j))
        times.append((14.9 + 1.55 * j, step_backward_pair, j))
        times.append((16.6 + (4.5 + 0.5 * j if j > 0 else 0.0), step_backward_own, j))
    for _, step, index in sorted(times, key=lambda entry: entry[0]):
        step(index)

    remote(results, results, send_sem.at[RESULT], result_sem, (pair, sp)).wait()

    def drain(cond, ref, i):
        when(cond, remote(ref, ref, send_sem.at[i], result_sem, (pair, sp)).wait_send)

    whole = near.at[:, :, :, PAIR, 0:tokens, :]
    drain(None, whole, TO_PAIR)
    drain(has_outer, whole, TO_FAR)
    drain(has_far, whole, TO_OUTER)
    for first, cond in ((UP, has_up), (DOWN, has_down)):
        drain(cond, near.at[:, :, :, OWN : PAIR + 1, 0:half, :], first)
        drain(cond & has_outer, near.at[:, :, :, OUTER, 0:half, :], first + 1)
        drain(cond & has_far, near.at[:, :, :, FAR, 0:half, :], first + 2)
    for n, (goes, count, _) in enumerate(stat_copies(0)):
        drain(goes, stats.at[:, 0:count], STAT + n)


def put_out(*refs):
    sources, targets, sems = refs[:4], refs[4:8], refs[8]
    copies = [pltpu.make_async_copy(sources[i], targets[i], sems.at[i]) for i in range(4)]
    for copy in copies:
        copy.start()
    for copy in copies:
        copy.wait()


def on_device(queries, key_vectors, values, grad_out, windows):
    local_shape = queries.shape
    row_count, col_count, features = local_shape[1:]
    head_count = windows.shape[1]
    head_size = features // head_count
    tokens = row_count * col_count
    mine = head_count // 2
    half = tokens // 2
    sizes = (
        head_count,
        head_size,
        row_count,
        col_count,
        lax.axis_size("tm"),
        lax.axis_size("space"),
    )
    flat = (tokens, features)
    low = jnp.bfloat16
    outs = pl.pallas_call(
        functools.partial(kernel, sizes),
        out_shape=[jax.ShapeDtypeStruct(flat, low)] * 4,
        in_specs=[pl.BlockSpec(memory_space=pltpu.HBM)] * 5,
        out_specs=[pl.BlockSpec(memory_space=pltpu.VMEM)] * 4,
        scratch_shapes=[
            pltpu.SMEM((2, head_count), jnp.int32),
            pltpu.VMEM((mine, tokens, 2 * tokens), jnp.float32),
            pltpu.VMEM((2, mine, 2, 4, 2 * tokens, head_size), low),
            pltpu.VMEM((4, mine, tokens, head_size), low),
            pltpu.VMEM((mine, 12, 8, tokens), jnp.float32),
            pltpu.VMEM((2 * tokens, 6 * tokens), jnp.float32),
            pltpu.VMEM((2 * tokens, 6 * tokens), jnp.float32),
            pltpu.VMEM((2 * tokens, 6 * tokens), low),
            pltpu.VMEM((2 * tokens, 6 * tokens), low),
            pltpu.VMEM((2, 4, half, head_size), low),
            pltpu.VMEM((4, 8, tokens), jnp.float32),
            pltpu.SemaphoreType.DMA((3,)),
            pltpu.SemaphoreType.DMA((STAT + 8,)),
            pltpu.SemaphoreType.DMA((4 * mine,)),
            pltpu.SemaphoreType.DMA((4 * mine,)),
            pltpu.SemaphoreType.DMA((2, mine)),
            pltpu.SemaphoreType.DMA((2, mine, 2)),
            pltpu.SemaphoreType.DMA((mine, 2)),
            pltpu.SemaphoreType.DMA,
        ],
        compiler_params=pltpu.CompilerParams(
            collective_id=0, has_side_effects=True, vmem_limit_bytes=55_600_000
        ),
    )(
        pltpu.with_memory_space_constraint(windows, pltpu.HBM),
        queries.reshape(flat),
        key_vectors.reshape(flat),
        values.reshape(flat),
        grad_out.reshape(flat),
    )
    outs = pl.pallas_call(
        put_out,
        out_shape=[jax.ShapeDtypeStruct(flat, low)] * 4,
        in_specs=[pl.BlockSpec(memory_space=pltpu.VMEM)] * 4,
        out_specs=[pl.BlockSpec(memory_space=pltpu.HBM)] * 4,
        scratch_shapes=[
            pltpu.SemaphoreType.DMA((4,)),
        ],
        compiler_params=pltpu.CompilerParams(vmem_limit_bytes=4_000_000),
    )(*outs)
    return tuple(out.reshape(local_shape) for out in outs)


def solution(mesh):
    spec = P("tm", "space", None, None)
    return jax.shard_map(
        on_device,
        mesh=mesh,
        in_specs=(spec, spec, spec, spec, P()),
        out_specs=(spec, spec, spec, spec),
        check_vma=False,
    )
```

```python
import functools
import math

import jax
import jax.numpy as jnp
from jax import lax
from jax.experimental import pallas as pl
from jax.experimental.pallas import tpu as pltpu
from jax.sharding import PartitionSpec as P

masked_score = -1e30
MESH = pl.DeviceIdType.MESH

OUTER, OWN, PAIR, FAR = range(4)

STAT_OWN, STAT_PAIR, STAT_FAR, STAT_OUTER = range(4)
ABOVE, BELOW = 4, 8

TO_PAIR, TO_FAR, TO_OUTER, RESULT, UP, DOWN, STAT = 0, 1, 2, 3, 4, 7, 10


def dot_nt(a, b):
    return lax.dot_general(a, b, (((1,), (1,)), ((), ())), preferred_element_type=jnp.float32)


def dot_nn(a, b):
    return lax.dot_general(a, b, (((1,), (0,)), ((), ())), preferred_element_type=jnp.float32)


def when(cond, action):
    if cond is None:
        action()
    else:
        pl.when(cond)(action)


def kernel(
    sizes,
    win_hbm,
    q_ref,
    k_ref,
    v_ref,
    g_ref,
    att_ref,
    gq_ref,
    gk_ref,
    gv_ref,
    win_ref,
    bias,
    near,
    results,
    stats,
    scores_ref,
    grad_weights_ref,
    powers_ref,
    grad_scores_ref,
    no_rows,
    no_stats,
    load_sem,
    send_sem,
    pair_sem,
    outer_sem,
    far_sem,
    halo_sem,
    stat_sem,
    result_sem,
):
    head_count, head_size, row_count, col_count, n_tm, n_space = sizes
    tokens = row_count * col_count
    half = tokens // 2
    mine = head_count // 2
    scale = 1.0 / math.sqrt(head_size)
    scale2 = scale * math.log2(math.e)
    tm, sp = lax.axis_index("tm"), lax.axis_index("space")
    side = lax.rem(tm, 2)
    pair = tm + 1 - 2 * side
    inner_to = tm + 2 - 4 * side
    outer_to = tm - 2 + 4 * side
    has_far = (inner_to >= 0) & (inner_to < n_tm)
    has_outer = (outer_to >= 0) & (outer_to < n_tm)
    has_up = sp > 0
    has_down = sp < n_space - 1
    heads = range(mine)
    pieces = [(phase, j, a) for phase in range(2) for j in heads for a in range(2)]
    ins = ((k_ref, v_ref), (q_ref, g_ref))
    outs = (att_ref, gq_ref, gk_ref, gv_ref)

    def head_cols(j, of_pair=False):
        first = (1 - side if of_pair else side) * mine + j
        return pl.ds(pl.multiple_of(first * head_size, head_size), head_size)

    barrier = pltpu.get_barrier_semaphore()

    def greet(cond, tm_to, sp_to):
        def signal():
            pl.semaphore_signal(barrier, inc=1, device_id=(tm_to, sp_to), device_id_type=MESH)

        when(cond, signal)

    greet(None, pair, sp)
    greet(has_far, inner_to, sp)
    greet(has_outer, outer_to, sp)
    greet(has_up, tm, sp - 1)
    greet(has_down, tm, sp + 1)

    def main_rows(i, slot):
        phase, j, a = pieces[i]
        return near.at[phase, j, a, slot, 0:tokens, :]

    def load(i):
        phase, j, a = pieces[i]
        return pltpu.make_async_copy(
            ins[phase][a].at[:, head_cols(j)], main_rows(i, OWN), load_sem.at[phase]
        )

    for i in range(len(pieces)):
        load(i).start()
    get_windows = pltpu.make_async_copy(win_hbm, win_ref, load_sem.at[2])
    get_windows.start()
    no_rows[...] = jnp.zeros_like(no_rows)
    no_stats[...] = jnp.zeros_like(no_stats)

    def remote(src, dst, send, recv, device):
        return pltpu.make_async_remote_copy(
            src_ref=src,
            dst_ref=dst,
            send_sem=send,
            recv_sem=recv,
            device_id=device,
            device_id_type=MESH,
        )

    def to_pair(i):
        phase, j, a = pieces[i]
        return remote(
            ins[phase][a].at[:, head_cols(j, True)],
            main_rows(i, PAIR),
            send_sem.at[TO_PAIR],
            pair_sem.at[i],
            (pair, sp),
        )

    def own_to_far(i):
        phase, j, a = pieces[i]
        return remote(
            main_rows(i, OWN),
            main_rows(i, FAR),
            send_sem.at[TO_FAR],
            far_sem.at[phase, j],
            (outer_to, sp),
        )

    def pair_to_outer(i):
        return remote(
            main_rows(i, PAIR),
            main_rows(i, OUTER),
            send_sem.at[TO_OUTER],
            outer_sem.at[i],
            (inner_to, sp),
        )

    def of_kind(slot):
        return {OUTER: 1, FAR: 2}.get(slot, 0)

    def halo_up(i, slot):
        phase, j, a = pieces[i]
        rows = near.at[phase, j, a, slot]
        return remote(
            rows.at[0:half, :],
            rows.at[tokens : tokens + half, :],
            send_sem.at[UP + of_kind(slot)],
            halo_sem.at[phase, j, of_kind(slot) % 2],
            (tm, sp - 1),
        )

    def halo_down(i, slot):
        phase, j, a = pieces[i]
        rows = near.at[phase, j, a, slot]
        return remote(
            rows.at[half:tokens, :],
            rows.at[tokens + half : 2 * tokens, :],
            send_sem.at[DOWN + of_kind(slot)],
            halo_sem.at[phase, j, of_kind(slot) % 2],
            (tm, sp + 1),
        )

    def halos(i, slot):
        when(has_up, lambda: halo_up(i, slot).start())
        when(has_down, lambda: halo_down(i, slot).start())

    expected = (
        1
        + has_far.astype(jnp.int32)
        + has_outer.astype(jnp.int32)
        + has_up.astype(jnp.int32)
        + has_down.astype(jnp.int32)
    )
    pl.semaphore_wait(barrier, expected)
    for i in range(len(pieces)):
        to_pair(i).start()
    def step_own_out(phase):
        rows = near.at[phase, :, :, OWN, 0:tokens, :]
        pltpu.make_async_copy(rows, rows, load_sem.at[phase]).wait()
        for i in range(len(pieces)):
            if pieces[i][0] == phase:
                when(has_outer, lambda: own_to_far(i).start())
                if phase == 0:
                    halos(i, OWN)

    def step_own_halo(j):
        for i in range(len(pieces)):
            if pieces[i][:2] == (1, j):
                halos(i, OWN)

    def fill(source, target, sem):
        pltpu.make_async_copy(source, target, sem).start()

    def fill_side(first_row, first_stat):
        rows = slice(first_row, first_row + half)

        def all_frames():
            for phase in range(2):
                for j in heads:
                    at = near.at[phase, j, :, :, rows, :]
                    fill(no_rows.at[:, 0:1], at.at[:, 0:1], halo_sem.at[phase, j, 1])
                    fill(no_rows.at[:, 1:4], at.at[:, 1:4], halo_sem.at[phase, j, 0])
            for j in heads:
                last = first_stat + STAT_OUTER
                fill(no_stats.at[0:3], stats.at[j, first_stat:last], stat_sem.at[j, 0])
                fill(no_stats.at[3], stats.at[j, last], stat_sem.at[j, 1])

        def one_frame(slot, stat):
            for phase in range(2):
                for j in heads:
                    sem = halo_sem.at[phase, j, of_kind(slot) % 2]
                    fill(no_rows.at[:, slot], near.at[phase, j, :, slot, rows, :], sem)
            for j in heads:
                sem = stat_sem.at[j, stat // STAT_OUTER]
                fill(no_stats.at[0], stats.at[j, first_stat + stat], sem)

        return all_frames, one_frame

    for has_side, parts in (
        (has_down, fill_side(tokens, BELOW)),
        (has_up, fill_side(tokens + half, ABOVE)),
    ):
        all_frames, one_frame = parts
        pl.when(jnp.logical_not(has_side))(all_frames)
        no_outer, no_far = jnp.logical_not(has_outer), jnp.logical_not(has_far)
        pl.when(has_side & no_outer)(lambda: one_frame(OUTER, STAT_OUTER))
        pl.when(has_side & no_far)(lambda: one_frame(FAR, STAT_FAR))

    for has_frame, slot, stat in ((has_outer, OUTER, STAT_OUTER), (has_far, FAR, STAT_FAR)):

        @pl.when(jnp.logical_not(has_frame))
        def _():
            for phase in range(2):
                for j in heads:
                    near[phase, j, :, slot, 0:tokens, :] = jnp.zeros(
                        (2, tokens, head_size), near.dtype
                    )
            for j in heads:
                fill(no_stats.at[0], stats.at[j, stat], stat_sem.at[j, stat // STAT_OUTER])

    own_id = lax.broadcasted_iota(jnp.int32, (tokens, 2 * tokens), 0)
    near_id = lax.broadcasted_iota(jnp.int32, (tokens, 2 * tokens), 1)
    own_row, own_col = own_id // col_count, own_id % col_count
    near_row, near_col = near_id // col_count, near_id % col_count
    upper = near_row >= row_count + row_count // 2
    near_row = jnp.where(upper, near_row - 2 * row_count, near_row)
    global_row = sp * row_count + near_row
    row_inside = (global_row >= 0) & (global_row < n_space * row_count)
    row_gap = jnp.where(row_inside, jnp.abs(own_row - near_row), 1 << 20)
    col_gap = jnp.abs(own_col - near_col)

    get_windows.wait()
    for j in heads:
        h = side * mine + j
        inside = (row_gap <= win_ref[0, h]) & (col_gap <= win_ref[1, h])
        bias[j] = jnp.where(inside, 0.0, masked_score)

    def window(j, frame):
        here = bias[j]
        there = here + jnp.where(has_outer if frame == OWN else has_far, 0.0, masked_score)
        order = [there, here, here] if frame == OWN else [here, here, there]
        return jnp.concatenate(order, axis=1)

    def around(phase, j, a, frame):
        return near[phase, j, a, frame - 1 : frame + 2].reshape(6 * tokens, head_size)

    def put(kind, j, frame, value):
        if frame == OWN:
            outs[kind][:, head_cols(j)] = value
        else:
            results[kind, j] = value

    def give(kind, j):
        return remote(
            results.at[kind, j],
            outs[kind].at[:, head_cols(j)],
            send_sem.at[RESULT],
            result_sem,
            (pair, sp),
        )

    def forward(j, frame):
        at = slice((frame - OWN) * tokens, (frame - OWN + 1) * tokens)
        scores_ref[at] = dot_nt(near[1, j, 0, frame, 0:tokens, :], around(0, j, 0, frame))
        grad_weights_ref[at] = dot_nt(near[1, j, 1, frame, 0:tokens, :], around(0, j, 1, frame))
        scores = scores_ref[at] * scale2 + window(j, frame)
        top = jnp.max(scores, axis=1, keepdims=True)
        powers = jnp.exp2(scores - top)
        total = jnp.sum(powers, axis=1, keepdims=True)
        share = 1.0 / total
        powers_ref[at] = powers.astype(jnp.bfloat16)
        grad_weights = grad_weights_ref[at]
        out_dot = jnp.sum(powers * grad_weights, axis=1, keepdims=True) * share
        grad_scores_ref[at] = (powers * (grad_weights - out_dot)).astype(jnp.bfloat16)
        found = (top + jnp.log2(total), out_dot)
        if frame == PAIR:
            columns[j] = found
        else:
            send_stats(j, (*found, *columns.pop(j)))
        attended = dot_nn(powers_ref[at], around(0, j, 1, frame)) * share
        put(0, j, frame, attended.astype(jnp.bfloat16))
        query_sum = dot_nn(grad_scores_ref[at], around(0, j, 0, frame)) * (share * scale)
        put(1, j, frame, query_sum.astype(jnp.bfloat16))
    row_lane = lax.broadcasted_iota(jnp.int32, (1, tokens), 1)

    def stat_row(j, r, frame):
        order = (STAT_OUTER, STAT_OWN, STAT_PAIR, STAT_FAR)
        parts = []
        for stat in order[frame - 1 : frame + 2]:
            parts.append(stats[j, stat, r : r + 1, :])
            down, up = stats[j, BELOW + stat, r : r + 1, :], stats[j, ABOVE + stat, r : r + 1, :]
            parts.append(jnp.where(row_lane < half, down, up))
        return jnp.concatenate(parts, axis=1)

    def backward_rows(frame):
        return slice((frame - OWN) * tokens, (frame - OWN + 1) * tokens)

    def backward_start(j, frame):
        at = backward_rows(frame)
        key = near[0, j, 0, frame, 0:tokens, :]
        val = near[0, j, 1, frame, 0:tokens, :]
        scores_ref[at] = dot_nt(key, around(1, j, 0, frame)) * scale2 + window(j, frame)
        grad_weights_ref[at] = dot_nt(val, around(1, j, 1, frame))

    def backward(j, frame):
        at = backward_rows(frame)
        soft = jnp.exp2(scores_ref[at] - stat_row(j, 0, frame))
        grad_scores = soft * (grad_weights_ref[at] - stat_row(j, 1, frame))
        value_sum = dot_nn(soft.astype(jnp.bfloat16), around(1, j, 1, frame))
        put(3, j, frame, value_sum.astype(jnp.bfloat16))
        key_sum = dot_nn(grad_scores.astype(jnp.bfloat16), around(1, j, 0, frame))
        put(2, j, frame, (key_sum * scale).astype(jnp.bfloat16))

    def stat_copies(j):
        block = stats.at[j]
        found = [
            (has_far, STAT_PAIR, STAT_OUTER, 1, (inner_to, sp)),
            (has_outer, STAT_OWN, STAT_FAR, 1, (outer_to, sp)),
        ]
        for at, there, goes in ((BELOW, sp - 1, has_up), (ABOVE, sp + 1, has_down)):
            found += [
                (goes, STAT_OWN, at + STAT_OWN, 2, (tm, there)),
                (goes & has_far, STAT_PAIR, at + STAT_OUTER, 1, (inner_to, there)),
                (goes & has_outer, STAT_OWN, at + STAT_FAR, 1, (outer_to, there)),
            ]
        return [
            (
                goes,
                count,
                remote(
                    block.at[src : src + count],
                    block.at[dst : dst + count],
                    send_sem.at[STAT + n],
                    stat_sem.at[j, dst % 4 // STAT_OUTER],
                    device,
                ),
            )
            for n, (goes, src, dst, count, device) in enumerate(found)
        ]

    def step_pair_in(i):
        to_pair(i).wait_recv()
        when(has_far, lambda: pair_to_outer(i).start())
        halos(i, PAIR)

    def step_far_in(i):
        phase, j, _ = pieces[i]

        @pl.when(has_far)
        def _():
            rows = near.at[phase, j, :, FAR, 0:tokens, :]
            remote(rows, rows, send_sem.at[TO_FAR], far_sem.at[phase, j], (pair, sp)).wait_recv()
            for at in (i, i + 1):
                halos(at, FAR)

    def step_outer_in(i):
        @pl.when(has_outer)
        def _():
            pair_to_outer(i).wait_recv()
            halos(i, OUTER)

    def arrived(ref, sem):
        pltpu.make_async_copy(ref, ref, sem).wait()

    def arrive_halos(phase, j, outer):
        rows = slice(tokens, 2 * tokens)
        if outer:
            arrived(near.at[phase, j, :, OUTER, rows, :], halo_sem.at[phase, j, 1])
        else:
            arrived(near.at[phase, j, :, OWN : FAR + 1, rows, :], halo_sem.at[phase, j, 0])

    columns = {}

    def step_forward_pair(j):
        arrive_halos(0, j, False)
        forward(j, PAIR)
        for kind in (0, 1):
            give(kind, j).start()

    def send_stats(j, found):
        lane = lax.broadcasted_iota(jnp.int32, (tokens, tokens), 1)
        spread = jnp.zeros((tokens, tokens), jnp.float32)
        for at, column in zip((0, 1, 8, 9), found, strict=True):
            spread = jnp.where(lane == at, column, spread)
        stats[j, STAT_OWN : STAT_PAIR + 1] = spread.T[0:16, :].reshape(2, 8, tokens)
        for goes, _, copy in stat_copies(j):
            when(goes, copy.start)

    def step_forward_own(j):
        arrive_halos(0, j, True)
        forward(j, OWN)

    def step_backward_pair(j):
        arrive_halos(1, j, False)
        backward_start(j, PAIR)
        arrived(stats.at[j, 0:7], stat_sem.at[j, 0])
        backward(j, PAIR)
        for kind in (3, 2):
            give(kind, j).start()

    def step_backward_own(j):
        arrive_halos(1, j, True)
        backward_start(j, OWN)
        arrived(stats.at[j, 0:3], stat_sem.at[j, 1])
        backward(j, OWN)

    times = [(0.0, step_own_out, 0), (7.5, step_own_out, 1)]
    for i, (phase, j, a) in enumerate(pieces):
        times.append((6.15 + 0.7 * i, step_pair_in, i))
        if a == 0:
            at = 6.9 + 0.7 * i if phase == 0 else (11.2 if j == 0 else 14.0)
            times.append((at, step_far_in, i))
        late = 0.3 if (j, a) == (mine - 1, 1) else 0.0
        if phase == 1:
            late = 2.2 if 0 < j < mine - 1 else 1.0
        times.append((8.75 + 0.7 * i + late, step_outer_in, i))
    for j in heads:
        times.append((7.55 + 2.8 * j, step_own_halo, j))
        times.append((11.06 + 1.42 * j, step_forward_pair, j))
        times.append((11.35 + 1.8 * j, step_forward_own, j))
        times.append((14.9 + 1.55 * j, step_backward_pair, j))
        times.append((16.6 + (4.5 + 0.5 * j if j > 0 else 0.0), step_backward_own, j))
    for _, step, index in sorted(times, key=lambda entry: entry[0]):
        step(index)

    remote(results, results, send_sem.at[RESULT], result_sem, (pair, sp)).wait()

    def drain(cond, ref, i):
        when(cond, remote(ref, ref, send_sem.at[i], result_sem, (pair, sp)).wait_send)

    whole = near.at[:, :, :, PAIR, 0:tokens, :]
    drain(None, whole, TO_PAIR)
    drain(has_outer, whole, TO_FAR)
    drain(has_far, whole, TO_OUTER)
    for first, cond in ((UP, has_up), (DOWN, has_down)):
        drain(cond, near.at[:, :, :, OWN : PAIR + 1, 0:half, :], first)
        drain(cond & has_outer, near.at[:, :, :, OUTER, 0:half, :], first + 1)
        drain(cond & has_far, near.at[:, :, :, FAR, 0:half, :], first + 2)
    for n, (goes, count, _) in enumerate(stat_copies(0)):
        drain(goes, stats.at[:, 0:count], STAT + n)


def put_out(*refs):
    sources, targets, sems = refs[:4], refs[4:8], refs[8]
    copies = [pltpu.make_async_copy(sources[i], targets[i], sems.at[i]) for i in range(4)]
    for copy in copies:
        copy.start()
    for copy in copies:
        copy.wait()


def on_device(queries, key_vectors, values, grad_out, windows):
    local_shape = queries.shape
    row_count, col_count, features = local_shape[1:]
    head_count = windows.shape[1]
    head_size = features // head_count
    tokens = row_count * col_count
    mine = head_count // 2
    half = tokens // 2
    sizes = (
        head_count,
        head_size,
        row_count,
        col_count,
        lax.axis_size("tm"),
        lax.axis_size("space"),
    )
    flat = (tokens, features)
    low = jnp.bfloat16
    outs = pl.pallas_call(
        functools.partial(kernel, sizes),
        out_shape=[jax.ShapeDtypeStruct(flat, low)] * 4,
        in_specs=[pl.BlockSpec(memory_space=pltpu.HBM)] * 5,
        out_specs=[pl.BlockSpec(memory_space=pltpu.VMEM)] * 4,
        scratch_shapes=[
            pltpu.SMEM((2, head_count), jnp.int32),
            pltpu.VMEM((mine, tokens, 2 * tokens), jnp.float32),
            pltpu.VMEM((2, mine, 2, 4, 2 * tokens, head_size), low),
            pltpu.VMEM((4, mine, tokens, head_size), low),
            pltpu.VMEM((mine, 12, 8, tokens), jnp.float32),
            pltpu.VMEM((2 * tokens, 6 * tokens), jnp.float32),
            pltpu.VMEM((2 * tokens, 6 * tokens), jnp.float32),
            pltpu.VMEM((2 * tokens, 6 * tokens), low),
            pltpu.VMEM((2 * tokens, 6 * tokens), low),
            pltpu.VMEM((2, 4, half, head_size), low),
            pltpu.VMEM((4, 8, tokens), jnp.float32),
            pltpu.SemaphoreType.DMA((3,)),
            pltpu.SemaphoreType.DMA((STAT + 8,)),
            pltpu.SemaphoreType.DMA((4 * mine,)),
            pltpu.SemaphoreType.DMA((4 * mine,)),
            pltpu.SemaphoreType.DMA((2, mine)),
            pltpu.SemaphoreType.DMA((2, mine, 2)),
            pltpu.SemaphoreType.DMA((mine, 2)),
            pltpu.SemaphoreType.DMA,
        ],
        compiler_params=pltpu.CompilerParams(
            collective_id=0, has_side_effects=True, vmem_limit_bytes=55_600_000
        ),
    )(
        pltpu.with_memory_space_constraint(windows, pltpu.HBM),
        queries.reshape(flat),
        key_vectors.reshape(flat),
        values.reshape(flat),
        grad_out.reshape(flat),
    )
    outs = pl.pallas_call(
        put_out,
        out_shape=[jax.ShapeDtypeStruct(flat, low)] * 4,
        in_specs=[pl.BlockSpec(memory_space=pltpu.VMEM)] * 4,
        out_specs=[pl.BlockSpec(memory_space=pltpu.HBM)] * 4,
        scratch_shapes=[
            pltpu.SemaphoreType.DMA((4,)),
        ],
        compiler_params=pltpu.CompilerParams(vmem_limit_bytes=4_000_000),
    )(*outs)
    return tuple(out.reshape(local_shape) for out in outs)


def solution(mesh):
    spec = P("tm", "space", None, None)
    return jax.shard_map(
        on_device,
        mesh=mesh,
        in_specs=(spec, spec, spec, spec, P()),
        out_specs=(spec, spec, spec, spec),
        check_vma=False,
    )
```
